128 devices in a mesh: net: 32 (over y, z, core), hour: 4 (over x).
Axes of the slice: x: 4, y: 4, z: 4, core: 2. Of those that a mesh axis runs over, the one named last changes fastest.
Arguments:
- measured: float32 [4096, 2048], P('net', 'hour')
- prior_flow: float32 [4096, 2048], P('net', 'hour'), may hold values from -6 to 6
- demand: float32 [3072, 2048], P('net', 'hour'), may hold values from -6 to 6
- pipe_sigma: float32 [4096], P('net'), may hold values from 0.5 to 2
- whiten_coef: float32 [512], replicated
- pipe_tail: int32 [4096], P('net'), may hold values from 0 to 95
- pipe_head: int32 [4096], P('net'), may hold values from 0 to 95
- boundary_pipe: int32 [32, 2, 8], P('net'), may hold values from 0 to 127, as said below
- boundary_count: int32 [32, 2], P('net'), may hold values from 0 to 8, as said below
- arrival_junction: int32 [32, 2, 8], P('net'), may hold values from 0 to 95
Outputs:
- flows: float32 [4096, 2048], P('net', 'hour')
- residual: float32 [4096, 2048], P('net', 'hour')
The draws below stay inside these ranges and needn't reach their ends.
Inputs may be any that keep to these rules, and one draw needn't show every extreme that they name: `boundary_pipe`: the 16 entries of one partition's two lists are distinct local pipe numbers. `boundary_count`: partition 0 has no live slot toward side 0 and partition 32 - 1 none toward side 1.
All inputs are finite; a program needn't handle non-finite values.
Results may differ from the reference program's by a relative error of at most 0.00026.
Values sent between devices are 32-bit elements; how exact they have to be, the bound alone decides.
No kernel may reach another device: no remote copies, remote signals or barrier semaphores. Data moves between devices by JAX's collectives and lax.ppermute only.
A program may use at most 64 MiB of HBM per device.

```python
import math
import jax
import jax.numpy as jnp
from jax import lax

P_DEV = 128
BLK = 512
ITERS = 3
J_DEV = 96
CAP = 8
NETS = 32
PIPES = 4096
JUNCS = 3072
HOURS = 2048
N_HOUR = 4


def draw_measured(key, part):
    first_key = jax.random.fold_in(key, 0)
    row_pos = jnp.arange(PIPES, dtype=jnp.float32)[:, None]
    trend = 1.0 + 2.0 * row_pos / (PIPES - 1)
    base = jnp.clip(jax.random.normal(first_key, (PIPES, HOURS), jnp.float32), -6.0, 6.0)
    return (base * trend).astype(jnp.float32)


def draw_whiten_coef(key, part):
    lead_key, tap_key = jax.random.split(key)
    lags = jnp.arange(BLK, dtype=jnp.float32)
    ratio = 1.0 - 4.0 / BLK
    decay = 0.6 * (4.0 / BLK) * jnp.exp((lags - 1.0) * math.log(ratio))
    taps = jax.random.uniform(tap_key, (BLK,), jnp.float32, -1.0, 1.0)
    lead = jax.random.uniform(lead_key, (), jnp.float32, 0.8, 1.2)
    return jnp.where(lags == 0.0, lead, taps * decay).astype(jnp.float32)


def draw_boundary_pipe(key, part):
    keys = jax.random.split(key, NETS)

    def one_partition(sub_key):
        order = jax.random.permutation(sub_key, P_DEV)
        return order[:2 * CAP].reshape(2, CAP)
    return jax.vmap(one_partition)(keys).astype(jnp.int32)


def draw_boundary_count(key, part):
    count_key, full_key = jax.random.split(key)
    counts = jax.random.randint(count_key, (NETS, 2), CAP // 4, CAP + 1).astype(jnp.int32)
    full_row = jax.random.randint(full_key, (), 0, NETS - 1).astype(jnp.int32)
    partitions = jnp.arange(NETS, dtype=jnp.int32)
    upper_side = jnp.where(partitions == full_row, CAP, counts[:, 1])
    counts = jnp.stack([counts[:, 0], upper_side], axis=1)
    counts = counts.at[0, 0].set(0)
    counts = counts.at[NETS - 1, 1].set(0)
    return counts.astype(jnp.int32)


def plant(values, stream_key, smallest, top_value):
    extent = values.shape
    index_at = [jax.random.randint(jax.random.fold_in(stream_key, axis), (), 0, extent[axis]) for axis in range(len(extent))]
    values = values.at[tuple(index_at)].set(smallest)
    longest = extent.index(max(extent))
    index_at[longest] = (index_at[longest] + 1) % extent[longest]
    return values.at[tuple(index_at)].set(top_value)


def level_of(rng, dims, cuts, smallest, largest):
    def one(dim, parts):
        heights = jax.random.uniform(jax.random.fold_in(jax.random.fold_in(rng, 6), dim), (parts,), jnp.float32, smallest / len(cuts), largest / len(cuts))
        return jnp.repeat(jnp.exp(heights), dims[dim] // parts).reshape((-1,) + (1,) * (len(dims) - dim - 1))

    gain = one(*cuts[0])
    for cut in cuts[1:]:
        gain = gain * one(*cut)
    return gain


def scatter_about(own_key, dims, spread, most, cuts=(), held_as=jnp.bfloat16):
    entries = jax.random.normal(own_key, dims, jnp.float32) * spread
    if len(cuts) > 0:
        entries = level_of(own_key, dims, cuts, -0.22, 0.18) * entries
    return jnp.clip(entries, min=-most, max=most).astype(held_as)


def setup_inputs(seed: int = 0) -> dict:
    streams_of = jax.random.split(jax.random.key(seed), 11)
    measured = draw_measured(jax.random.fold_in(streams_of[10], 71), 0)
    prior_flow = scatter_about(streams_of[1], (PIPES, HOURS), 1.0, 6.0, ((0, 32), (1, 4)), jnp.float32)
    demand = scatter_about(streams_of[2], (JUNCS, HOURS), 1.0, 6.0, ((0, 32), (1, 4)), jnp.float32)
    pipe_sigma = jnp.clip(jnp.exp(math.log(2.0) - 1.3862944 * jax.random.uniform(streams_of[3], (PIPES,), jnp.float32) ** level_of(streams_of[3], (PIPES,), ((0, 32),), -0.2, 0.2)), 0.5, 2.0)
    whiten_coef = draw_whiten_coef(jax.random.fold_in(streams_of[10], 71), 0)
    pipe_tail = plant(jax.random.randint(streams_of[5], (PIPES,), 0, J_DEV), jax.random.fold_in(streams_of[5], 1), 0, J_DEV - 1).astype(jnp.int32)
    pipe_head = plant(jax.random.randint(streams_of[6], (PIPES,), 0, J_DEV), jax.random.fold_in(streams_of[6], 1), 0, J_DEV - 1).astype(jnp.int32)
    boundary_pipe = draw_boundary_pipe(jax.random.fold_in(streams_of[10], 71), 0)
    boundary_count = draw_boundary_count(jax.random.fold_in(streams_of[10], 71), 0)
    arrival_junction = plant(jax.random.randint(streams_of[9], (NETS, 2, CAP), 0, J_DEV), jax.random.fold_in(streams_of[9], 1), 0, J_DEV - 1).astype(jnp.int32)
    return {"measured": measured, "prior_flow": prior_flow, "demand": demand, "pipe_sigma": pipe_sigma, "whiten_coef": whiten_coef, "pipe_tail": pipe_tail, "pipe_head": pipe_head, "boundary_pipe": boundary_pipe, "boundary_count": boundary_count, "arrival_junction": arrival_junction}


huber_edge = 1.5
penalty = 4.0


def whiten_matrix(whiten_coef):
    length = whiten_coef.shape[0]
    positions = jnp.arange(length, dtype=jnp.int32)
    lag_index = positions[:, None] - positions[None, :]
    taps = whiten_coef[jnp.clip(lag_index, 0, length - 1)]
    return jnp.where(lag_index >= 0, taps, jnp.zeros_like(taps))


def reference(measured, prior_flow, demand, pipe_sigma, whiten_coef, pipe_tail, pipe_head, boundary_pipe, boundary_count, arrival_junction):
    whitener = whiten_matrix(whiten_coef)

    def forward_filter(field):
        blocks = field.reshape(PIPES, N_HOUR, BLK)
        out = jnp.einsum("pnb,cb->pnc", blocks, whitener, precision=lax.Precision.HIGHEST)
        return out.reshape(PIPES, HOURS)

    def backward_filter(field):
        blocks = field.reshape(PIPES, N_HOUR, BLK)
        out = jnp.einsum("pnc,cb->pnb", blocks, whitener, precision=lax.Precision.HIGHEST)
        return out.reshape(PIPES, HOURS)

    variance = (pipe_sigma * pipe_sigma)[:, None]
    whitened = forward_filter((measured - prior_flow) / pipe_sigma[:, None])
    huber_weight = huber_edge / jnp.maximum(jnp.abs(whitened), huber_edge)

    def quadratic(field):
        return backward_filter(huber_weight * forward_filter(field)) / variance

    pipe_ids = jnp.arange(PIPES, dtype=jnp.int32)
    owner = pipe_ids // P_DEV
    tail_global = owner * J_DEV + pipe_tail
    head_global = owner * J_DEV + pipe_head
    slot_ids = jnp.arange(CAP, dtype=jnp.int32)
    live_mask = (slot_ids[None, None, :] < boundary_count[:, :, None]).astype(jnp.float32)
    partitions = jnp.arange(NETS, dtype=jnp.int32)
    source_global = partitions[:, None, None] * P_DEV + boundary_pipe
    below_junction = jnp.roll(arrival_junction[:, 1, :], 1, axis=0)
    above_junction = jnp.roll(arrival_junction[:, 0, :], -1, axis=0)
    dest_below = (partitions[:, None] - 1) * J_DEV + below_junction
    dest_above = (partitions[:, None] + 1) * J_DEV + above_junction
    dest_global = jnp.clip(jnp.stack([dest_below, dest_above], axis=1), 0, JUNCS - 1).astype(jnp.int32)
    source_flat = source_global.reshape(-1)
    dest_flat = dest_global.reshape(-1)
    live_flat = live_mask.reshape(-1)
    interior = (1.0 - jnp.zeros((PIPES,), jnp.float32).at[source_flat].add(live_flat))[:, None]
    live_rows = live_flat[:, None]

    def balance_of(field):
        heads = jnp.zeros((JUNCS, HOURS), jnp.float32).at[head_global].add(field * interior)
        tails = jnp.zeros((JUNCS, HOURS), jnp.float32).at[tail_global].add(field)
        remote = jnp.zeros((JUNCS, HOURS), jnp.float32).at[dest_flat].add(field[source_flat] * live_rows)
        return heads - tails + remote

    def adjoint_of(balance):
        remote = jnp.zeros((PIPES, HOURS), jnp.float32).at[source_flat].add(balance[dest_flat] * live_rows)
        return balance[head_global] * interior - balance[tail_global] + remote

    def operator(field):
        return quadratic(field) + penalty * adjoint_of(balance_of(field))

    rhs = quadratic(measured) + penalty * adjoint_of(demand)
    flows = prior_flow
    residual = rhs - operator(flows)
    direction = residual
    norm_now = jnp.sum(residual * residual)
    for iteration in range(ITERS):
        image = operator(direction)
        step_size = norm_now / jnp.sum(direction * image)
        flows = flows + step_size * direction
        residual = residual - step_size * image
        norm_next = jnp.sum(residual * residual)
        direction = residual + (norm_next / norm_now) * direction
        norm_now = norm_next
    return flows, residual
```

```python
import jax
import jax.numpy as jnp
from jax import lax
from jax.experimental import pallas as pl
from jax.experimental.pallas import tpu as pltpu
from jax.sharding import PartitionSpec as P

EDGE = 1.5
PENALTY = 4.0
F32 = jnp.float32
BF16 = jnp.bfloat16


def iota(shape, dim):
    return lax.broadcasted_iota(jnp.int32, shape, dim)


def thirds(v):
    a = v.astype(BF16)
    rest = v - a.astype(F32)
    b = rest.astype(BF16)
    c = (rest - b.astype(F32)).astype(BF16)
    return a, b, c


def halves(v):
    a = v.astype(BF16)
    return a, (v - a.astype(F32)).astype(BF16)


def mm(a, b):
    return jnp.dot(a, b, preferred_element_type=F32)


def pick(exact, v):
    a, b, c = thirds(v)
    return (mm(exact, c) + mm(exact, b)) + mm(exact, a)


def product(x, t_hi, t_lo):
    hi, lo = halves(x)
    return (mm(lo, t_hi) + mm(hi, t_lo)) + mm(hi, t_hi)


def forward(v, taps):
    t0h, t0l, t1h, t1l = taps
    rows = v.shape[0]
    half = v.shape[1] // 2
    both = jnp.concatenate([v[:, :half], v[:, half:]], axis=0)
    near = product(both, t0h[...], t0l[...])
    far = product(v[:, :half], t1h[...], t1l[...])
    return jnp.concatenate([near[:rows], near[rows:] + far], axis=1)


def backward(v, taps):
    t0h, t0l, t1h, t1l = taps
    rows = v.shape[0]
    half = v.shape[1] // 2
    both = jnp.concatenate([v[:, :half], v[:, half:]], axis=0)
    near = product(both, t0h[...], t0l[...])
    far = product(v[:, half:], t1h[...], t1l[...])
    return jnp.concatenate([near[:rows] + far, near[rows:]], axis=1)


def lanes_sum(v):
    rows, cols = v.shape
    total = None
    for i in range(0, rows, 8):
        for j in range(0, cols, 128):
            part = v[i : i + 8, j : j + 128]
            total = part if total is None else total + part
    return total


def column(row, n):
    return jnp.sum(jnp.where(iota((n, n), 0) == iota((n, n), 1), row, 0.0), axis=1, keepdims=True)


def lists_kernel(par, prior, bp, bc, aj, head, tail, msg, s_a, s_b, inc, l_a, l_b, match):
    cap = bp.shape[2]
    pipes = prior.shape[0]
    juncs = inc.shape[0]
    odd = par[0, 0] == 1

    def side(ref, flip):
        lower, upper = ref[0, 0:1, :].astype(F32), ref[0, 1:2, :].astype(F32)
        return jnp.where(odd != flip, lower, upper)

    counts = bc[0:1, :].astype(F32)
    count_a = jnp.where(odd, counts[:, 0:1], counts[:, 1:2])
    count_b = jnp.where(odd, counts[:, 1:2], counts[:, 0:1])
    slot = iota((cap, 1), 0).astype(F32)
    live_a = jnp.where(slot < count_a, 1.0, 0.0)
    live_b = jnp.where(slot < count_b, 1.0, 0.0)
    pipe = iota((cap, pipes), 1).astype(F32)
    sel_a = jnp.where(column(side(bp, False), cap) == pipe, live_a, 0.0)
    sel_b = jnp.where(column(side(bp, True), cap) == pipe, live_b, 0.0)
    inner = 1.0 - jnp.sum(sel_a + sel_b, axis=0, keepdims=True)
    junction = iota((juncs, pipes), 0)
    heads = jnp.where(junction == head[...], inner, 0.0)
    tails = jnp.where(junction == tail[...], 1.0, 0.0)
    s_a[...] = sel_a.astype(BF16)
    s_b[...] = sel_b.astype(BF16)
    inc[...] = (heads - tails).astype(BF16)
    land = iota((juncs, cap), 0).astype(F32)
    to_a, to_b = side(aj, False), side(aj, True)
    l_a[...] = jnp.where(land == to_a, 1.0, 0.0).astype(BF16)
    l_b[...] = jnp.where(land == to_b, 1.0, 0.0).astype(BF16)
    same = jnp.where(column(to_b, cap) == to_b, 1.0, 0.0)
    match[...] = jnp.concatenate([same, jnp.zeros((cap, 128 - cap), F32)], axis=1)
    msg[0:cap, :] = -pick(sel_a.astype(BF16), prior[...])
    msg[cap:, :] = jnp.broadcast_to(live_a, (cap, prior.shape[1]))


def whiten_kernel(coef, sigma, measured, prior, t0h, t0l, t1h, t1l, u0h, u0l, u1h, u1l, weight, base, rvar, tau):
    length = coef.shape[1]
    half = length // 2
    c = coef[...]
    shifted = pltpu.roll(jnp.broadcast_to(c, (half, length)), 0, 1, stride=1, stride_axis=0)
    upper = iota((half, half), 1) >= iota((half, half), 0)
    t0 = jnp.where(upper, shifted[:, :half], 0.0)
    t1 = shifted[:, half:]
    for hi, lo, x in ((t0h, t0l, t0), (t1h, t1l, t1), (u0h, u0l, t0.T), (u1h, u1l, t1.T)):
        a, b = halves(x)
        hi[...] = a
        lo[...] = b
    size = jnp.sum(jnp.abs(c), axis=1, keepdims=True)
    scale = 1.0 / (4.0 * size * size + 64.0)
    tau[...] = jnp.broadcast_to(scale, tau.shape)
    sig = jnp.transpose(jnp.broadcast_to(sigma[...], (128, 128)))[:, 0:1]
    rsig = 1.0 / sig
    whitened = forward((measured[...] - prior[...]) * rsig, (t0h, t0l, t1h, t1l))
    h = EDGE / jnp.maximum(jnp.abs(whitened), EDGE)
    weight[...] = h
    base[...] = backward(h * whitened, (u0h, u0l, u1h, u1l)) * rsig
    rvar[...] = jnp.broadcast_to(rsig * rsig * scale, rvar.shape)


def first_kernel(demand, prior, got, s_b, inc, l_a, l_b, match, part, msg, l_am):
    cap = s_b.shape[0]
    live = jnp.sum(jnp.where(iota((cap, cap), 0) == iota((cap, cap), 1), got[cap:, 0:cap], 0.0), axis=0, keepdims=True)
    masked = (l_a[...].astype(F32) * live).astype(BF16)
    l_am[...] = masked
    part[...] = demand[...] - pick(inc[...], prior[...]) + pick(masked, got[0:cap, :])
    msg[0:cap, :] = -pick(s_b[...], prior[...])
    msg[cap : 2 * cap, :] = pick(l_b[...].T, part[...])
    msg[2 * cap :, :] = jnp.broadcast_to(match[:, 0:1], (cap, prior.shape[1]))
    msg[2 * cap :, 0:128] = match[...]


def meet(near, gain, part, sent, got, s_a, s_b, inc, l_am, l_b, match, y_out, w_out, msg):
    cap = s_a.shape[0]
    y = part[...] + pick(l_b[...], got[0:cap, :])
    y_far = got[cap : 2 * cap, :] + pick(match, sent[0:cap, :])
    w = near + gain * (pick(inc[...].T, y) + pick(s_b[...].T, y_far))
    y_out[...] = y
    w_out[...] = w
    msg[0:cap, :] = pick(l_am[...].T, y)
    msg[cap:, :] = pick(s_a[...], w)


def meet_first(base, part, sent, got, s_a, s_b, inc, l_am, l_b, y_out, w_out, msg, match):
    cap = s_a.shape[0]
    match[...] = got[2 * cap :, 0:128]
    meet(base[...], PENALTY, part, sent, got, s_a, s_b, inc, l_am, l_b, match[:, 0:cap].astype(BF16), y_out, w_out, msg)


def meet_next(q, rvar, tau, part, sent, got, s_a, s_b, inc, l_am, l_b, match, y_out, w_out, msg):
    cap = s_a.shape[0]
    near = q[...] * rvar[:, 0:1]
    meet(near, PENALTY * tau[0:1, 0:1], part, sent, got, s_a, s_b, inc, l_am, l_b, match[:, 0:cap].astype(BF16), y_out, w_out, msg)


def meet_last(r0m, r1m, r2m, r, q, rvar, tau, part, sent, got, s_a, s_b, inc, l_am, l_b, match, w_out, msg, row, y_s):
    cap = s_a.shape[0]
    near = q[...] * rvar[:, 0:1]
    gain = PENALTY * tau[0:1, 0:1]
    meet(near, gain, part, sent, got, s_a, s_b, inc, l_am, l_b, match[:, 0:cap].astype(BF16), y_s, w_out, msg)
    y = y_s[...]
    m5 = lanes_sum(r[...] * near) + gain * lanes_sum(y * y)
    lane = iota((1, 128), 1) // 16
    out = jnp.zeros((1, 128), F32)
    for g, tile in enumerate((r0m[0:8, :], r1m[0:8, :], r1m[8:16, :], r2m[0:8, :], r2m[8:16, :], m5)):
        x = jnp.sum(tile, axis=0, keepdims=True)
        for s in (64, 32, 16):
            x = x + pltpu.roll(x, s, 1)
        out = jnp.where(lane == g, x, out)
    row[...] = out


def open_kernel(gain, w, sent, got, s_a, s_b, inc, l_am, l_b, r_out, part, msg):
    cap = s_a.shape[0]
    r = w[...] + gain * pick(s_a[...].T, got[0:cap, :])
    arrived = got[cap:, :] + gain * sent[0:cap, :]
    r_out[...] = r
    part[...] = pick(inc[...], r) + pick(l_am[...], arrived)
    msg[0:cap, :] = pick(s_b[...], r)
    msg[cap:, :] = pick(l_b[...].T, part[...])


def open_first(*refs):
    open_kernel(PENALTY, *refs)


def open_next(tau, *refs):
    open_kernel(PENALTY * tau[0:1, 0:1], *refs)


def filter_first(r, weight, t0h, t0l, t1h, t1l, u0h, u0l, u1h, u1l, q, sums):
    x = r[...]
    q[...] = backward(weight[...] * forward(x, (t0h, t0l, t1h, t1l)), (u0h, u0l, u1h, u1l))
    sums[...] = lanes_sum(x * x)


def filter_next(r, before, weight, t0h, t0l, t1h, t1l, u0h, u0l, u1h, u1l, q, sums):
    x = r[...]
    q[...] = backward(weight[...] * forward(x, (t0h, t0l, t1h, t1l)), (u0h, u0l, u1h, u1l))
    sums[0:8, :] = lanes_sum(before[...] * x)
    sums[8:16, :] = lanes_sum(x * x)


def two_sum(a, b):
    s = a + b
    t = s - a
    return s, (a - (s - t)) + (b - t)


def split(a):
    t = 4097.0 * a
    hi = t - (t - a)
    return hi, a - hi


def two_prod(a, b):
    p = a * b
    ah, al = split(a)
    bh, bl = split(b)
    return p, ((ah * bh - p) + ah * bl + al * bh) + al * bl


def pair_add(x, y):
    s, e = two_sum(x[0], y[0])
    return two_sum(s, e + (x[1] + y[1]))


def finish_kernel(rows, tau, prior, r0, r1, r2, w, got, s_a, flows, residual):
    n = rows.shape[0]
    tot = (rows[0:8, :], jnp.zeros((8, 128), F32))
    for i in range(8, n, 8):
        s, e = two_sum(tot[0], rows[i : i + 8, :])
        tot = (s, tot[1] + e)
    for sh in (4, 2, 1):
        tot = pair_add(tot, tuple(pltpu.roll(t, sh, 0) for t in tot))
    for sh in (8, 4, 2, 1):
        tot = pair_add(tot, tuple(pltpu.roll(t, 128 - sh, 1) for t in tot))
    hi, lo = tot
    s0 = pltpu.roll(hi, 112, 1) / hi
    s = jnp.broadcast_to(s0[:, 0:1], (8, 128))
    mu = [hi]
    for _ in range(5):
        ph, pe = two_prod(hi, s)
        pe = pe + lo * s
        nh, nl = pltpu.roll(hi, 112, 1), pltpu.roll(lo, 112, 1)
        a, e = two_sum(nh, -ph)
        hi, lo = two_sum(a, e + (nl - pe))
        mu.append(hi)
    nu = [mu[k + 1] + s * mu[k] for k in range(5)]

    def form(u, v, m):
        total = None
        for i, a in enumerate(u):
            for j, b in enumerate(v):
                term = a * b * m[i + j]
                total = term if total is None else total + term
        return total

    def image(d):
        out = [s * x for x in d] + [jnp.zeros_like(s)]
        return [out[k] + (d[k - 1] if k else 0.0) for k in range(len(out))]

    a0 = mu[0] / nu[0]
    res1 = [mu[1] / nu[0], -a0]
    rr1 = form(res1, res1, mu)
    b0 = rr1 / mu[0]
    d1 = [res1[0] + b0, res1[1]]
    a1 = rr1 / form(d1, d1, nu)
    im1 = image(d1)
    res2 = [res1[0] - a1 * im1[0], res1[1] - a1 * im1[1], -a1 * im1[2]]
    rr2 = form(res2, res2, mu)
    b1 = rr2 / rr1
    d2 = [res2[0] + b1 * d1[0], res2[1] + b1 * d1[1], res2[2]]
    a2 = rr2 / form(d2, d2, nu)
    im2 = image(d2)
    f = [a0 + a1 * d1[0] + a2 * d2[0], a1 * d1[1] + a2 * d2[1], a2 * d2[2]]
    e = [res2[0] - a2 * im2[0], res2[1] - a2 * im2[1], res2[2] - a2 * im2[2], -a2 * im2[3]]
    ss = s * s
    f = [f[0] - s * f[1] + ss * f[2], f[1] - 2.0 * s * f[2], f[2]]
    e = [
        ((e[0] - s * e[1]) + ss * e[2]) - ss * s * e[3],
        (e[1] - 2.0 * s * e[2]) + 3.0 * ss * e[3],
        e[2] - 3.0 * s * e[3],
        e[3],
    ]
    f = [x[0:1, 0:1] * tau[0:1, 0:1] for x in f]
    e = [x[0:1, 0:1] for x in e]
    cap = s_a.shape[0]
    x0, x1, x2 = r0[...], r1[...], r2[...]
    x3 = w[...] + PENALTY * tau[0:1, 0:1] * pick(s_a[...].T, got[0:cap, :])
    flows[...] = prior[...] + ((f[0] * x0 + f[1] * x1) + f[2] * x2)
    residual[...] = ((e[0] * x0 + e[1] * x1) + e[2] * x2) + e[3] * x3


def call(kernel, outs, *args, smem=0, scratch=()):
    specs = [pl.BlockSpec(memory_space=pltpu.SMEM)] * smem
    specs += [pl.BlockSpec(memory_space=pltpu.VMEM)] * (len(args) - smem)
    return pl.pallas_call(
        kernel,
        out_shape=tuple(jax.ShapeDtypeStruct(s, d) for s, d in outs),
        in_specs=specs,
        out_specs=tuple(pl.BlockSpec(memory_space=pltpu.VMEM) for _ in outs),
        scratch_shapes=list(scratch),
    )(*args)


def shards(
    measured,
    prior_flow,
    demand,
    pipe_sigma,
    whiten_coef,
    pipe_tail,
    pipe_head,
    boundary_pipe,
    boundary_count,
    arrival_junction,
):
    pipes, hours = prior_flow.shape
    juncs = demand.shape[0]
    cap = boundary_pipe.shape[2]
    nets = lax.axis_size("net")
    devices = nets * lax.axis_size("hour")
    field = ((pipes, hours), F32)
    heads = ((juncs, hours), F32)
    msg2 = ((2 * cap, hours), F32)
    half = ((hours // 2, hours // 2), BF16)
    on_chip = [(i, i ^ 1) for i in range(nets)]
    across = [(i, i + 1) for i in range(1, nets - 1, 2)] + [(i + 1, i) for i in range(1, nets - 1, 2)]

    def swap(x):
        return lax.ppermute(x, "net", on_chip)

    def cross(x):
        return lax.ppermute(x, "net", across)

    odd = (lax.axis_index("net") % 2).astype(jnp.int32).reshape(1, 1)
    msg, s_a, s_b, inc, l_a, l_b, own_match = call(
        lists_kernel,
        [msg2, ((cap, pipes), BF16), ((cap, pipes), BF16), ((juncs, pipes), BF16), ((juncs, cap), BF16), ((juncs, cap), BF16), ((cap, 128), F32)],
        odd,
        prior_flow,
        boundary_pipe,
        boundary_count,
        arrival_junction,
        pipe_head.reshape(1, pipes),
        pipe_tail.reshape(1, pipes),
        smem=1,
    )
    got = swap(msg)
    part, msg, l_am = call(
        first_kernel,
        [heads, ((3 * cap, hours), F32), ((juncs, cap), BF16)],
        demand, prior_flow, got, s_b, inc, l_a, l_b, own_match,
    )
    got = cross(msg)
    out = call(
        whiten_kernel,
        [half] * 8 + [field, field, ((pipes, 128), F32), ((8, 128), F32)],
        whiten_coef.reshape(1, hours), pipe_sigma.reshape(1, pipes), measured, prior_flow,
    )
    taps, (weight, base, rvar, tau) = out[:8], out[8:]
    lists = (s_a, s_b, inc, l_am, l_b)
    y, w, msg, match = call(
        meet_first, [heads, field, msg2, ((cap, 128), F32)], base, part, msg, got, *lists
    )
    fields, sums = [], []
    for step in range(3):
        got = swap(msg)
        if step == 0:
            r, part, msg = call(open_first, [field, heads, msg2], w, msg, got, *lists)
        else:
            r, part, msg = call(open_next, [field, heads, msg2], tau, w, msg, got, *lists)
        got = cross(msg)
        if step == 0:
            q, acc = call(filter_first, [field, ((8, 128), F32)], r, weight, *taps)
        else:
            q, acc = call(filter_next, [field, ((16, 128), F32)], r, fields[-1], weight, *taps)
        fields.append(r)
        sums.append(acc)
        if step < 2:
            y, w, msg = call(meet_next, [heads, field, msg2], q, rvar, tau, part, msg, got, *lists, match)
    w, msg, row = call(
        meet_last, [field, msg2, ((1, 128), F32)],
        *sums, r, q, rvar, tau, part, msg, got, *lists, match,
        scratch=[pltpu.VMEM((juncs, hours), F32)],
    )
    got = swap(msg)
    rows = lax.all_to_all(
        jnp.broadcast_to(row[None], (devices, 1, 128)), ("net", "hour"), 0, 0, tiled=True
    ).reshape(devices, 128)
    return call(finish_kernel, [field, field], rows, tau, prior_flow, *fields, w, got, s_a)


def solution(mesh):
    placed = (
        P("net", "hour"),
        P("net", "hour"),
        P("net", "hour"),
        P("net"),
        P(),
        P("net"),
        P("net"),
        P("net", None, None),
        P("net", None),
        P("net", None, None),
    )
    return jax.shard_map(
        shards,
        mesh=mesh,
        in_specs=placed,
        out_specs=(P("net", "hour"), P("net", "hour")),
        check_vma=False,
    )
```

```python
import jax
import jax.numpy as jnp
from jax import lax
from jax.experimental import pallas as pl
from jax.experimental.pallas import tpu as pltpu
from jax.sharding import PartitionSpec as P

EDGE = 1.5
PENALTY = 4.0
F32 = jnp.float32
BF16 = jnp.bfloat16


def iota(shape, dim):
    return lax.broadcasted_iota(jnp.int32, shape, dim)


def thirds(v):
    a = v.astype(BF16)
    rest = v - a.astype(F32)
    b = rest.astype(BF16)
    c = (rest - b.astype(F32)).astype(BF16)
    return a, b, c


def halves(v):
    a = v.astype(BF16)
    return a, (v - a.astype(F32)).astype(BF16)


def mm(a, b):
    return jnp.dot(a, b, preferred_element_type=F32)


def pick(exact, v):
    a, b, c = thirds(v)
    return (mm(exact, c) + mm(exact, b)) + mm(exact, a)


def product(x, t_hi, t_lo):
    hi, lo = halves(x)
    return (mm(lo, t_hi) + mm(hi, t_lo)) + mm(hi, t_hi)


def forward(v, taps):
    t0h, t0l, t1h, t1l = taps
    rows = v.shape[0]
    half = v.shape[1] // 2
    both = jnp.concatenate([v[:, :half], v[:, half:]], axis=0)
    near = product(both, t0h[...], t0l[...])
    far = product(v[:, :half], t1h[...], t1l[...])
    return jnp.concatenate([near[:rows], near[rows:] + far], axis=1)


def backward(v, taps):
    t0h, t0l, t1h, t1l = taps
    rows = v.shape[0]
    half = v.shape[1] // 2
    both = jnp.concatenate([v[:, :half], v[:, half:]], axis=0)
    near = product(both, t0h[...], t0l[...])
    far = product(v[:, half:], t1h[...], t1l[...])
    return jnp.concatenate([near[:rows] + far, near[rows:]], axis=1)


def lanes_sum(v):
    rows, cols = v.shape
    total = None
    for i in range(0, rows, 8):
        for j in range(0, cols, 128):
            part = v[i : i + 8, j : j + 128]
            total = part if total is None else total + part
    return total


def column(row, n):
    return jnp.sum(jnp.where(iota((n, n), 0) == iota((n, n), 1), row, 0.0), axis=1, keepdims=True)


def lists_kernel(par, prior, bp, bc, aj, head, tail, msg, s_a, s_b, inc, l_a, l_b, match):
    cap = bp.shape[2]
    pipes = prior.shape[0]
    juncs = inc.shape[0]
    odd = par[0, 0] == 1

    def side(ref, flip):
        lower, upper = ref[0, 0:1, :].astype(F32), ref[0, 1:2, :].astype(F32)
        return jnp.where(odd != flip, lower, upper)

    counts = bc[0:1, :].astype(F32)
    count_a = jnp.where(odd, counts[:, 0:1], counts[:, 1:2])
    count_b = jnp.where(odd, counts[:, 1:2], counts[:, 0:1])
    slot = iota((cap, 1), 0).astype(F32)
    live_a = jnp.where(slot < count_a, 1.0, 0.0)
    live_b = jnp.where(slot < count_b, 1.0, 0.0)
    pipe = iota((cap, pipes), 1).astype(F32)
    sel_a = jnp.where(column(side(bp, False), cap) == pipe, live_a, 0.0)
    sel_b = jnp.where(column(side(bp, True), cap) == pipe, live_b, 0.0)
    inner = 1.0 - jnp.sum(sel_a + sel_b, axis=0, keepdims=True)
    junction = iota((juncs, pipes), 0)
    heads = jnp.where(junction == head[...], inner, 0.0)
    tails = jnp.where(junction == tail[...], 1.0, 0.0)
    s_a[...] = sel_a.astype(BF16)
    s_b[...] = sel_b.astype(BF16)
    inc[...] = (heads - tails).astype(BF16)
    land = iota((juncs, cap), 0).astype(F32)
    to_a, to_b = side(aj, False), side(aj, True)
    l_a[...] = jnp.where(land == to_a, 1.0, 0.0).astype(BF16)
    l_b[...] = jnp.where(land == to_b, 1.0, 0.0).astype(BF16)
    same = jnp.where(column(to_b, cap) == to_b, 1.0, 0.0)
    match[...] = jnp.concatenate([same, jnp.zeros((cap, 128 - cap), F32)], axis=1)
    msg[0:cap, :] = -pick(sel_a.astype(BF16), prior[...])
    msg[cap:, :] = jnp.broadcast_to(live_a, (cap, prior.shape[1]))


def whiten_kernel(coef, sigma, measured, prior, t0h, t0l, t1h, t1l, u0h, u0l, u1h, u1l, weight, base, rvar, tau):
    length = coef.shape[1]
    half = length // 2
    c = coef[...]
    shifted = pltpu.roll(jnp.broadcast_to(c, (half, length)), 0, 1, stride=1, stride_axis=0)
    upper = iota((half, half), 1) >= iota((half, half), 0)
    t0 = jnp.where(upper, shifted[:, :half], 0.0)
    t1 = shifted[:, half:]
    for hi, lo, x in ((t0h, t0l, t0), (t1h, t1l, t1), (u0h, u0l, t0.T), (u1h, u1l, t1.T)):
        a, b = halves(x)
        hi[...] = a
        lo[...] = b
    size = jnp.sum(jnp.abs(c), axis=1, keepdims=True)
    scale = 1.0 / (4.0 * size * size + 64.0)
    tau[...] = jnp.broadcast_to(scale, tau.shape)
    sig = jnp.transpose(jnp.broadcast_to(sigma[...], (128, 128)))[:, 0:1]
    rsig = 1.0 / sig
    whitened = forward((measured[...] - prior[...]) * rsig, (t0h, t0l, t1h, t1l))
    h = EDGE / jnp.maximum(jnp.abs(whitened), EDGE)
    weight[...] = h
    base[...] = backward(h * whitened, (u0h, u0l, u1h, u1l)) * rsig
    rvar[...] = jnp.broadcast_to(rsig * rsig * scale, rvar.shape)


def first_kernel(demand, prior, got, s_b, inc, l_a, l_b, match, part, msg, l_am):
    cap = s_b.shape[0]
    live = jnp.sum(jnp.where(iota((cap, cap), 0) == iota((cap, cap), 1), got[cap:, 0:cap], 0.0), axis=0, keepdims=True)
    masked = (l_a[...].astype(F32) * live).astype(BF16)
    l_am[...] = masked
    part[...] = demand[...] - pick(inc[...], prior[...]) + pick(masked, got[0:cap, :])
    msg[0:cap, :] = -pick(s_b[...], prior[...])
    msg[cap : 2 * cap, :] = pick(l_b[...].T, part[...])
    msg[2 * cap :, :] = jnp.broadcast_to(match[:, 0:1], (cap, prior.shape[1]))
    msg[2 * cap :, 0:128] = match[...]


def meet(near, gain, part, sent, got, s_a, s_b, inc, l_am, l_b, match, w_out, msg):
    cap = s_a.shape[0]
    y = part[...] + pick(l_b[...], got[0:cap, :])
    y_far = got[cap : 2 * cap, :] + pick(match, sent[0:cap, :])
    w = near + gain * (pick(inc[...].T, y) + pick(s_b[...].T, y_far))
    w_out[...] = w
    msg[0:cap, :] = pick(l_am[...].T, y)
    msg[cap:, :] = pick(s_a[...], w)
    return y


def meet_first(base, part, sent, got, s_a, s_b, inc, l_am, l_b, w_out, msg, match):
    cap = s_a.shape[0]
    match[...] = got[2 * cap :, 0:128]
    meet(base[...], PENALTY, part, sent, got, s_a, s_b, inc, l_am, l_b, match[:, 0:cap].astype(BF16), w_out, msg)


def meet_next(q, rvar, tau, part, sent, got, s_a, s_b, inc, l_am, l_b, match, w_out, msg):
    cap = s_a.shape[0]
    near = q[...] * rvar[:, 0:1]
    meet(near, PENALTY * tau[0:1, 0:1], part, sent, got, s_a, s_b, inc, l_am, l_b, match[:, 0:cap].astype(BF16), w_out, msg)


def meet_last(r0m, r1m, r2m, r, q, rvar, tau, part, sent, got, s_a, s_b, inc, l_am, l_b, match, w_out, msg, row):
    cap = s_a.shape[0]
    near = q[...] * rvar[:, 0:1]
    gain = PENALTY * tau[0:1, 0:1]
    y = meet(near, gain, part, sent, got, s_a, s_b, inc, l_am, l_b, match[:, 0:cap].astype(BF16), w_out, msg)
    m5 = lanes_sum(r[...] * near) + gain * lanes_sum(y * y)
    lane = iota((1, 128), 1) // 16
    out = jnp.zeros((1, 128), F32)
    for g, tile in enumerate((r0m[0:8, :], r1m[0:8, :], r1m[8:16, :], r2m[0:8, :], r2m[8:16, :], m5)):
        x = jnp.sum(tile, axis=0, keepdims=True)
        for s in (64, 32, 16):
            x = x + pltpu.roll(x, s, 1)
        out = jnp.where(lane == g, x, out)
    row[...] = jnp.broadcast_to(out, row.shape)


def open_kernel(gain, w, sent, got, s_a, s_b, inc, l_am, l_b, r_out, part, msg):
    cap = s_a.shape[0]
    r = w[...] + gain * pick(s_a[...].T, got[0:cap, :])
    arrived = got[cap:, :] + gain * sent[0:cap, :]
    r_out[...] = r
    part[...] = pick(inc[...], r) + pick(l_am[...], arrived)
    msg[0:cap, :] = pick(s_b[...], r)
    msg[cap:, :] = pick(l_b[...].T, part[...])


def open_first(*refs):
    open_kernel(PENALTY, *refs)


def open_next(tau, *refs):
    open_kernel(PENALTY * tau[0:1, 0:1], *refs)


def filter_first(r, weight, t0h, t0l, t1h, t1l, u0h, u0l, u1h, u1l, q, sums):
    x = r[...]
    q[...] = backward(weight[...] * forward(x, (t0h, t0l, t1h, t1l)), (u0h, u0l, u1h, u1l))
    sums[...] = lanes_sum(x * x)


def filter_next(r, before, weight, t0h, t0l, t1h, t1l, u0h, u0l, u1h, u1l, q, sums):
    x = r[...]
    q[...] = backward(weight[...] * forward(x, (t0h, t0l, t1h, t1l)), (u0h, u0l, u1h, u1l))
    sums[0:8, :] = lanes_sum(before[...] * x)
    sums[8:16, :] = lanes_sum(x * x)


def two_sum(a, b):
    s = a + b
    t = s - a
    return s, (a - (s - t)) + (b - t)


def split(a):
    t = 4097.0 * a
    hi = t - (t - a)
    return hi, a - hi


def two_prod(a, b):
    p = a * b
    ah, al = split(a)
    bh, bl = split(b)
    return p, ((ah * bh - p) + ah * bl + al * bh) + al * bl


def pair_add(x, y):
    s, e = two_sum(x[0], y[0])
    return two_sum(s, e + (x[1] + y[1]))


def finish_kernel(rows, tau, prior, r0, r1, r2, w, got, s_a, flows, residual):
    n = rows.shape[0]
    tot = (rows[0:8, :], jnp.zeros((8, 128), F32))
    for i in range(8, n, 8):
        s, e = two_sum(tot[0], rows[i : i + 8, :])
        tot = (s, tot[1] + e)
    for sh in (4, 2, 1):
        tot = pair_add(tot, tuple(pltpu.roll(t, sh, 0) for t in tot))
    for sh in (8, 4, 2, 1):
        tot = pair_add(tot, tuple(pltpu.roll(t, 128 - sh, 1) for t in tot))
    hi, lo = tot
    s0 = pltpu.roll(hi, 112, 1) / hi
    s = jnp.broadcast_to(s0[:, 0:1], (8, 128))
    mu = [hi]
    for _ in range(5):
        ph, pe = two_prod(hi, s)
        pe = pe + lo * s
        nh, nl = pltpu.roll(hi, 112, 1), pltpu.roll(lo, 112, 1)
        a, e = two_sum(nh, -ph)
        hi, lo = two_sum(a, e + (nl - pe))
        mu.append(hi)
    nu = [mu[k + 1] + s * mu[k] for k in range(5)]

    def form(u, v, m):
        total = None
        for i, a in enumerate(u):
            for j, b in enumerate(v):
                term = a * b * m[i + j]
                total = term if total is None else total + term
        return total

    def image(d):
        out = [s * x for x in d] + [jnp.zeros_like(s)]
        return [out[k] + (d[k - 1] if k else 0.0) for k in range(len(out))]

    a0 = mu[0] / nu[0]
    res1 = [mu[1] / nu[0], -a0]
    rr1 = form(res1, res1, mu)
    b0 = rr1 / mu[0]
    d1 = [res1[0] + b0, res1[1]]
    a1 = rr1 / form(d1, d1, nu)
    im1 = image(d1)
    res2 = [res1[0] - a1 * im1[0], res1[1] - a1 * im1[1], -a1 * im1[2]]
    rr2 = form(res2, res2, mu)
    b1 = rr2 / rr1
    d2 = [res2[0] + b1 * d1[0], res2[1] + b1 * d1[1], res2[2]]
    a2 = rr2 / form(d2, d2, nu)
    im2 = image(d2)
    f = [a0 + a1 * d1[0] + a2 * d2[0], a1 * d1[1] + a2 * d2[1], a2 * d2[2]]
    e = [res2[0] - a2 * im2[0], res2[1] - a2 * im2[1], res2[2] - a2 * im2[2], -a2 * im2[3]]
    ss = s * s
    f = [f[0] - s * f[1] + ss * f[2], f[1] - 2.0 * s * f[2], f[2]]
    e = [
        ((e[0] - s * e[1]) + ss * e[2]) - ss * s * e[3],
        (e[1] - 2.0 * s * e[2]) + 3.0 * ss * e[3],
        e[2] - 3.0 * s * e[3],
        e[3],
    ]
    f = [x[0:1, 0:1] * tau[0:1, 0:1] for x in f]
    e = [x[0:1, 0:1] for x in e]
    cap = s_a.shape[0]
    x0, x1, x2 = r0[...], r1[...], r2[...]
    x3 = w[...] + PENALTY * tau[0:1, 0:1] * pick(s_a[...].T, got[0:cap, :])
    flows[...] = prior[...] + ((f[0] * x0 + f[1] * x1) + f[2] * x2)
    residual[...] = ((e[0] * x0 + e[1] * x1) + e[2] * x2) + e[3] * x3


def call(kernel, outs, *args, smem=0, final=False):
    specs = [pl.BlockSpec(memory_space=pltpu.SMEM)] * smem
    specs += [pl.BlockSpec(memory_space=pltpu.VMEM)] * (len(args) - smem)
    args = args[:smem] + tuple(pltpu.with_memory_space_constraint(x, pltpu.VMEM) for x in args[smem:])
    shape = jax.ShapeDtypeStruct if final else pltpu.VMEM
    return pl.pallas_call(
        kernel,
        out_shape=tuple(shape(s, d) for s, d in outs),
        in_specs=specs,
        out_specs=tuple(pl.BlockSpec(memory_space=pltpu.VMEM) for _ in outs),
        compiler_params=pltpu.CompilerParams(vmem_limit_bytes=16 * 2**20),
    )(*args)


def shards(
    measured,
    prior_flow,
    demand,
    pipe_sigma,
    whiten_coef,
    pipe_tail,
    pipe_head,
    boundary_pipe,
    boundary_count,
    arrival_junction,
):
    pipes, hours = prior_flow.shape
    juncs = demand.shape[0]
    cap = boundary_pipe.shape[2]
    nets = lax.axis_size("net")
    devices = nets * lax.axis_size("hour")
    field = ((pipes, hours), F32)
    heads = ((juncs, hours), F32)
    msg2 = ((2 * cap, hours), F32)
    half = ((hours // 2, hours // 2), BF16)
    on_chip = [(i, i ^ 1) for i in range(nets)]
    across = [(i, i + 1) for i in range(1, nets - 1, 2)] + [(i + 1, i) for i in range(1, nets - 1, 2)]

    def swap(x):
        return lax.ppermute(x, "net", on_chip)

    def cross(x):
        return lax.ppermute(x, "net", across)

    odd = (lax.axis_index("net") % 2).astype(jnp.int32).reshape(1, 1)
    msg, s_a, s_b, inc, l_a, l_b, own_match = call(
        lists_kernel,
        [msg2, ((cap, pipes), BF16), ((cap, pipes), BF16), ((juncs, pipes), BF16), ((juncs, cap), BF16), ((juncs, cap), BF16), ((cap, 128), F32)],
        odd,
        prior_flow,
        boundary_pipe,
        boundary_count,
        arrival_junction,
        pipe_head.reshape(1, pipes),
        pipe_tail.reshape(1, pipes),
        smem=1,
    )
    got = swap(msg)
    part, msg, l_am = call(
        first_kernel,
        [heads, ((3 * cap, hours), F32), ((juncs, cap), BF16)],
        demand, prior_flow, got, s_b, inc, l_a, l_b, own_match,
    )
    got = cross(msg)
    out = call(
        whiten_kernel,
        [half] * 8 + [field, field, ((pipes, 128), F32), ((8, 128), F32)],
        whiten_coef.reshape(1, hours), pipe_sigma.reshape(1, pipes), measured, prior_flow,
    )
    taps, (weight, base, rvar, tau) = out[:8], out[8:]
    lists = (s_a, s_b, inc, l_am, l_b)
    w, msg, match = call(
        meet_first, [field, msg2, ((cap, 128), F32)], base, part, msg, got, *lists
    )
    fields, sums = [], []
    for step in range(3):
        got = swap(msg)
        if step == 0:
            r, part, msg = call(open_first, [field, heads, msg2], w, msg, got, *lists)
        else:
            r, part, msg = call(open_next, [field, heads, msg2], tau, w, msg, got, *lists)
        got = cross(msg)
        if step == 0:
            q, acc = call(filter_first, [field, ((8, 128), F32)], r, weight, *taps)
        else:
            q, acc = call(filter_next, [field, ((16, 128), F32)], r, fields[-1], weight, *taps)
        fields.append(r)
        sums.append(acc)
        if step < 2:
            w, msg = call(meet_next, [field, msg2], q, rvar, tau, part, msg, got, *lists, match)
    w, msg, row = call(
        meet_last, [field, msg2, ((devices, 128), F32)],
        *sums, r, q, rvar, tau, part, msg, got, *lists, match,
    )
    got = swap(msg)
    rows = lax.all_to_all(
        row.reshape(devices, 1, 128), ("net", "hour"), 0, 0, tiled=True
    ).reshape(devices, 128)
    return call(finish_kernel, [field, field], rows, tau, prior_flow, *fields, w, got, s_a, final=True)


def solution(mesh):
    placed = (
        P("net", "hour"),
        P("net", "hour"),
        P("net", "hour"),
        P("net"),
        P(),
        P("net"),
        P("net"),
        P("net", None, None),
        P("net", None),
        P("net", None, None),
    )
    return jax.shard_map(
        shards,
        mesh=mesh,
        in_specs=placed,
        out_specs=(P("net", "hour"), P("net", "hour")),
        check_vma=False,
    )
```

```python
import jax
import jax.numpy as jnp
from jax import lax
from jax.experimental import pallas as pl
from jax.experimental.pallas import tpu as pltpu
from jax.sharding import PartitionSpec as P

EDGE = 1.5
PENALTY = 4.0
F32 = jnp.float32
BF16 = jnp.bfloat16


def iota(shape, dim):
    return lax.broadcasted_iota(jnp.int32, shape, dim)


def thirds(v):
    a = v.astype(BF16)
    rest = v - a.astype(F32)
    b = rest.astype(BF16)
    c = (rest - b.astype(F32)).astype(BF16)
    return a, b, c


def halves(v):
    a = v.astype(BF16)
    return a, (v - a.astype(F32)).astype(BF16)


def mm(a, b):
    return jnp.dot(a, b, preferred_element_type=F32)


def pick(exact, v):
    a, b, c = thirds(v)
    return (mm(exact, c) + mm(exact, b)) + mm(exact, a)


def product(x, t_hi, t_lo):
    hi, lo = halves(x)
    return (mm(lo, t_hi) + mm(hi, t_lo)) + mm(hi, t_hi)


def forward(v, taps):
    t0h, t0l, t1h, t1l = taps
    rows = v.shape[0]
    half = v.shape[1] // 2
    both = jnp.concatenate([v[:, :half], v[:, half:]], axis=0)
    near = product(both, t0h[...], t0l[...])
    far = product(v[:, :half], t1h[...], t1l[...])
    return jnp.concatenate([near[:rows], near[rows:] + far], axis=1)


def backward(v, taps):
    t0h, t0l, t1h, t1l = taps
    rows = v.shape[0]
    half = v.shape[1] // 2
    both = jnp.concatenate([v[:, :half], v[:, half:]], axis=0)
    near = product(both, t0h[...], t0l[...])
    far = product(v[:, half:], t1h[...], t1l[...])
    return jnp.concatenate([near[:rows] + far, near[rows:]], axis=1)


def lanes_sum(v):
    rows, cols = v.shape
    total = None
    for i in range(0, rows, 8):
        for j in range(0, cols, 128):
            part = v[i : i + 8, j : j + 128]
            total = part if total is None else total + part
    return total


def column(row, n):
    return jnp.sum(jnp.where(iota((n, n), 0) == iota((n, n), 1), row, 0.0), axis=1, keepdims=True)


def lists_kernel(par, prior, bp, bc, aj, head, tail, msg, s_a, s_b, inc, l_a, l_b, match):
    cap = bp.shape[2]
    pipes = prior.shape[0]
    juncs = inc.shape[0]
    odd = par[0, 0] == 1

    def side(ref, flip):
        lower, upper = ref[0, 0:1, :].astype(F32), ref[0, 1:2, :].astype(F32)
        return jnp.where(odd != flip, lower, upper)

    counts = bc[0:1, :].astype(F32)
    count_a = jnp.where(odd, counts[:, 0:1], counts[:, 1:2])
    count_b = jnp.where(odd, counts[:, 1:2], counts[:, 0:1])
    slot = iota((cap, 1), 0).astype(F32)
    live_a = jnp.where(slot < count_a, 1.0, 0.0)
    live_b = jnp.where(slot < count_b, 1.0, 0.0)
    pipe = iota((cap, pipes), 1).astype(F32)
    sel_a = jnp.where(column(side(bp, False), cap) == pipe, live_a, 0.0)
    sel_b = jnp.where(column(side(bp, True), cap) == pipe, live_b, 0.0)
    inner = 1.0 - jnp.sum(sel_a + sel_b, axis=0, keepdims=True)
    junction = iota((juncs, pipes), 0)
    heads = jnp.where(junction == head[...], inner, 0.0)
    tails = jnp.where(junction == tail[...], 1.0, 0.0)
    s_a[...] = sel_a.astype(BF16)
    s_b[...] = sel_b.astype(BF16)
    inc[...] = (heads - tails).astype(BF16)
    land = iota((juncs, cap), 0).astype(F32)
    to_a, to_b = side(aj, False), side(aj, True)
    l_a[...] = jnp.where(land == to_a, 1.0, 0.0).astype(BF16)
    l_b[...] = jnp.where(land == to_b, 1.0, 0.0).astype(BF16)
    same = jnp.where(column(to_b, cap) == to_b, 1.0, 0.0)
    match[...] = jnp.concatenate([same, jnp.zeros((cap, 128 - cap), F32)], axis=1)
    msg[0:cap, :] = -pick(sel_a.astype(BF16), prior[...])
    msg[cap:, :] = jnp.broadcast_to(live_a, (cap, prior.shape[1]))


def whiten_kernel(coef, sigma, measured, prior, t0h, t0l, t1h, t1l, u0h, u0l, u1h, u1l, weight, base, rvar, tau):
    length = coef.shape[1]
    half = length // 2
    c = coef[...]
    shifted = pltpu.roll(jnp.broadcast_to(c, (half, length)), 0, 1, stride=1, stride_axis=0)
    upper = iota((half, half), 1) >= iota((half, half), 0)
    t0 = jnp.where(upper, shifted[:, :half], 0.0)
    t1 = shifted[:, half:]
    for hi, lo, x in ((t0h, t0l, t0), (t1h, t1l, t1), (u0h, u0l, t0.T), (u1h, u1l, t1.T)):
        a, b = halves(x)
        hi[...] = a
        lo[...] = b
    size = jnp.sum(jnp.abs(c), axis=1, keepdims=True)
    scale = 1.0 / (4.0 * size * size + 64.0)
    tau[...] = jnp.broadcast_to(scale, tau.shape)
    sig = jnp.transpose(jnp.broadcast_to(sigma[...], (128, 128)))[:, 0:1]
    rsig = 1.0 / sig
    whitened = forward((measured[...] - prior[...]) * rsig, (t0h, t0l, t1h, t1l))
    h = EDGE / jnp.maximum(jnp.abs(whitened), EDGE)
    weight[...] = h
    base[...] = backward(h * whitened, (u0h, u0l, u1h, u1l)) * rsig
    rvar[...] = jnp.broadcast_to(rsig * rsig * scale, rvar.shape)


def first_kernel(demand, prior, got, s_b, inc, l_a, l_b, match, part, msg, l_am):
    cap = s_b.shape[0]
    live = jnp.sum(jnp.where(iota((cap, cap), 0) == iota((cap, cap), 1), got[cap:, 0:cap], 0.0), axis=0, keepdims=True)
    masked = (l_a[...].astype(F32) * live).astype(BF16)
    l_am[...] = masked
    part[...] = demand[...] - pick(inc[...], prior[...]) + pick(masked, got[0:cap, :])
    msg[0:cap, :] = -pick(s_b[...], prior[...])
    msg[cap : 2 * cap, :] = pick(l_b[...].T, part[...])
    msg[2 * cap :, :] = jnp.broadcast_to(match[:, 0:1], (cap, prior.shape[1]))
    msg[2 * cap :, 0:128] = match[...]


def meet(near, gain, part, sent, got, s_a, s_b, inc, l_am, l_b, match, w_out, msg):
    cap = s_a.shape[0]
    y = part[...] + pick(l_b[...], got[0:cap, :])
    y_far = got[cap : 2 * cap, :] + pick(match, sent[0:cap, :])
    w = near + gain * (pick(inc[...].T, y) + pick(s_b[...].T, y_far))
    w_out[...] = w
    msg[0:cap, :] = pick(l_am[...].T, y)
    msg[cap:, :] = pick(s_a[...], w)
    return y


def meet_first(base, part, sent, got, s_a, s_b, inc, l_am, l_b, w_out, msg, match):
    cap = s_a.shape[0]
    match[...] = got[2 * cap :, 0:128]
    meet(base[...], PENALTY, part, sent, got, s_a, s_b, inc, l_am, l_b, match[:, 0:cap].astype(BF16), w_out, msg)


def meet_next(q, rvar, tau, part, sent, got, s_a, s_b, inc, l_am, l_b, match, w_out, msg):
    cap = s_a.shape[0]
    near = q[...] * rvar[:, 0:1]
    meet(near, PENALTY * tau[0:1, 0:1], part, sent, got, s_a, s_b, inc, l_am, l_b, match[:, 0:cap].astype(BF16), w_out, msg)


def meet_last(r0m, r1m, r2m, r, q, rvar, tau, part, sent, got, s_a, s_b, inc, l_am, l_b, match, w_out, msg, row):
    cap = s_a.shape[0]
    near = q[...] * rvar[:, 0:1]
    gain = PENALTY * tau[0:1, 0:1]
    y = meet(near, gain, part, sent, got, s_a, s_b, inc, l_am, l_b, match[:, 0:cap].astype(BF16), w_out, msg)
    m5 = lanes_sum(r[...] * near) + gain * lanes_sum(y * y)
    lane = iota((1, 128), 1) // 16
    out = jnp.zeros((1, 128), F32)
    for g, tile in enumerate((r0m[0:8, :], r1m[0:8, :], r1m[8:16, :], r2m[0:8, :], r2m[8:16, :], m5)):
        x = jnp.sum(tile, axis=0, keepdims=True)
        for s in (64, 32, 16):
            x = x + pltpu.roll(x, s, 1)
        out = jnp.where(lane == g, x, out)
    row[...] = jnp.broadcast_to(out, row.shape)


def open_kernel(gain, w, sent, got, s_a, s_b, inc, l_am, l_b, r_out, part, msg):
    cap = s_a.shape[0]
    r = w[...] + gain * pick(s_a[...].T, got[0:cap, :])
    arrived = got[cap:, :] + gain * sent[0:cap, :]
    r_out[...] = r
    part[...] = pick(inc[...], r) + pick(l_am[...], arrived)
    msg[0:cap, :] = pick(s_b[...], r)
    msg[cap:, :] = pick(l_b[...].T, part[...])


def open_first(*refs):
    open_kernel(PENALTY, *refs)


def open_next(tau, *refs):
    open_kernel(PENALTY * tau[0:1, 0:1], *refs)


def filter_first(r, weight, t0h, t0l, t1h, t1l, u0h, u0l, u1h, u1l, q, sums):
    x = r[...]
    q[...] = backward(weight[...] * forward(x, (t0h, t0l, t1h, t1l)), (u0h, u0l, u1h, u1l))
    sums[...] = lanes_sum(x * x)


def filter_next(r, before, weight, t0h, t0l, t1h, t1l, u0h, u0l, u1h, u1l, q, sums):
    x = r[...]
    q[...] = backward(weight[...] * forward(x, (t0h, t0l, t1h, t1l)), (u0h, u0l, u1h, u1l))
    sums[0:8, :] = lanes_sum(before[...] * x)
    sums[8:16, :] = lanes_sum(x * x)


def two_sum(a, b):
    s = a + b
    t = s - a
    return s, (a - (s - t)) + (b - t)


def split(a):
    t = 4097.0 * a
    hi = t - (t - a)
    return hi, a - hi


def two_prod(a, b):
    p = a * b
    ah, al = split(a)
    bh, bl = split(b)
    return p, ((ah * bh - p) + ah * bl + al * bh) + al * bl


def pair_add(x, y):
    s, e = two_sum(x[0], y[0])
    return two_sum(s, e + (x[1] + y[1]))


def finish_kernel(rows, tau, prior, r0, r1, r2, w, got, s_a, flows, residual):
    n = rows.shape[0]
    tot = (rows[0:8, :], jnp.zeros((8, 128), F32))
    for i in range(8, n, 8):
        s, e = two_sum(tot[0], rows[i : i + 8, :])
        tot = (s, tot[1] + e)
    for sh in (4, 2, 1):
        tot = pair_add(tot, tuple(pltpu.roll(t, sh, 0) for t in tot))
    for sh in (8, 4, 2, 1):
        tot = pair_add(tot, tuple(pltpu.roll(t, 128 - sh, 1) for t in tot))
    hi, lo = tot
    s0 = pltpu.roll(hi, 112, 1) / hi
    s = jnp.broadcast_to(s0[:, 0:1], (8, 128))
    mu = [hi]
    for _ in range(5):
        ph, pe = two_prod(hi, s)
        pe = pe + lo * s
        nh, nl = pltpu.roll(hi, 112, 1), pltpu.roll(lo, 112, 1)
        a, e = two_sum(nh, -ph)
        hi, lo = two_sum(a, e + (nl - pe))
        mu.append(hi)
    nu = [mu[k + 1] + s * mu[k] for k in range(5)]

    def form(u, v, m):
        total = None
        for i, a in enumerate(u):
            for j, b in enumerate(v):
                term = a * b * m[i + j]
                total = term if total is None else total + term
        return total

    def image(d):
        out = [s * x for x in d] + [jnp.zeros_like(s)]
        return [out[k] + (d[k - 1] if k else 0.0) for k in range(len(out))]

    a0 = mu[0] / nu[0]
    res1 = [mu[1] / nu[0], -a0]
    rr1 = form(res1, res1, mu)
    b0 = rr1 / mu[0]
    d1 = [res1[0] + b0, res1[1]]
    a1 = rr1 / form(d1, d1, nu)
    im1 = image(d1)
    res2 = [res1[0] - a1 * im1[0], res1[1] - a1 * im1[1], -a1 * im1[2]]
    rr2 = form(res2, res2, mu)
    b1 = rr2 / rr1
    d2 = [res2[0] + b1 * d1[0], res2[1] + b1 * d1[1], res2[2]]
    a2 = rr2 / form(d2, d2, nu)
    im2 = image(d2)
    f = [a0 + a1 * d1[0] + a2 * d2[0], a1 * d1[1] + a2 * d2[1], a2 * d2[2]]
    e = [res2[0] - a2 * im2[0], res2[1] - a2 * im2[1], res2[2] - a2 * im2[2], -a2 * im2[3]]
    ss = s * s
    f = [f[0] - s * f[1] + ss * f[2], f[1] - 2.0 * s * f[2], f[2]]
    e = [
        ((e[0] - s * e[1]) + ss * e[2]) - ss * s * e[3],
        (e[1] - 2.0 * s * e[2]) + 3.0 * ss * e[3],
        e[2] - 3.0 * s * e[3],
        e[3],
    ]
    f = [x[0:1, 0:1] * tau[0:1, 0:1] for x in f]
    e = [x[0:1, 0:1] for x in e]
    cap = s_a.shape[0]
    x0, x1, x2 = r0[...], r1[...], r2[...]
    x3 = w[...] + PENALTY * tau[0:1, 0:1] * pick(s_a[...].T, got[0:cap, :])
    flows[...] = prior[...] + ((f[0] * x0 + f[1] * x1) + f[2] * x2)
    residual[...] = ((e[0] * x0 + e[1] * x1) + e[2] * x2) + e[3] * x3


def call(kernel, outs, *args, smem=0, final=False):
    specs = [pl.BlockSpec(memory_space=pltpu.SMEM)] * smem
    specs += [pl.BlockSpec(memory_space=pltpu.VMEM)] * (len(args) - smem)
    args = args[:smem] + tuple(pltpu.with_memory_space_constraint(x, pltpu.VMEM) for x in args[smem:])
    shape = jax.ShapeDtypeStruct if final else pltpu.VMEM
    return pl.pallas_call(
        kernel,
        out_shape=tuple(shape(s, d) for s, d in outs),
        in_specs=specs,
        out_specs=tuple(pl.BlockSpec(memory_space=pltpu.VMEM) for _ in outs),
        compiler_params=pltpu.CompilerParams(vmem_limit_bytes=16 * 2**20),
    )(*args)


def shards(
    measured,
    prior_flow,
    demand,
    pipe_sigma,
    whiten_coef,
    pipe_tail,
    pipe_head,
    boundary_pipe,
    boundary_count,
    arrival_junction,
):
    pipes, hours = prior_flow.shape
    juncs = demand.shape[0]
    cap = boundary_pipe.shape[2]
    nets = lax.axis_size("net")
    hour_blocks = lax.axis_size("hour")
    devices = nets * hour_blocks
    field = ((pipes, hours), F32)
    heads = ((juncs, hours), F32)
    msg2 = ((2 * cap, hours), F32)
    half = ((hours // 2, hours // 2), BF16)
    on_chip = [(i, i ^ 1) for i in range(nets)]
    across = []
    for h in range(hour_blocks):
        for i in range(1, nets - 1, 2):
            a, b = i * hour_blocks + h, (i + 1) * hour_blocks + h
            across += [(a, b), (b, a)]
        for i in (0, nets - 1):
            across.append((i * hour_blocks + h, i * hour_blocks + (h ^ 1)))

    def swap(x):
        return lax.ppermute(x, "net", on_chip)

    def cross(x):
        return lax.ppermute(x, ("net", "hour"), across)

    odd = (lax.axis_index("net") % 2).astype(jnp.int32).reshape(1, 1)
    msg, s_a, s_b, inc, l_a, l_b, own_match = call(
        lists_kernel,
        [msg2, ((cap, pipes), BF16), ((cap, pipes), BF16), ((juncs, pipes), BF16), ((juncs, cap), BF16), ((juncs, cap), BF16), ((cap, 128), F32)],
        odd,
        prior_flow,
        boundary_pipe,
        boundary_count,
        arrival_junction,
        pipe_head.reshape(1, pipes),
        pipe_tail.reshape(1, pipes),
        smem=1,
    )
    got = swap(msg)
    part, msg, l_am = call(
        first_kernel,
        [heads, ((3 * cap, hours), F32), ((juncs, cap), BF16)],
        demand, prior_flow, got, s_b, inc, l_a, l_b, own_match,
    )
    got = cross(msg)
    out = call(
        whiten_kernel,
        [half] * 8 + [field, field, ((pipes, 128), F32), ((8, 128), F32)],
        whiten_coef.reshape(1, hours), pipe_sigma.reshape(1, pipes), measured, prior_flow,
    )
    taps, (weight, base, rvar, tau) = out[:8], out[8:]
    lists = (s_a, s_b, inc, l_am, l_b)
    w, msg, match = call(
        meet_first, [field, msg2, ((cap, 128), F32)], base, part, msg, got, *lists
    )
    fields, sums = [], []
    for step in range(3):
        got = swap(msg)
        if step == 0:
            r, part, msg = call(open_first, [field, heads, msg2], w, msg, got, *lists)
        else:
            r, part, msg = call(open_next, [field, heads, msg2], tau, w, msg, got, *lists)
        got = cross(msg)
        if step == 0:
            q, acc = call(filter_first, [field, ((8, 128), F32)], r, weight, *taps)
        else:
            q, acc = call(filter_next, [field, ((16, 128), F32)], r, fields[-1], weight, *taps)
        fields.append(r)
        sums.append(acc)
        if step < 2:
            w, msg = call(meet_next, [field, msg2], q, rvar, tau, part, msg, got, *lists, match)
    w, msg, row = call(
        meet_last, [field, msg2, ((devices, 128), F32)],
        *sums, r, q, rvar, tau, part, msg, got, *lists, match,
    )
    got = swap(msg)
    rows = lax.all_to_all(
        row.reshape(devices, 1, 128), ("net", "hour"), 0, 0, tiled=True
    ).reshape(devices, 128)
    return call(finish_kernel, [field, field], rows, tau, prior_flow, *fields, w, got, s_a, final=True)


def solution(mesh):
    placed = (
        P("net", "hour"),
        P("net", "hour"),
        P("net", "hour"),
        P("net"),
        P(),
        P("net"),
        P("net"),
        P("net", None, None),
        P("net", None),
        P("net", None, None),
    )
    return jax.shard_map(
        shards,
        mesh=mesh,
        in_specs=placed,
        out_specs=(P("net", "hour"), P("net", "hour")),
        check_vma=False,
    )
```

```python
import jax
import jax.numpy as jnp
from jax import lax
from jax.experimental import pallas as pl
from jax.experimental.pallas import tpu as pltpu
from jax.sharding import PartitionSpec as P

EDGE = 1.5
PENALTY = 4.0
F32 = jnp.float32
BF16 = jnp.bfloat16


def iota(shape, dim):
    return lax.broadcasted_iota(jnp.int32, shape, dim)


def thirds(v):
    a = v.astype(BF16)
    rest = v - a.astype(F32)
    b = rest.astype(BF16)
    c = (rest - b.astype(F32)).astype(BF16)
    return a, b, c


def halves(v):
    a = v.astype(BF16)
    return a, (v - a.astype(F32)).astype(BF16)


def mm(a, b):
    return jnp.dot(a, b, preferred_element_type=F32)


def pick(exact, v):
    a, b, c = thirds(v)
    return (mm(exact, c) + mm(exact, b)) + mm(exact, a)


def product(x, t_hi, t_lo):
    hi, lo = halves(x)
    return (mm(lo, t_hi) + mm(hi, t_lo)) + mm(hi, t_hi)


def forward(v, taps):
    t0h, t0l, t1h, t1l = taps
    rows = v.shape[0]
    half = v.shape[1] // 2
    both = jnp.concatenate([v[:, :half], v[:, half:]], axis=0)
    near = product(both, t0h[...], t0l[...])
    far = product(v[:, :half], t1h[...], t1l[...])
    return jnp.concatenate([near[:rows], near[rows:] + far], axis=1)


def backward(v, taps):
    t0h, t0l, t1h, t1l = taps
    rows = v.shape[0]
    half = v.shape[1] // 2
    both = jnp.concatenate([v[:, :half], v[:, half:]], axis=0)
    near = product(both, t0h[...], t0l[...])
    far = product(v[:, half:], t1h[...], t1l[...])
    return jnp.concatenate([near[:rows] + far, near[rows:]], axis=1)


def lanes_sum(v):
    rows, cols = v.shape
    total = None
    for i in range(0, rows, 8):
        for j in range(0, cols, 128):
            part = v[i : i + 8, j : j + 128]
            total = part if total is None else total + part
    return total


def column(row, n):
    return jnp.sum(jnp.where(iota((n, n), 0) == iota((n, n), 1), row, 0.0), axis=1, keepdims=True)


def stack3(v):
    a = v.astype(BF16).astype(F32)
    rest = v - a
    b = rest.astype(BF16).astype(F32)
    return jnp.concatenate([rest - b, b, a], axis=0).astype(BF16)


def thrice(m):
    return jnp.concatenate([m, m, m], axis=1).astype(BF16)


def fold(tile):
    x = jnp.sum(tile, axis=0, keepdims=True)
    for s in (64, 32, 16):
        x = x + pltpu.roll(x, s, 1)
    return x


def chosen(odd, ref, flip):
    lower, upper = ref[0, 0:1, :].astype(F32), ref[0, 1:2, :].astype(F32)
    return jnp.where(odd != flip, lower, upper)


def selectors(odd, bp, bc, pipes):
    cap = bp.shape[2]
    counts = bc[0:1, :].astype(F32)
    count_a = jnp.where(odd, counts[:, 0:1], counts[:, 1:2])
    count_b = jnp.where(odd, counts[:, 1:2], counts[:, 0:1])
    slot = iota((cap, 1), 0).astype(F32)
    live_a = jnp.where(slot < count_a, 1.0, 0.0)
    live_b = jnp.where(slot < count_b, 1.0, 0.0)
    pipe = iota((cap, pipes), 1).astype(F32)
    sel_a = jnp.where(column(chosen(odd, bp, False), cap) == pipe, live_a, 0.0)
    sel_b = jnp.where(column(chosen(odd, bp, True), cap) == pipe, live_b, 0.0)
    return sel_a, sel_b, live_a


def open_kernel(par, prior_in, *refs):
    count = 9
    ins, prior, copies = (prior_in, *refs[: count - 1]), refs[count - 1], refs[count - 1 : 2 * count - 1]
    msg, sems = refs[2 * count - 1 :]
    moves = [pltpu.make_async_copy(i, o, sems.at[k]) for k, (i, o) in enumerate(zip(ins, copies))]
    bp, bc = copies[1], copies[2]
    for m in moves:
        m.start()
    for m in moves[:3]:
        m.wait()
    cap = bp.shape[2]
    sel_a, _, live_a = selectors(par[0, 0] == 1, bp, bc, prior.shape[0])
    msg[0:cap, :] = -pick(sel_a.astype(BF16), prior[...])
    msg[cap:, :] = jnp.broadcast_to(live_a, (cap, prior.shape[1]))
    for m in moves[3:]:
        m.wait()


def lists_kernel(par, sent, prior, bp, bc, aj, head, tail, demand, s_a, s_at, inc, l_a, l_b, it_sb, out_b, out_a, mid_b, mid_a, own, gain, part, base):
    cap = bp.shape[2]
    pipes = prior.shape[0]
    juncs = inc.shape[0]
    odd = par[0, 0] == 1
    sel_a, sel_b, _ = selectors(odd, bp, bc, pipes)
    inner = 1.0 - jnp.sum(sel_a + sel_b, axis=0, keepdims=True)
    junction = iota((juncs, pipes), 0)
    heads = jnp.where(junction == head[...], inner, 0.0)
    tails = jnp.where(junction == tail[...], 1.0, 0.0)
    both = heads - tails
    land = iota((juncs, cap), 0).astype(F32)
    to_a, to_b = chosen(odd, aj, False), chosen(odd, aj, True)
    land_a = jnp.where(land == to_a, 1.0, 0.0)
    land_b = jnp.where(land == to_b, 1.0, 0.0)
    row = iota((cap, juncs), 1).astype(F32)
    land_at = jnp.where(row == column(to_a, cap), 1.0, 0.0)
    land_bt = jnp.where(row == column(to_b, cap), 1.0, 0.0)
    square = jnp.transpose(jnp.concatenate([both, jnp.zeros((pipes - juncs, pipes), F32)], axis=0))
    both_t = square[:, :juncs]
    pad = jnp.zeros((128 - 2 * cap, 128), F32)
    turned = jnp.transpose(jnp.concatenate([sel_a, sel_b, pad], axis=0))
    sel_at, sel_bt = turned[:, :cap], turned[:, cap : 2 * cap]
    both16, a16, b16 = both.astype(BF16), land_a.astype(BF16), land_b.astype(BF16)
    bt16 = land_bt.astype(BF16)
    s_a[...] = sel_a.astype(BF16)
    s_at[...] = sel_at.astype(BF16)
    inc[...] = both16
    l_a[...] = a16
    l_b[...] = b16
    it_sb[...] = jnp.concatenate([both_t, sel_bt], axis=1).astype(BF16)
    b_inc = mm(bt16, both16)
    a_inc = mm(sel_a.astype(BF16), both_t.astype(BF16))
    out_b[...] = jnp.concatenate([sel_b, b_inc], axis=0).astype(BF16)
    out_a[...] = jnp.concatenate([land_at, a_inc], axis=0).astype(BF16)
    mid_b[...] = thrice(jnp.concatenate([mm(b_inc.astype(BF16), sel_at.astype(BF16)), mm(bt16, a16)], axis=1))
    mid_a[...] = thrice(jnp.concatenate([mm(land_at.astype(BF16), b16), mm(a_inc.astype(BF16), b16)], axis=0))
    own[...] = mm(bt16, b16)
    gain[...] = jnp.full(gain.shape, PENALTY, F32)
    x = prior[...]
    p = demand[...] - pick(both16, x)
    part[...] = p
    base[0:cap, :] = -pick(sel_b.astype(BF16), x)
    base[cap:, :] = pick(bt16, p)


def across_first(got, base, mid_b, own, msg, arrived, live):
    cap = own.shape[0]
    arr = got[0:cap, :]
    arrived[...] = arr
    live[...] = got[cap:, 0:128]
    msg[0:cap, :] = base[0:cap, :]
    both = jnp.concatenate([jnp.zeros_like(arr), arr], axis=0)
    msg[cap : 2 * cap, :] = base[cap:, :] + mm(mid_b[...], stack3(both))
    msg[2 * cap :, :] = jnp.zeros((cap, msg.shape[1]), F32)
    msg[2 * cap :, 0:cap] = own[...]


def across_next(gain, sent, got, live, base, mid_b, msg, arrived):
    cap = live.shape[0]
    g = gain[0:1, 0:1]
    added = g * got[0:cap, :]
    arr = got[cap:, :] + (g * live[:, 0:1]) * sent[0:cap, :]
    arrived[...] = arr
    msg[0:cap, :] = base[0:cap, :]
    msg[cap:, :] = base[cap:, :] + mm(mid_b[...], stack3(jnp.concatenate([added, arr], axis=0)))


def back_kernel(gain, got, base, mid_a, msg):
    cap = got.shape[0] // 2 if got.shape[0] == msg.shape[0] else got.shape[0] // 3
    x = mm(mid_a[...], stack3(got[0:cap, :]))
    msg[0:cap, :] = base[0:cap, :] + x[0:cap]
    msg[cap:, :] = base[cap:, :] + gain[0:1, 0:1] * x[cap:]


def outward(gain, part, near, s_a, out_a, base):
    cap = s_a.shape[0]
    x = pick(out_a[...], part)
    base[0:cap, :] = x[0:cap]
    base[cap:, :] = gain * x[cap:] + pick(s_a[...], near)


def inside_first(
    sent, coef, sigma, measured, prior, part_in, arrived, l_a, s_a, out_a,
    t0h, t0l, t1h, t1l, u0h, u0l, u1h, u1l, weight, near, rvar, gain, part, base,
):
    length = coef.shape[1]
    half = length // 2
    c = coef[...]
    shifted = pltpu.roll(jnp.broadcast_to(c, (half, length)), 0, 1, stride=1, stride_axis=0)
    upper = iota((half, half), 1) >= iota((half, half), 0)
    t0 = jnp.where(upper, shifted[:, :half], 0.0)
    t1 = shifted[:, half:]
    for hi, lo, x in ((t0h, t0l, t0), (t1h, t1l, t1), (u0h, u0l, t0.T), (u1h, u1l, t1.T)):
        a, b = halves(x)
        hi[...] = a
        lo[...] = b
    size = jnp.sum(jnp.abs(c), axis=1, keepdims=True)
    scale = 1.0 / (4.0 * size * size + 64.0)
    gain[...] = jnp.broadcast_to(PENALTY * scale, gain.shape)
    sig = jnp.transpose(jnp.broadcast_to(sigma[...], (128, 128)))[:, 0:1]
    rsig = 1.0 / sig
    whitened = forward((measured[...] - prior[...]) * rsig, (t0h, t0l, t1h, t1l))
    h = EDGE / jnp.maximum(jnp.abs(whitened), EDGE)
    weight[...] = h
    n = backward(h * whitened, (u0h, u0l, u1h, u1l)) * rsig
    near[...] = n
    rvar[...] = jnp.broadcast_to(rsig * rsig * scale, rvar.shape)
    p = part_in[...] + pick(l_a[...], arrived[...])
    part[...] = p
    outward(PENALTY, p, n, s_a, out_a, base)


def inside(gain0, gain, sent, w, got, arrived, weight, rvar, s_a, s_at, inc, l_a, out_a, taps, r_out, part, near, base):
    cap = s_a.shape[0]
    r = w[...] + gain0[0:1, 0:1] * pick(s_at[...], got[0:cap, :])
    r_out[...] = r
    p = pick(inc[...], r) + pick(l_a[...], arrived[...])
    part[...] = p
    n = backward(weight[...] * forward(r, taps[:4]), taps[4:]) * rvar[:, 0:1]
    near[...] = n
    outward(gain[0:1, 0:1], p, n, s_a, out_a, base)
    return r, p, n


def inside_one(*refs):
    *refs, sums = refs
    r, _, _ = inside(*refs[:13], refs[13:21], *refs[21:])
    sums[...] = lanes_sum(r * r)


def inside_two(before, *refs):
    *refs, sums = refs
    r, _, _ = inside(*refs[:13], refs[13:21], *refs[21:])
    sums[0:8, :] = lanes_sum(before[...] * r)
    sums[8:16, :] = lanes_sum(r * r)


def inside_three(before, sum0, sum1, *refs):
    *refs, row = refs
    gain = refs[1]
    r, p, n = inside(*refs[:13], refs[13:21], *refs[21:])
    tiles = (
        sum0[0:8, :], sum1[0:8, :], sum1[8:16, :], lanes_sum(before[...] * r), lanes_sum(r * r),
        lanes_sum(r * n) + gain[0:1, 0:1] * lanes_sum(p * p),
    )
    lane = iota((1, 128), 1) // 16
    out = jnp.zeros((1, 128), F32)
    for k, tile in enumerate(tiles):
        out = jnp.where(lane == k, fold(tile), out)
    row[...] = jnp.broadcast_to(out, row.shape)


def close_kernel(gain, sent, got, own, row, rows):
    cap = own.shape[0]
    f = got[0:cap, :]
    extra = f * (2.0 * sent[cap : 2 * cap, :] + pick(own[...].astype(BF16), f))
    x = gain[0:1, 0:1] * fold(lanes_sum(extra))
    out = row[0:1, :] + jnp.where(iota((1, 128), 1) // 16 == 5, x, 0.0)
    rows[...] = jnp.broadcast_to(out, rows.shape)


def join(gain, sent_back, got, sent, far, part, near, l_b, it_sb, w_out):
    cap = far.shape[0]
    f = got[0:cap, :]
    y = part[...] + pick(l_b[...], f)
    y_far = got[cap : 2 * cap, :] + pick(far[...].astype(BF16), sent[0:cap, :])
    w = near[...] + gain[0:1, 0:1] * pick(it_sb[...], jnp.concatenate([y, y_far], axis=0))
    w_out[...] = w
    return w


def join_first(gain, sent_back, got, sent, part, near, l_b, it_sb, out_b, w_out, base, far):
    cap = far.shape[0]
    far[...] = got[2 * cap :, 0:cap]
    w = join(gain, sent_back, got, sent, far, part, near, l_b, it_sb, w_out)
    base[...] = pick(out_b[...], w)


def join_next(gain, sent_back, got, sent, far, part, near, l_b, it_sb, out_b, w_out, base):
    w = join(gain, sent_back, got, sent, far, part, near, l_b, it_sb, w_out)
    base[...] = pick(out_b[...], w)


def two_sum(a, b):
    s = a + b
    t = s - a
    return s, (a - (s - t)) + (b - t)


def split(a):
    t = 4097.0 * a
    hi = t - (t - a)
    return hi, a - hi


def two_prod(a, b):
    p = a * b
    ah, al = split(a)
    bh, bl = split(b)
    return p, ((ah * bh - p) + ah * bl + al * bh) + al * bl


def pair_add(x, y):
    s, e = two_sum(x[0], y[0])
    return two_sum(s, e + (x[1] + y[1]))


def finish_kernel(rows, gain, prior, r0, r1, r2, w, got, s_at, flows, residual):
    n = rows.shape[0]
    tot = (rows[0:8, :], jnp.zeros((8, 128), F32))
    for i in range(8, n, 8):
        s, e = two_sum(tot[0], rows[i : i + 8, :])
        tot = (s, tot[1] + e)
    for sh in (4, 2, 1):
        tot = pair_add(tot, tuple(pltpu.roll(t, sh, 0) for t in tot))
    for sh in (8, 4, 2, 1):
        tot = pair_add(tot, tuple(pltpu.roll(t, 128 - sh, 1) for t in tot))
    hi, lo = tot
    s0 = pltpu.roll(hi, 112, 1) / hi
    s = jnp.broadcast_to(s0[:, 0:1], (8, 128))
    mu = [hi]
    for _ in range(5):
        ph, pe = two_prod(hi, s)
        pe = pe + lo * s
        nh, nl = pltpu.roll(hi, 112, 1), pltpu.roll(lo, 112, 1)
        a, e = two_sum(nh, -ph)
        hi, lo = two_sum(a, e + (nl - pe))
        mu.append(hi)
    nu = [mu[k + 1] + s * mu[k] for k in range(5)]

    def form(u, v, m):
        total = None
        for i, a in enumerate(u):
            for j, b in enumerate(v):
                term = a * b * m[i + j]
                total = term if total is None else total + term
        return total

    def image(d):
        out = [s * x for x in d] + [jnp.zeros_like(s)]
        return [out[k] + (d[k - 1] if k else 0.0) for k in range(len(out))]

    a0 = mu[0] / nu[0]
    res1 = [mu[1] / nu[0], -a0]
    rr1 = form(res1, res1, mu)
    b0 = rr1 / mu[0]
    d1 = [res1[0] + b0, res1[1]]
    a1 = rr1 / form(d1, d1, nu)
    im1 = image(d1)
    res2 = [res1[0] - a1 * im1[0], res1[1] - a1 * im1[1], -a1 * im1[2]]
    rr2 = form(res2, res2, mu)
    b1 = rr2 / rr1
    d2 = [res2[0] + b1 * d1[0], res2[1] + b1 * d1[1], res2[2]]
    a2 = rr2 / form(d2, d2, nu)
    im2 = image(d2)
    f = [a0 + a1 * d1[0] + a2 * d2[0], a1 * d1[1] + a2 * d2[1], a2 * d2[2]]
    e = [res2[0] - a2 * im2[0], res2[1] - a2 * im2[1], res2[2] - a2 * im2[2], -a2 * im2[3]]
    ss = s * s
    f = [f[0] - s * f[1] + ss * f[2], f[1] - 2.0 * s * f[2], f[2]]
    e = [
        ((e[0] - s * e[1]) + ss * e[2]) - ss * s * e[3],
        (e[1] - 2.0 * s * e[2]) + 3.0 * ss * e[3],
        e[2] - 3.0 * s * e[3],
        e[3],
    ]
    g = gain[0:1, 0:1]
    f = [x[0:1, 0:1] * (g * (1.0 / PENALTY)) for x in f]
    e = [x[0:1, 0:1] for x in e]
    cap = s_at.shape[1]
    x0, x1, x2 = r0[...], r1[...], r2[...]
    x3 = w[...] + g * pick(s_at[...], got[0:cap, :])
    flows[...] = prior[...] + ((f[0] * x0 + f[1] * x1) + f[2] * x2)
    residual[...] = ((e[0] * x0 + e[1] * x1) + e[2] * x2) + e[3] * x3


def call(kernel, outs, *args, smem=0, final=False):
    specs = [pl.BlockSpec(memory_space=pltpu.SMEM)] * smem
    specs += [pl.BlockSpec(memory_space=pltpu.VMEM)] * (len(args) - smem)
    args = args[:smem] + tuple(pltpu.with_memory_space_constraint(x, pltpu.VMEM) for x in args[smem:])
    shape = jax.ShapeDtypeStruct if final else pltpu.VMEM
    return pl.pallas_call(
        kernel,
        out_shape=tuple(shape(s, d) for s, d in outs),
        in_specs=specs,
        out_specs=tuple(pl.BlockSpec(memory_space=pltpu.VMEM) for _ in outs),
        compiler_params=pltpu.CompilerParams(vmem_limit_bytes=16 * 2**20),
    )(*args)


def bring(odd, args, msg):
    return pl.pallas_call(
        open_kernel,
        out_shape=tuple(pltpu.VMEM(x.shape, x.dtype) for x in args) + (pltpu.VMEM(*msg),),
        in_specs=[pl.BlockSpec(memory_space=pltpu.SMEM)] + [pl.BlockSpec(memory_space=pltpu.HBM)] * len(args),
        out_specs=tuple(pl.BlockSpec(memory_space=pltpu.VMEM) for _ in range(len(args) + 1)),
        scratch_shapes=[pltpu.SemaphoreType.DMA((len(args),))],
        compiler_params=pltpu.CompilerParams(vmem_limit_bytes=16 * 2**20),
    )(odd, *(pltpu.with_memory_space_constraint(x, pltpu.HBM) for x in args))


def shards(
    measured,
    prior_flow,
    demand,
    pipe_sigma,
    whiten_coef,
    pipe_tail,
    pipe_head,
    boundary_pipe,
    boundary_count,
    arrival_junction,
):
    pipes, hours = prior_flow.shape
    juncs = demand.shape[0]
    cap = boundary_pipe.shape[2]
    nets = lax.axis_size("net")
    hour_blocks = lax.axis_size("hour")
    devices = nets * hour_blocks
    field = ((pipes, hours), F32)
    heads = ((juncs, hours), F32)
    slots = ((cap, hours), F32)
    msg2 = ((2 * cap, hours), F32)
    msg3 = ((3 * cap, hours), F32)
    tile = ((8, 128), F32)
    half = ((hours // 2, hours // 2), BF16)
    on_chip = [(i, i ^ 1) for i in range(nets)]
    across = []
    for h in range(hour_blocks):
        for i in range(1, nets - 1, 2):
            a, b = i * hour_blocks + h, (i + 1) * hour_blocks + h
            across += [(a, b), (b, a)]
        for i in (0, nets - 1):
            across.append((i * hour_blocks + h, i * hour_blocks + (h ^ 1)))

    def swap(x):
        return lax.ppermute(x, "net", on_chip)

    def cross(x):
        return lax.ppermute(x, ("net", "hour"), across)

    odd = (lax.axis_index("net") % 2).astype(jnp.int32).reshape(1, 1)
    args = (
        prior_flow, boundary_pipe, boundary_count, arrival_junction,
        pipe_head.reshape(1, pipes), pipe_tail.reshape(1, pipes), demand, measured, whiten_coef.reshape(1, hours),
    )
    prior, bp, bc, aj, head, tail, dem, meas, coef, back = bring(odd, args, msg2)
    sigma = pipe_sigma.reshape(1, pipes)
    got = swap(back)
    s_a, s_at, inc, l_a, l_b, it_sb, out_b, out_a, mid_b, mid_a, own, gain0, part, base = call(
        lists_kernel,
        [
            ((cap, pipes), BF16), ((pipes, cap), BF16), ((juncs, pipes), BF16), ((juncs, cap), BF16),
            ((juncs, cap), BF16), ((pipes, juncs + cap), BF16), ((2 * cap, pipes), BF16), ((2 * cap, juncs), BF16),
            ((cap, 6 * cap), BF16), ((2 * cap, 3 * cap), BF16), ((cap, cap), F32), tile, heads, msg2,
        ],
        odd, back, prior, bp, bc, aj, head, tail, dem,
        smem=1,
    )
    sent, arrived, live = call(across_first, [msg3, slots, tile], got, base, mid_b, own)
    got = cross(sent)
    out = call(
        inside_first,
        [half] * 8 + [field, field, ((pipes, 128), F32), tile, heads, msg2],
        sent, coef, sigma, meas, prior, part, arrived, l_a, s_a, out_a,
    )
    taps, (weight, near, rvar, gain, part, base) = out[:8], out[8:]
    (back,) = call(back_kernel, [msg2], gain0, got, base, mid_a)
    back_got = swap(back)
    w, base, far = call(
        join_first, [field, msg2, ((cap, cap), F32)], gain0, back, got, sent, part, near, l_b, it_sb, out_b
    )
    fields, sums = [], []
    for step in range(3):
        g = gain if step else gain0
        sent, arrived = call(across_next, [msg2, slots], g, back, back_got, live, base, mid_b)
        got = cross(sent)
        given = (g, gain, sent, w, back_got, arrived, weight, rvar, s_a, s_at, inc, l_a, out_a, *taps)
        gives = [field, heads, field, msg2]
        if step == 0:
            r, part, near, base, acc = call(inside_one, gives + [tile], *given)
        elif step == 1:
            r, part, near, base, acc = call(inside_two, gives + [((16, 128), F32)], fields[-1], *given)
        else:
            r, part, near, base, acc = call(inside_three, gives + [tile], fields[-1], *sums, *given)
        fields.append(r)
        sums.append(acc)
        if step == 2:
            (rows,) = call(close_kernel, [((devices, 128), F32)], gain, sent, got, own, acc)
            rows = lax.all_to_all(
                rows.reshape(devices, 1, 128), ("net", "hour"), 0, 0, tiled=True
            ).reshape(devices, 128)
        (back,) = call(back_kernel, [msg2], gain, got, base, mid_a)
        back_got = swap(back)
        w, base = call(join_next, [field, msg2], gain, back, got, sent, far, part, near, l_b, it_sb, out_b)
    return call(finish_kernel, [field, field], rows, gain, prior, *fields, w, back_got, s_at, final=True)


def solution(mesh):
    placed = (
        P("net", "hour"),
        P("net", "hour"),
        P("net", "hour"),
        P("net"),
        P(),
        P("net"),
        P("net"),
        P("net", None, None),
        P("net", None),
        P("net", None, None),
    )
    return jax.shard_map(
        shards,
        mesh=mesh,
        in_specs=placed,
        out_specs=(P("net", "hour"), P("net", "hour")),
        check_vma=False,
    )
```

```python
import jax
import jax.numpy as jnp
from jax import lax
from jax.experimental import pallas as pl
from jax.experimental.pallas import tpu as pltpu
from jax.sharding import PartitionSpec as P

EDGE = 1.5
PENALTY = 4.0
F32 = jnp.float32
BF16 = jnp.bfloat16


def iota(shape, dim):
    return lax.broadcasted_iota(jnp.int32, shape, dim)


def thirds(v):
    a = v.astype(BF16)
    rest = v - a.astype(F32)
    b = rest.astype(BF16)
    c = (rest - b.astype(F32)).astype(BF16)
    return a, b, c


def halves(v):
    a = v.astype(BF16)
    return a, (v - a.astype(F32)).astype(BF16)


def mm(a, b):
    return jnp.dot(a, b, preferred_element_type=F32)


def pick(exact, v):
    a, b, c = thirds(v)
    return (mm(exact, c) + mm(exact, b)) + mm(exact, a)


def product(x, t_hi, t_lo):
    hi, lo = halves(x)
    return (mm(lo, t_hi) + mm(hi, t_lo)) + mm(hi, t_hi)


def forward(v, taps):
    t0h, t0l, t1h, t1l = taps
    rows = v.shape[0]
    half = v.shape[1] // 2
    both = jnp.concatenate([v[:, :half], v[:, half:]], axis=0)
    near = product(both, t0h[...], t0l[...])
    far = product(v[:, :half], t1h[...], t1l[...])
    return jnp.concatenate([near[:rows], near[rows:] + far], axis=1)


def backward(v, taps):
    t0h, t0l, t1h, t1l = taps
    rows = v.shape[0]
    half = v.shape[1] // 2
    both = jnp.concatenate([v[:, :half], v[:, half:]], axis=0)
    near = product(both, t0h[...], t0l[...])
    far = product(v[:, half:], t1h[...], t1l[...])
    return jnp.concatenate([near[:rows] + far, near[rows:]], axis=1)


def lanes_sum(v):
    rows, cols = v.shape
    total = None
    for i in range(0, rows, 8):
        for j in range(0, cols, 128):
            part = v[i : i + 8, j : j + 128]
            total = part if total is None else total + part
    return total


def column(row, n):
    return jnp.sum(jnp.where(iota((n, n), 0) == iota((n, n), 1), row, 0.0), axis=1, keepdims=True)


def stack3(v):
    a = v.astype(BF16).astype(F32)
    rest = v - a
    b = rest.astype(BF16).astype(F32)
    return jnp.concatenate([rest - b, b, a], axis=0).astype(BF16)


def thrice(m):
    return jnp.concatenate([m, m, m], axis=1).astype(BF16)


def fold(tile):
    hi, lo = tile, jnp.zeros_like(tile)
    for axis, shifts in ((0, (4, 2, 1)), (1, (64, 32, 16, 8, 4, 2, 1))):
        for s in shifts:
            hi, e = two_sum(hi, pltpu.roll(hi, s, axis))
            lo = (lo + pltpu.roll(lo, s, axis)) + e
    return hi[0:1, :], lo[0:1, :]


def chosen(odd, ref, flip):
    lower, upper = ref[0, 0:1, :].astype(F32), ref[0, 1:2, :].astype(F32)
    return jnp.where(odd != flip, lower, upper)


def selectors(odd, bp, bc, pipes):
    cap = bp.shape[2]
    counts = bc[0:1, :].astype(F32)
    count_a = jnp.where(odd, counts[:, 0:1], counts[:, 1:2])
    count_b = jnp.where(odd, counts[:, 1:2], counts[:, 0:1])
    slot = iota((cap, 1), 0).astype(F32)
    live_a = jnp.where(slot < count_a, 1.0, 0.0)
    live_b = jnp.where(slot < count_b, 1.0, 0.0)
    pipe = iota((cap, pipes), 1).astype(F32)
    sel_a = jnp.where(column(chosen(odd, bp, False), cap) == pipe, live_a, 0.0)
    sel_b = jnp.where(column(chosen(odd, bp, True), cap) == pipe, live_b, 0.0)
    return sel_a, sel_b


def is_odd():
    return lax.rem(lax.axis_index("net"), 2) == 1


def open_kernel(prior_in, *refs):
    count = 9
    ins, prior, copies = (prior_in, *refs[: count - 1]), refs[count - 1], refs[count - 1 : 2 * count - 1]
    msg, sems, pipe_of, count_of = refs[2 * count - 1 :]
    moves = [pltpu.make_async_copy(ins[1], pipe_of, sems.at[count]), pltpu.make_async_copy(ins[2], count_of, sems.at[count + 1])]
    moves += [pltpu.make_async_copy(i, o, sems.at[k]) for k, (i, o) in enumerate(zip(ins, copies))]
    for m in moves:
        m.start()
    for m in moves[:3]:
        m.wait()
    cap = pipe_of.shape[2]
    side = jnp.where(is_odd(), 0, 1)
    live = count_of[0, side]
    for k in range(cap):
        row = prior[pl.ds(pipe_of[0, side, k], 1), :]
        msg[k : k + 1, :] = jnp.where(k < live, -row, 0.0)
    msg[cap:, :] = jnp.where(iota((cap, prior.shape[1]), 0) < live, 1.0, 0.0)
    for m in moves[3:]:
        m.wait()


def lists_kernel(sent, prior, bp, bc, aj, head, tail, demand, s_a, s_at, inc, l_a, l_b, it_sb, out_b, out_a, mid_b, mid_a, own, gain, part, base):
    cap = bp.shape[2]
    pipes = prior.shape[0]
    juncs = inc.shape[0]
    odd = is_odd()
    sel_a, sel_b = selectors(odd, bp, bc, pipes)
    inner = 1.0 - jnp.sum(sel_a + sel_b, axis=0, keepdims=True)
    junction = iota((juncs, pipes), 0)
    heads = jnp.where(junction == head[...], inner, 0.0)
    tails = jnp.where(junction == tail[...], 1.0, 0.0)
    both = heads - tails
    land = iota((juncs, cap), 0).astype(F32)
    to_a, to_b = chosen(odd, aj, False), chosen(odd, aj, True)
    land_a = jnp.where(land == to_a, 1.0, 0.0)
    land_b = jnp.where(land == to_b, 1.0, 0.0)
    row = iota((cap, juncs), 1).astype(F32)
    land_at = jnp.where(row == column(to_a, cap), 1.0, 0.0)
    land_bt = jnp.where(row == column(to_b, cap), 1.0, 0.0)
    square = jnp.transpose(jnp.concatenate([both, jnp.zeros((pipes - juncs, pipes), F32)], axis=0))
    both_t = square[:, :juncs]
    pad = jnp.zeros((128 - 2 * cap, 128), F32)
    turned = jnp.transpose(jnp.concatenate([sel_a, sel_b, pad], axis=0))
    sel_at, sel_bt = turned[:, :cap], turned[:, cap : 2 * cap]
    both16, a16, b16 = both.astype(BF16), land_a.astype(BF16), land_b.astype(BF16)
    bt16 = land_bt.astype(BF16)
    s_a[...] = sel_a.astype(BF16)
    s_at[...] = sel_at.astype(BF16)
    inc[...] = both16
    l_a[...] = a16
    l_b[...] = b16
    it_sb[...] = jnp.concatenate([both_t, sel_bt], axis=1).astype(BF16)
    b_inc = mm(bt16, both16)
    a_inc = mm(sel_a.astype(BF16), both_t.astype(BF16))
    out_b[...] = jnp.concatenate([sel_b, b_inc], axis=0).astype(BF16)
    out_a[...] = jnp.concatenate([land_at, a_inc], axis=0).astype(BF16)
    mid_b[...] = thrice(jnp.concatenate([mm(b_inc.astype(BF16), sel_at.astype(BF16)), mm(bt16, a16)], axis=1))
    mid_a[...] = thrice(jnp.concatenate([mm(land_at.astype(BF16), b16), mm(a_inc.astype(BF16), b16)], axis=0))
    own[...] = mm(bt16, b16)
    gain[...] = jnp.full(gain.shape, PENALTY, F32)
    x = prior[...]
    p = demand[...] - pick(both16, x)
    part[...] = p
    base[0:cap, :] = -pick(sel_b.astype(BF16), x)
    base[cap:, :] = pick(bt16, p)


def across_first(got, base, mid_b, own, msg, arrived, live):
    cap = own.shape[0]
    arr = got[0:cap, :]
    arrived[...] = arr
    live[...] = got[cap:, 0:128]
    msg[0:cap, :] = base[0:cap, :]
    both = jnp.concatenate([jnp.zeros_like(arr), arr], axis=0)
    msg[cap : 2 * cap, :] = base[cap:, :] + mm(mid_b[...], stack3(both))
    msg[2 * cap :, :] = jnp.zeros((cap, msg.shape[1]), F32)
    msg[2 * cap :, 0:cap] = own[...]


def across_next(gain, sent, got, live, base, mid_b, msg, arrived):
    cap = live.shape[0]
    g = gain[0:1, 0:1]
    added = g * got[0:cap, :]
    arr = got[cap:, :] + (g * live[:, 0:1]) * sent[0:cap, :]
    arrived[...] = arr
    msg[0:cap, :] = base[0:cap, :]
    msg[cap:, :] = base[cap:, :] + mm(mid_b[...], stack3(jnp.concatenate([added, arr], axis=0)))


def whole_kernel(gain, w, got, s_at, r_out):
    cap = s_at.shape[1]
    r_out[...] = w[...] + gain[0:1, 0:1] * pick(s_at[...], got[0:cap, :])


def back_kernel(gain, got, base, mid_a, msg):
    cap = got.shape[0] // 2 if got.shape[0] == msg.shape[0] else got.shape[0] // 3
    x = mm(mid_a[...], stack3(got[0:cap, :]))
    msg[0:cap, :] = base[0:cap, :] + x[0:cap]
    msg[cap:, :] = base[cap:, :] + gain[0:1, 0:1] * x[cap:]


def outward(gain, part, near, s_a, out_a, base):
    cap = s_a.shape[0]
    x = pick(out_a[...], part)
    base[0:cap, :] = x[0:cap]
    base[cap:, :] = gain * x[cap:] + pick(s_a[...], near)


def inside_first(
    sent, coef, sigma, measured, prior, part_in, arrived, l_a, s_a, out_a,
    t0h, t0l, t1h, t1l, u0h, u0l, u1h, u1l, weight, near, rvar, gain, part, base,
):
    length = coef.shape[1]
    half = length // 2
    c = coef[...]
    shifted = pltpu.roll(jnp.broadcast_to(c, (half, length)), 0, 1, stride=1, stride_axis=0)
    upper = iota((half, half), 1) >= iota((half, half), 0)
    t0 = jnp.where(upper, shifted[:, :half], 0.0)
    t1 = shifted[:, half:]
    for hi, lo, x in ((t0h, t0l, t0), (t1h, t1l, t1), (u0h, u0l, t0.T), (u1h, u1l, t1.T)):
        a, b = halves(x)
        hi[...] = a
        lo[...] = b
    size = jnp.sum(jnp.abs(c), axis=1, keepdims=True)
    scale = 1.0 / (4.0 * size * size + 64.0)
    gain[...] = jnp.broadcast_to(PENALTY * scale, gain.shape)
    sig = jnp.transpose(jnp.broadcast_to(sigma[...], (128, 128)))[:, 0:1]
    rsig = 1.0 / sig
    whitened = forward((measured[...] - prior[...]) * rsig, (t0h, t0l, t1h, t1l))
    h = EDGE / jnp.maximum(jnp.abs(whitened), EDGE)
    weight[...] = h
    n = backward(h * whitened, (u0h, u0l, u1h, u1l)) * rsig
    near[...] = n
    rvar[...] = jnp.broadcast_to(rsig * rsig * scale, rvar.shape)
    p = part_in[...] + pick(l_a[...], arrived[...])
    part[...] = p
    outward(PENALTY, p, n, s_a, out_a, base)


def inside(gain0, gain, sent, w, got, arrived, weight, rvar, s_a, s_at, inc, l_a, out_a, taps, r_out, part, near, base):
    cap = s_a.shape[0]
    r = w[...] + gain0[0:1, 0:1] * pick(s_at[...], got[0:cap, :])
    r_out[...] = r
    p = pick(inc[...], r) + pick(l_a[...], arrived[...])
    part[...] = p
    n = backward(weight[...] * forward(r, taps[:4]), taps[4:]) * rvar[:, 0:1]
    near[...] = n
    outward(gain[0:1, 0:1], p, n, s_a, out_a, base)
    return r, p, n


def inside_one(*refs):
    *refs, sums = refs
    r, _, _ = inside(*refs[:13], refs[13:21], *refs[21:])
    sums[...] = lanes_sum(r * r)


def inside_two(before, *refs):
    *refs, sums = refs
    r, _, _ = inside(*refs[:13], refs[13:21], *refs[21:])
    sums[0:8, :] = lanes_sum(before[...] * r)
    sums[8:16, :] = lanes_sum(r * r)


def inside_three(before, sum0, sum1, *refs):
    *refs, row = refs
    gain = refs[1]
    r, p, n = inside(*refs[:13], refs[13:21], *refs[21:])
    tiles = (
        sum0[0:8, :], sum1[0:8, :], sum1[8:16, :], lanes_sum(before[...] * r), lanes_sum(r * r),
        lanes_sum(r * n) + gain[0:1, 0:1] * lanes_sum(p * p),
    )
    lane = iota((1, 128), 1)
    out = jnp.zeros((1, 128), F32)
    for k, tile in enumerate(tiles):
        hi, lo = fold(tile)
        out = jnp.where(lane == 2 * k, hi, jnp.where(lane == 2 * k + 1, lo, out))
    row[...] = jnp.broadcast_to(out, row.shape)


def close_kernel(gain, sent, got, own, row, rows):
    cap = own.shape[0]
    f = got[0:cap, :]
    extra = f * (2.0 * sent[cap : 2 * cap, :] + pick(own[...].astype(BF16), f))
    x = gain[0:1, 0:1] * jnp.sum(lanes_sum(extra), axis=0, keepdims=True)
    x = x + pltpu.roll(x, 64, 1)
    out = jnp.where(iota((1, 128), 1) < 64, row[0:1, :], x)
    rows[...] = jnp.broadcast_to(out, rows.shape)


def join(gain, sent_back, got, sent, far, part, near, l_b, it_sb, w_out):
    cap = far.shape[0]
    f = got[0:cap, :]
    y = part[...] + pick(l_b[...], f)
    y_far = got[cap : 2 * cap, :] + pick(far[...].astype(BF16), sent[0:cap, :])
    w = near[...] + gain[0:1, 0:1] * pick(it_sb[...], jnp.concatenate([y, y_far], axis=0))
    w_out[...] = w
    return w


def join_first(gain, sent_back, got, sent, part, near, l_b, it_sb, out_b, w_out, base, far):
    cap = far.shape[0]
    far[...] = got[2 * cap :, 0:cap]
    w = join(gain, sent_back, got, sent, far, part, near, l_b, it_sb, w_out)
    base[...] = pick(out_b[...], w)


def join_next(gain, sent_back, got, sent, far, part, near, l_b, it_sb, out_b, w_out, base):
    w = join(gain, sent_back, got, sent, far, part, near, l_b, it_sb, w_out)
    base[...] = pick(out_b[...], w)


def two_sum(a, b):
    s = a + b
    t = s - a
    return s, (a - (s - t)) + (b - t)


def finish_kernel(rows, gain, prior, r0, r1, r2, r3, flows, residual, x_s, e_s, sems):
    n = rows.shape[0]
    tots = [(rows[i : i + 8, :], None) for i in range(0, n, 8)]
    while len(tots) > 1:
        pairs = []
        for (a, ae), (b, be) in zip(tots[::2], tots[1::2]):
            t, e = two_sum(a, b)
            pairs.append((t, e if ae is None else (ae + be) + e))
        tots = pairs
    hi, lo = tots[0]
    for sh in (4, 2, 1):
        hi, e = two_sum(hi, pltpu.roll(hi, sh, 0))
        lo = (lo + pltpu.roll(lo, sh, 0)) + e
    cut, cut_e = hi, lo
    for sh in (32, 16, 8, 4, 2, 1):
        cut, e = two_sum(cut, pltpu.roll(cut, 128 - sh, 1))
        cut_e = (cut_e + pltpu.roll(cut_e, 128 - sh, 1)) + e

    def lane(v, k):
        return jnp.broadcast_to(v[:, k : k + 1], (8, 128))

    m = []
    for k in range(6):
        low = lane(lo, 2 * k) + (lane(hi, 2 * k + 1) + lane(lo, 2 * k + 1))
        high = lane(hi, 2 * k)
        if k == 5:
            high, e = two_sum(high, lane(cut, 64))
            low = (low + lane(cut_e, 64)) + e
        m.append(two_sum(high, low))
    s = (m[1][0] / m[0][0]).astype(BF16).astype(F32)
    mu = [m[0][0]]
    for _ in range(5):
        level = []
        for (h0, l0), (h1, l1) in zip(m[:-1], m[1:]):
            top = h0.astype(BF16).astype(F32)
            a, e = two_sum(h1, -(s * top))
            b, e2 = two_sum(a, -(s * (h0 - top)))
            level.append((b, (e + e2) + (l1 - s * l0)))
        m = level
        mu.append(m[0][0] + m[0][1])
    nu = [mu[k + 1] + s * mu[k] for k in range(5)]

    def form(u, v, m):
        total = None
        for i, a in enumerate(u):
            for j, b in enumerate(v):
                term = a * b * m[i + j]
                total = term if total is None else total + term
        return total

    def image(d):
        out = [s * x for x in d] + [jnp.zeros_like(s)]
        return [out[k] + (d[k - 1] if k else 0.0) for k in range(len(out))]

    a0 = mu[0] / nu[0]
    res1 = [mu[1] / nu[0], -a0]
    rr1 = form(res1, res1, mu)
    b0 = rr1 / mu[0]
    d1 = [res1[0] + b0, res1[1]]
    a1 = rr1 / form(d1, d1, nu)
    im1 = image(d1)
    res2 = [res1[0] - a1 * im1[0], res1[1] - a1 * im1[1], -a1 * im1[2]]
    rr2 = form(res2, res2, mu)
    b1 = rr2 / rr1
    d2 = [res2[0] + b1 * d1[0], res2[1] + b1 * d1[1], res2[2]]
    a2 = rr2 / form(d2, d2, nu)
    im2 = image(d2)
    f = [a0 + a1 * d1[0] + a2 * d2[0], a1 * d1[1] + a2 * d2[1], a2 * d2[2]]
    e = [res2[0] - a2 * im2[0], res2[1] - a2 * im2[1], res2[2] - a2 * im2[2], -a2 * im2[3]]
    ss = s * s
    f = [f[0] - s * f[1] + ss * f[2], f[1] - 2.0 * s * f[2], f[2]]
    e = [
        ((e[0] - s * e[1]) + ss * e[2]) - ss * s * e[3],
        (e[1] - 2.0 * s * e[2]) + 3.0 * ss * e[3],
        e[2] - 3.0 * s * e[3],
        e[3],
    ]
    g = jnp.broadcast_to(gain[0:1, 0:1], (8, 128)) * (1.0 / PENALTY)
    f = [x[0:1, 0:1] * g[0:1, 0:1] for x in f]
    e = [x[0:1, 0:1] for x in e]
    moves = []
    step = prior.shape[0] // 4
    for i in range(4):
        at = slice(i * step, (i + 1) * step)
        x0, x1, x2 = r0[at, :], r1[at, :], r2[at, :]
        x_s[at, :] = prior[at, :] + ((f[0] * x0 + f[1] * x1) + f[2] * x2)
        e_s[at, :] = ((e[0] * x0 + e[1] * x1) + e[2] * x2) + e[3] * r3[at, :]
        for k, (src, dst) in enumerate(((x_s, flows), (e_s, residual))):
            moves.append(pltpu.make_async_copy(src.at[pl.ds(i * step, step), :], dst.at[pl.ds(i * step, step), :], sems.at[2 * i + k]))
            moves[-1].start()
    for m in moves:
        m.wait()


def call(kernel, outs, *args):
    return pl.pallas_call(
        kernel,
        out_shape=tuple(pltpu.VMEM(s, d) for s, d in outs),
        in_specs=[pl.BlockSpec(memory_space=pltpu.VMEM)] * len(args),
        out_specs=tuple(pl.BlockSpec(memory_space=pltpu.VMEM) for _ in outs),
        compiler_params=pltpu.CompilerParams(vmem_limit_bytes=16 * 2**20),
    )(*(pltpu.with_memory_space_constraint(x, pltpu.VMEM) for x in args))


def bring(args, msg):
    lists = (args[1], args[2])
    return pl.pallas_call(
        open_kernel,
        out_shape=tuple(pltpu.VMEM(x.shape, x.dtype) for x in args) + (pltpu.VMEM(*msg),),
        in_specs=[pl.BlockSpec(memory_space=pltpu.HBM)] * len(args),
        out_specs=tuple(pl.BlockSpec(memory_space=pltpu.VMEM) for _ in range(len(args) + 1)),
        scratch_shapes=[pltpu.SemaphoreType.DMA((len(args) + 2,))] + [pltpu.SMEM(x.shape, x.dtype) for x in lists],
        compiler_params=pltpu.CompilerParams(vmem_limit_bytes=16 * 2**20),
    )(*(pltpu.with_memory_space_constraint(x, pltpu.HBM) for x in args))


def finish(rows, *args):
    field = args[1]
    args = (rows, *args)
    return pl.pallas_call(
        finish_kernel,
        out_shape=(jax.ShapeDtypeStruct(field.shape, F32),) * 2,
        in_specs=[pl.BlockSpec(memory_space=pltpu.VMEM)] * len(args),
        out_specs=(pl.BlockSpec(memory_space=pltpu.HBM),) * 2,
        scratch_shapes=[pltpu.VMEM(field.shape, F32)] * 2 + [pltpu.SemaphoreType.DMA((8,))],
        compiler_params=pltpu.CompilerParams(vmem_limit_bytes=16 * 2**20),
    )(*(pltpu.with_memory_space_constraint(x, pltpu.VMEM) for x in args))


def shards(
    measured,
    prior_flow,
    demand,
    pipe_sigma,
    whiten_coef,
    pipe_tail,
    pipe_head,
    boundary_pipe,
    boundary_count,
    arrival_junction,
):
    pipes, hours = prior_flow.shape
    juncs = demand.shape[0]
    cap = boundary_pipe.shape[2]
    nets = lax.axis_size("net")
    hour_blocks = lax.axis_size("hour")
    devices = nets * hour_blocks
    field = ((pipes, hours), F32)
    heads = ((juncs, hours), F32)
    slots = ((cap, hours), F32)
    msg2 = ((2 * cap, hours), F32)
    msg3 = ((3 * cap, hours), F32)
    tile = ((8, 128), F32)
    half = ((hours // 2, hours // 2), BF16)
    on_chip = [(i, i ^ 1) for i in range(nets)]
    across = []
    for h in range(hour_blocks):
        for i in range(1, nets - 1, 2):
            a, b = i * hour_blocks + h, (i + 1) * hour_blocks + h
            across += [(a, b), (b, a)]
        for i in (0, nets - 1):
            across.append((i * hour_blocks + h, i * hour_blocks + (h ^ 1)))

    def swap(x):
        return lax.ppermute(x, "net", on_chip)

    def cross(x):
        return lax.ppermute(x, ("net", "hour"), across)

    args = (
        prior_flow, boundary_pipe, boundary_count, arrival_junction,
        pipe_head.reshape(1, pipes), pipe_tail.reshape(1, pipes), demand, measured, whiten_coef.reshape(1, hours),
    )
    prior, bp, bc, aj, head, tail, dem, meas, coef, back = bring(args, msg2)
    sigma = pipe_sigma.reshape(1, pipes)
    got = swap(back)
    s_a, s_at, inc, l_a, l_b, it_sb, out_b, out_a, mid_b, mid_a, own, gain0, part, base = call(
        lists_kernel,
        [
            ((cap, pipes), BF16), ((pipes, cap), BF16), ((juncs, pipes), BF16), ((juncs, cap), BF16),
            ((juncs, cap), BF16), ((pipes, juncs + cap), BF16), ((2 * cap, pipes), BF16), ((2 * cap, juncs), BF16),
            ((cap, 6 * cap), BF16), ((2 * cap, 3 * cap), BF16), ((cap, cap), F32), tile, heads, msg2,
        ],
        back, prior, bp, bc, aj, head, tail, dem,
    )
    sent, arrived, live = call(across_first, [msg3, slots, tile], got, base, mid_b, own)
    got = cross(sent)
    out = call(
        inside_first,
        [half] * 8 + [field, field, ((pipes, 128), F32), tile, heads, msg2],
        sent, coef, sigma, meas, prior, part, arrived, l_a, s_a, out_a,
    )
    taps, (weight, near, rvar, gain, part, base) = out[:8], out[8:]
    (back,) = call(back_kernel, [msg2], gain0, got, base, mid_a)
    back_got = swap(back)
    w, base, far = call(
        join_first, [field, msg2, ((cap, cap), F32)], gain0, back, got, sent, part, near, l_b, it_sb, out_b
    )
    fields, sums = [], []
    for step in range(3):
        g = gain if step else gain0
        sent, arrived = call(across_next, [msg2, slots], g, back, back_got, live, base, mid_b)
        got = cross(sent)
        given = (g, gain, sent, w, back_got, arrived, weight, rvar, s_a, s_at, inc, l_a, out_a, *taps)
        gives = [field, heads, field, msg2]
        if step == 0:
            r, part, near, base, acc = call(inside_one, gives + [tile], *given)
        elif step == 1:
            r, part, near, base, acc = call(inside_two, gives + [((16, 128), F32)], fields[-1], *given)
        else:
            r, part, near, base, acc = call(inside_three, gives + [tile], fields[-1], *sums, *given)
        fields.append(r)
        sums.append(acc)
        if step == 2:
            (rows,) = call(close_kernel, [((devices, 128), F32)], gain, sent, got, own, acc)
            rows = lax.all_to_all(
                rows.reshape(devices, 1, 128), ("net", "hour"), 0, 0, tiled=True
            ).reshape(devices, 128)
        (back,) = call(back_kernel, [msg2], gain, got, base, mid_a)
        back_got = swap(back)
        w, base = call(join_next, [field, msg2], gain, back, got, sent, far, part, near, l_b, it_sb, out_b)
    (last,) = call(whole_kernel, [field], gain, w, back_got, s_at)
    return finish(rows, gain, prior, *fields, last)


def solution(mesh):
    placed = (
        P("net", "hour"),
        P("net", "hour"),
        P("net", "hour"),
        P("net"),
        P(),
        P("net"),
        P("net"),
        P("net", None, None),
        P("net", None),
        P("net", None, None),
    )
    return jax.shard_map(
        shards,
        mesh=mesh,
        in_specs=placed,
        out_specs=(P("net", "hour"), P("net", "hour")),
        check_vma=False,
    )
```

```python
import jax
import jax.numpy as jnp
from jax import lax
from jax.experimental import pallas as pl
from jax.experimental.pallas import tpu as pltpu
from jax.sharding import PartitionSpec as P

EDGE = 1.5
PENALTY = 4.0
F32 = jnp.float32
BF16 = jnp.bfloat16


def iota(shape, dim):
    return lax.broadcasted_iota(jnp.int32, shape, dim)


def thirds(v):
    a = v.astype(BF16)
    rest = v - a.astype(F32)
    b = rest.astype(BF16)
    c = (rest - b.astype(F32)).astype(BF16)
    return a, b, c


def halves(v):
    a = v.astype(BF16)
    return a, (v - a.astype(F32)).astype(BF16)


def mm(a, b):
    return jnp.dot(a, b, preferred_element_type=F32)


def pick(exact, v):
    a, b, c = thirds(v)
    return (mm(exact, c) + mm(exact, b)) + mm(exact, a)


def product(x, t_hi, t_lo):
    hi, lo = halves(x)
    return (mm(lo, t_hi) + mm(hi, t_lo)) + mm(hi, t_hi)


def forward(v, taps):
    t0h, t0l, t1h, t1l = taps
    rows = v.shape[0]
    half = v.shape[1] // 2
    both = jnp.concatenate([v[:, :half], v[:, half:]], axis=0)
    near = product(both, t0h[...], t0l[...])
    far = product(v[:, :half], t1h[...], t1l[...])
    return jnp.concatenate([near[:rows], near[rows:] + far], axis=1)


def backward(v, taps):
    t0h, t0l, t1h, t1l = taps
    rows = v.shape[0]
    half = v.shape[1] // 2
    both = jnp.concatenate([v[:, :half], v[:, half:]], axis=0)
    near = product(both, t0h[...], t0l[...])
    far = product(v[:, half:], t1h[...], t1l[...])
    return jnp.concatenate([near[:rows] + far, near[rows:]], axis=1)


def lanes_sum(v):
    rows, cols = v.shape
    total = None
    for i in range(0, rows, 8):
        for j in range(0, cols, 128):
            part = v[i : i + 8, j : j + 128]
            total = part if total is None else total + part
    return total


def column(row, n):
    return jnp.sum(jnp.where(iota((n, n), 0) == iota((n, n), 1), row, 0.0), axis=1, keepdims=True)


def stack3(v):
    a = v.astype(BF16).astype(F32)
    rest = v - a
    b = rest.astype(BF16).astype(F32)
    return jnp.concatenate([rest - b, b, a], axis=0).astype(BF16)


def thrice(m):
    return jnp.concatenate([m, m, m], axis=1).astype(BF16)


def fold(tile):
    hi, lo = tile, jnp.zeros_like(tile)
    for axis, shifts in ((0, (4, 2, 1)), (1, (64, 32, 16, 8, 4, 2, 1))):
        for s in shifts:
            hi, e = two_sum(hi, pltpu.roll(hi, s, axis))
            lo = (lo + pltpu.roll(lo, s, axis)) + e
    return hi[0:1, :], lo[0:1, :]


def chosen(odd, ref, flip):
    lower, upper = ref[0, 0:1, :].astype(F32), ref[0, 1:2, :].astype(F32)
    return jnp.where(odd != flip, lower, upper)


def selectors(odd, bp, bc, pipes):
    cap = bp.shape[2]
    counts = bc[0:1, :].astype(F32)
    count_a = jnp.where(odd, counts[:, 0:1], counts[:, 1:2])
    count_b = jnp.where(odd, counts[:, 1:2], counts[:, 0:1])
    slot = iota((cap, 1), 0).astype(F32)
    live_a = jnp.where(slot < count_a, 1.0, 0.0)
    live_b = jnp.where(slot < count_b, 1.0, 0.0)
    pipe = iota((cap, pipes), 1).astype(F32)
    sel_a = jnp.where(column(chosen(odd, bp, False), cap) == pipe, live_a, 0.0)
    sel_b = jnp.where(column(chosen(odd, bp, True), cap) == pipe, live_b, 0.0)
    return sel_a, sel_b


def is_odd():
    return lax.rem(lax.axis_index("net"), 2) == 1


def open_kernel(prior_in, *refs):
    count = 8
    ins, prior, copies = (prior_in, *refs[: count - 1]), refs[count - 1], refs[count - 1 : 2 * count - 1]
    msg, sems, pipe_of, count_of = refs[2 * count - 1 :]
    moves = [pltpu.make_async_copy(ins[1], pipe_of, sems.at[count]), pltpu.make_async_copy(ins[2], count_of, sems.at[count + 1])]
    moves += [pltpu.make_async_copy(i, o, sems.at[k]) for k, (i, o) in enumerate(zip(ins, copies))]
    for m in moves:
        m.start()
    for m in moves[:3]:
        m.wait()
    cap = pipe_of.shape[2]
    side = jnp.where(is_odd(), 0, 1)
    live = count_of[0, side]
    for k in range(cap):
        row = prior[pl.ds(pipe_of[0, side, k], 1), :]
        msg[k : k + 1, :] = jnp.where(k < live, -row, 0.0)
    msg[cap:, :] = jnp.where(iota((cap, prior.shape[1]), 0) < live, 1.0, 0.0)
    for m in moves[3:]:
        m.wait()


def lists_kernel(sent, prior, bp, bc, aj, head, tail, demand, s_a, s_at, inc, l_a, l_b, it_sb, out_b, out_a, mid_b, mid_a, own, gain, part, base):
    cap = bp.shape[2]
    pipes = prior.shape[0]
    juncs = inc.shape[0]
    odd = is_odd()
    sel_a, sel_b = selectors(odd, bp, bc, pipes)
    inner = 1.0 - jnp.sum(sel_a + sel_b, axis=0, keepdims=True)
    junction = iota((juncs, pipes), 0)
    heads = jnp.where(junction == head[...], inner, 0.0)
    tails = jnp.where(junction == tail[...], 1.0, 0.0)
    both = heads - tails
    land = iota((juncs, cap), 0).astype(F32)
    to_a, to_b = chosen(odd, aj, False), chosen(odd, aj, True)
    land_a = jnp.where(land == to_a, 1.0, 0.0)
    land_b = jnp.where(land == to_b, 1.0, 0.0)
    row = iota((cap, juncs), 1).astype(F32)
    land_at = jnp.where(row == column(to_a, cap), 1.0, 0.0)
    land_bt = jnp.where(row == column(to_b, cap), 1.0, 0.0)
    square = jnp.transpose(jnp.concatenate([both, jnp.zeros((pipes - juncs, pipes), F32)], axis=0))
    both_t = square[:, :juncs]
    pad = jnp.zeros((128 - 2 * cap, 128), F32)
    turned = jnp.transpose(jnp.concatenate([sel_a, sel_b, pad], axis=0))
    sel_at, sel_bt = turned[:, :cap], turned[:, cap : 2 * cap]
    both16, a16, b16 = both.astype(BF16), land_a.astype(BF16), land_b.astype(BF16)
    bt16 = land_bt.astype(BF16)
    s_a[...] = sel_a.astype(BF16)
    s_at[...] = sel_at.astype(BF16)
    inc[...] = both16
    l_a[...] = a16
    l_b[...] = b16
    it_sb[...] = jnp.concatenate([both_t, sel_bt], axis=1).astype(BF16)
    b_inc = mm(bt16, both16)
    a_inc = mm(sel_a.astype(BF16), both_t.astype(BF16))
    out_b[...] = jnp.concatenate([sel_b, b_inc], axis=0).astype(BF16)
    out_a[...] = jnp.concatenate([land_at, a_inc], axis=0).astype(BF16)
    mid_b[...] = thrice(jnp.concatenate([mm(b_inc.astype(BF16), sel_at.astype(BF16)), mm(bt16, a16)], axis=1))
    mid_a[...] = thrice(jnp.concatenate([mm(land_at.astype(BF16), b16), mm(a_inc.astype(BF16), b16)], axis=0))
    own[...] = mm(bt16, b16)
    gain[...] = jnp.full(gain.shape, PENALTY, F32)
    x = prior[...]
    p = demand[...] - pick(both16, x)
    part[...] = p
    base[0:cap, :] = -pick(sel_b.astype(BF16), x)
    base[cap:, :] = pick(bt16, p)


def across_first(got, base, mid_b, own, msg, arrived, live):
    cap = own.shape[0]
    hours = base.shape[1]
    arr = got[0:cap, :]
    arrived[...] = arr
    live[...] = got[cap:, 0:128]
    msg[0:cap, 0:hours] = base[0:cap, :]
    both = jnp.concatenate([jnp.zeros_like(arr), arr], axis=0)
    msg[cap:, 0:hours] = base[cap:, :] + mm(mid_b[...], stack3(both))
    msg[:, hours:] = jnp.zeros((2 * cap, msg.shape[1] - hours), F32)
    msg[0:cap, hours : hours + cap] = own[...]


def wide(tile, v):
    return jnp.concatenate([tile] * (v.shape[1] // 128), axis=1)


def across_next(gain, sent, got, live, base, mid_b, msg, arrived):
    cap = live.shape[0]
    g = gain[...]
    added = wide(g, sent) * got[0:cap, :]
    arr = got[cap:, :] + wide(g * live[...], sent) * sent[0:cap, :]
    arrived[...] = arr
    msg[0:cap, :] = base[0:cap, :]
    msg[cap:, :] = base[cap:, :] + mm(mid_b[...], stack3(jnp.concatenate([added, arr], axis=0)))


def whole_kernel(gain, w, got, s_at, r_out):
    cap = s_at.shape[1]
    r_out[...] = w[...] + gain[0:1, 0:1] * pick(s_at[...], got[0:cap, :])


def back_kernel(gain, got, base, mid_a, msg):
    cap, hours = msg.shape[0] // 2, msg.shape[1]
    x = mm(mid_a[...], stack3(got[0:cap, 0:hours]))
    msg[0:cap, :] = base[0:cap, :] + x[0:cap]
    msg[cap:, :] = base[cap:, :] + wide(gain[...], msg) * x[cap:]


def outward(gain, part, near, s_a, out_a, base):
    cap = s_a.shape[0]
    x = pick(out_a[...], part)
    base[0:cap, :] = x[0:cap]
    base[cap:, :] = gain * x[cap:] + pick(s_a[...], near)


def inside_first(
    sent, coef, sigma, measured, prior, part_in, arrived, l_a, s_a, out_a,
    t0h, t0l, t1h, t1l, u0h, u0l, u1h, u1l, weight, near, rvar, gain, part, base,
):
    length = coef.shape[1]
    half = length // 2
    c = coef[...]
    shifted = pltpu.roll(jnp.broadcast_to(c, (half, length)), 0, 1, stride=1, stride_axis=0)
    upper = iota((half, half), 1) >= iota((half, half), 0)
    t0 = jnp.where(upper, shifted[:, :half], 0.0)
    t1 = shifted[:, half:]
    for hi, lo, x in ((t0h, t0l, t0), (t1h, t1l, t1), (u0h, u0l, t0.T), (u1h, u1l, t1.T)):
        a, b = halves(x)
        hi[...] = a
        lo[...] = b
    size = jnp.sum(jnp.abs(c), axis=1, keepdims=True)
    scale = 1.0 / (4.0 * size * size + 64.0)
    gain[...] = jnp.broadcast_to(PENALTY * scale, gain.shape)
    sig = jnp.transpose(jnp.broadcast_to(sigma[...], (128, 128)))[:, 0:1]
    rsig = 1.0 / sig
    whitened = forward((measured[...] - prior[...]) * rsig, (t0h, t0l, t1h, t1l))
    h = EDGE / jnp.maximum(jnp.abs(whitened), EDGE)
    weight[...] = h
    n = backward(h * whitened, (u0h, u0l, u1h, u1l)) * rsig
    near[...] = n
    rvar[...] = jnp.broadcast_to(rsig * rsig * scale, rvar.shape)
    p = part_in[...] + pick(l_a[...], arrived[...])
    part[...] = p
    outward(PENALTY, p, n, s_a, out_a, base)


def inside(gain0, gain, sent, w, got, arrived, weight, rvar, s_a, s_at, inc, l_a, out_a, taps, r_out, part, near, base):
    cap = s_a.shape[0]
    r = w[...] + gain0[0:1, 0:1] * pick(s_at[...], got[0:cap, :])
    r_out[...] = r
    p = pick(inc[...], r) + pick(l_a[...], arrived[...])
    part[...] = p
    n = backward(weight[...] * forward(r, taps[:4]), taps[4:]) * rvar[:, 0:1]
    near[...] = n
    outward(gain[0:1, 0:1], p, n, s_a, out_a, base)
    return r, p, n


def inside_one(*refs):
    *refs, sums = refs
    r, _, _ = inside(*refs[:13], refs[13:21], *refs[21:])
    sums[...] = lanes_sum(r * r)


def inside_two(before, *refs):
    *refs, sums = refs
    r, _, _ = inside(*refs[:13], refs[13:21], *refs[21:])
    sums[0:8, :] = lanes_sum(before[...] * r)
    sums[8:16, :] = lanes_sum(r * r)


def inside_three(before, sum0, sum1, *refs):
    *refs, row = refs
    gain = refs[1]
    r, p, n = inside(*refs[:13], refs[13:21], *refs[21:])
    tiles = (
        sum0[0:8, :], sum1[0:8, :], sum1[8:16, :], lanes_sum(before[...] * r), lanes_sum(r * r),
        lanes_sum(r * n) + gain[0:1, 0:1] * lanes_sum(p * p),
    )
    lane = iota((1, 128), 1)
    out = jnp.zeros((1, 128), F32)
    for k, tile in enumerate(tiles):
        hi, lo = fold(tile)
        out = jnp.where(lane == 2 * k, hi, jnp.where(lane == 2 * k + 1, lo, out))
    row[...] = jnp.broadcast_to(out, row.shape)


def close_kernel(gain, sent, got, own, row, rows):
    cap = own.shape[0]
    f = got[0:cap, :]
    extra = f * (2.0 * sent[cap : 2 * cap, :] + pick(own[...].astype(BF16), f))
    x = gain[0:1, 0:1] * jnp.sum(lanes_sum(extra), axis=0, keepdims=True)
    x = x + pltpu.roll(x, 64, 1)
    out = jnp.where(iota((1, 128), 1) < 64, row[0:1, :], x)
    rows[...] = jnp.broadcast_to(out, rows.shape)


def join(gain, sent_back, got, sent, far, part, near, l_b, it_sb, w_out):
    cap, hours = far.shape[0], part.shape[1]
    y = part[...] + pick(l_b[...], got[0:cap, 0:hours])
    y_far = got[cap:, 0:hours] + pick(far[...].astype(BF16), sent[0:cap, 0:hours])
    w = near[...] + gain[0:1, 0:1] * pick(it_sb[...], jnp.concatenate([y, y_far], axis=0))
    w_out[...] = w
    return w


def join_first(gain, sent_back, got, sent, part, near, l_b, it_sb, out_b, w_out, base, far):
    cap = far.shape[0]
    hours = part.shape[1]
    far[...] = got[0:cap, hours : hours + cap]
    w = join(gain, sent_back, got, sent, far, part, near, l_b, it_sb, w_out)
    base[...] = pick(out_b[...], w)


def join_next(gain, sent_back, got, sent, far, part, near, l_b, it_sb, out_b, w_out, base):
    w = join(gain, sent_back, got, sent, far, part, near, l_b, it_sb, w_out)
    base[...] = pick(out_b[...], w)


def two_sum(a, b):
    s = a + b
    t = s - a
    return s, (a - (s - t)) + (b - t)


def finish_kernel(rows, gain, prior, r0, r1, r2, r3, flows, residual, x_s, e_s, sems):
    n = rows.shape[0]
    tots = [(rows[i : i + 8, :], None) for i in range(0, n, 8)]
    while len(tots) > 1:
        pairs = []
        for (a, ae), (b, be) in zip(tots[::2], tots[1::2]):
            t, e = two_sum(a, b)
            pairs.append((t, e if ae is None else (ae + be) + e))
        tots = pairs
    hi, lo = tots[0]
    for sh in (4, 2, 1):
        hi, e = two_sum(hi, pltpu.roll(hi, sh, 0))
        lo = (lo + pltpu.roll(lo, sh, 0)) + e
    at = iota((8, 128), 1)
    cut = jnp.sum(jnp.where(at >= 64, hi + lo, 0.0), axis=1, keepdims=True)
    low = lo + (pltpu.roll(hi, 127, 1) + pltpu.roll(lo, 127, 1))
    hi, e = two_sum(hi, jnp.where(at == 10, cut, 0.0))
    hi, lo = two_sum(hi, low + e)

    def lane(v, k):
        return jnp.broadcast_to(v[:, k : k + 1], (8, 128))

    m = [(lane(hi, 2 * k), lane(lo, 2 * k)) for k in range(6)]
    s = (m[1][0] / m[0][0]).astype(BF16).astype(F32)
    mu = [m[0][0]]
    for _ in range(5):
        level = []
        for (h0, l0), (h1, l1) in zip(m[:-1], m[1:]):
            top = h0.astype(BF16).astype(F32)
            a, e = two_sum(h1, -(s * top))
            b, e2 = two_sum(a, -(s * (h0 - top)))
            level.append((b, (e + e2) + (l1 - s * l0)))
        m = level
        mu.append(m[0][0] + m[0][1])
    nu = [mu[k + 1] + s * mu[k] for k in range(5)]

    def form(u, v, m):
        total = None
        for i, a in enumerate(u):
            for j, b in enumerate(v):
                term = a * b * m[i + j]
                total = term if total is None else total + term
        return total

    def image(d):
        out = [s * x for x in d] + [jnp.zeros_like(s)]
        return [out[k] + (d[k - 1] if k else 0.0) for k in range(len(out))]

    a0 = mu[0] / nu[0]
    res1 = [mu[1] / nu[0], -a0]
    rr1 = form(res1, res1, mu)
    b0 = rr1 / mu[0]
    d1 = [res1[0] + b0, res1[1]]
    a1 = rr1 / form(d1, d1, nu)
    im1 = image(d1)
    res2 = [res1[0] - a1 * im1[0], res1[1] - a1 * im1[1], -a1 * im1[2]]
    rr2 = form(res2, res2, mu)
    b1 = rr2 / rr1
    d2 = [res2[0] + b1 * d1[0], res2[1] + b1 * d1[1], res2[2]]
    a2 = rr2 / form(d2, d2, nu)
    im2 = image(d2)
    f = [a0 + a1 * d1[0] + a2 * d2[0], a1 * d1[1] + a2 * d2[1], a2 * d2[2]]
    e = [res2[0] - a2 * im2[0], res2[1] - a2 * im2[1], res2[2] - a2 * im2[2], -a2 * im2[3]]
    ss = s * s
    f = [f[0] - s * f[1] + ss * f[2], f[1] - 2.0 * s * f[2], f[2]]
    e = [
        ((e[0] - s * e[1]) + ss * e[2]) - ss * s * e[3],
        (e[1] - 2.0 * s * e[2]) + 3.0 * ss * e[3],
        e[2] - 3.0 * s * e[3],
        e[3],
    ]
    g = jnp.broadcast_to(gain[0:1, 0:1], (8, 128)) * (1.0 / PENALTY)
    f = [x[0:1, 0:1] * g[0:1, 0:1] for x in f]
    e = [x[0:1, 0:1] for x in e]
    moves = []
    step = prior.shape[0] // 4
    for i in range(4):
        at = slice(i * step, (i + 1) * step)
        x0, x1, x2 = r0[at, :], r1[at, :], r2[at, :]
        x_s[at, :] = prior[at, :] + ((f[0] * x0 + f[1] * x1) + f[2] * x2)
        e_s[at, :] = ((e[0] * x0 + e[1] * x1) + e[2] * x2) + e[3] * r3[at, :]
        for k, (src, dst) in enumerate(((x_s, flows), (e_s, residual))):
            moves.append(pltpu.make_async_copy(src.at[pl.ds(i * step, step), :], dst.at[pl.ds(i * step, step), :], sems.at[2 * i + k]))
            moves[-1].start()
    for m in moves:
        m.wait()


def call(kernel, outs, *args):
    return pl.pallas_call(
        kernel,
        out_shape=tuple(pltpu.VMEM(s, d) for s, d in outs),
        in_specs=[pl.BlockSpec(memory_space=pltpu.VMEM)] * len(args),
        out_specs=tuple(pl.BlockSpec(memory_space=pltpu.VMEM) for _ in outs),
        compiler_params=pltpu.CompilerParams(vmem_limit_bytes=16 * 2**20),
    )(*(pltpu.with_memory_space_constraint(x, pltpu.VMEM) for x in args))


def bring(args, msg):
    lists = (args[1], args[2])
    return pl.pallas_call(
        open_kernel,
        out_shape=tuple(pltpu.VMEM(x.shape, x.dtype) for x in args) + (pltpu.VMEM(*msg),),
        in_specs=[pl.BlockSpec(memory_space=pltpu.HBM)] * len(args),
        out_specs=tuple(pl.BlockSpec(memory_space=pltpu.VMEM) for _ in range(len(args) + 1)),
        scratch_shapes=[pltpu.SemaphoreType.DMA((len(args) + 2,))] + [pltpu.SMEM(x.shape, x.dtype) for x in lists],
        compiler_params=pltpu.CompilerParams(vmem_limit_bytes=16 * 2**20),
    )(*(pltpu.with_memory_space_constraint(x, pltpu.HBM) for x in args))


def finish(rows, *args):
    field = args[1]
    args = (rows, *args)
    return pl.pallas_call(
        finish_kernel,
        out_shape=(jax.ShapeDtypeStruct(field.shape, F32),) * 2,
        in_specs=[pl.BlockSpec(memory_space=pltpu.VMEM)] * len(args),
        out_specs=(pl.BlockSpec(memory_space=pltpu.HBM),) * 2,
        scratch_shapes=[pltpu.VMEM(field.shape, F32)] * 2 + [pltpu.SemaphoreType.DMA((8,))],
        compiler_params=pltpu.CompilerParams(vmem_limit_bytes=16 * 2**20),
    )(*(pltpu.with_memory_space_constraint(x, pltpu.VMEM) for x in args))


def shards(
    measured,
    prior_flow,
    demand,
    pipe_sigma,
    whiten_coef,
    pipe_tail,
    pipe_head,
    boundary_pipe,
    boundary_count,
    arrival_junction,
):
    pipes, hours = prior_flow.shape
    juncs = demand.shape[0]
    cap = boundary_pipe.shape[2]
    nets = lax.axis_size("net")
    hour_blocks = lax.axis_size("hour")
    devices = nets * hour_blocks
    field = ((pipes, hours), F32)
    heads = ((juncs, hours), F32)
    slots = ((cap, hours), F32)
    msg2 = ((2 * cap, hours), F32)
    wide = ((2 * cap, hours + 128), F32)
    tile = ((8, 128), F32)
    half = ((hours // 2, hours // 2), BF16)
    on_chip = [(i, i ^ 1) for i in range(nets)]
    across = []
    for h in range(hour_blocks):
        for i in range(1, nets - 1, 2):
            a, b = i * hour_blocks + h, (i + 1) * hour_blocks + h
            across += [(a, b), (b, a)]
        for i in (0, nets - 1):
            across.append((i * hour_blocks + h, i * hour_blocks + (h ^ 1)))

    def swap(x):
        return lax.ppermute(x, "net", on_chip)

    def cross(x):
        return lax.ppermute(x, ("net", "hour"), across)

    args = (
        prior_flow, boundary_pipe, boundary_count, arrival_junction,
        pipe_head.reshape(1, pipes), pipe_tail.reshape(1, pipes), whiten_coef.reshape(1, hours), pipe_sigma.reshape(1, pipes),
    )
    prior, bp, bc, aj, head, tail, coef, sigma, back = bring(args, msg2)
    got = swap(back)
    s_a, s_at, inc, l_a, l_b, it_sb, out_b, out_a, mid_b, mid_a, own, gain0, part, base = call(
        lists_kernel,
        [
            ((cap, pipes), BF16), ((pipes, cap), BF16), ((juncs, pipes), BF16), ((juncs, cap), BF16),
            ((juncs, cap), BF16), ((pipes, juncs + cap), BF16), ((2 * cap, pipes), BF16), ((2 * cap, juncs), BF16),
            ((cap, 6 * cap), BF16), ((2 * cap, 3 * cap), BF16), ((cap, cap), F32), tile, heads, msg2,
        ],
        back, prior, bp, bc, aj, head, tail, demand,
    )
    sent, arrived, live = call(across_first, [wide, slots, tile], got, base, mid_b, own)
    got = cross(sent)
    out = call(
        inside_first,
        [half] * 8 + [field, field, ((pipes, 128), F32), tile, heads, msg2],
        sent, coef, sigma, measured, prior, part, arrived, l_a, s_a, out_a,
    )
    taps, (weight, near, rvar, gain, part, base) = out[:8], out[8:]
    (back,) = call(back_kernel, [msg2], gain0, got, base, mid_a)
    back_got = swap(back)
    w, base, far = call(
        join_first, [field, msg2, ((cap, cap), F32)], gain0, back, got, sent, part, near, l_b, it_sb, out_b
    )
    fields, sums = [], []
    for step in range(3):
        g = gain if step else gain0
        sent, arrived = call(across_next, [msg2, slots], g, back, back_got, live, base, mid_b)
        got = cross(sent)
        given = (g, gain, sent, w, back_got, arrived, weight, rvar, s_a, s_at, inc, l_a, out_a, *taps)
        gives = [field, heads, field, msg2]
        if step == 0:
            r, part, near, base, acc = call(inside_one, gives + [tile], *given)
        elif step == 1:
            r, part, near, base, acc = call(inside_two, gives + [((16, 128), F32)], fields[-1], *given)
        else:
            r, part, near, base, acc = call(inside_three, gives + [tile], fields[-1], *sums, *given)
        fields.append(r)
        sums.append(acc)
        if step == 2:
            (rows,) = call(close_kernel, [((devices, 128), F32)], gain, sent, got, own, acc)
            rows = lax.all_to_all(
                rows.reshape(devices, 1, 128), ("net", "hour"), 0, 0, tiled=True
            ).reshape(devices, 128)
        (back,) = call(back_kernel, [msg2], gain, got, base, mid_a)
        back_got = swap(back)
        w, base = call(join_next, [field, msg2], gain, back, got, sent, far, part, near, l_b, it_sb, out_b)
    (last,) = call(whole_kernel, [field], gain, w, back_got, s_at)
    return finish(rows, gain, prior, *fields, last)


def solution(mesh):
    placed = (
        P("net", "hour"),
        P("net", "hour"),
        P("net", "hour"),
        P("net"),
        P(),
        P("net"),
        P("net"),
        P("net", None, None),
        P("net", None),
        P("net", None, None),
    )
    return jax.shard_map(
        shards,
        mesh=mesh,
        in_specs=placed,
        out_specs=(P("net", "hour"), P("net", "hour")),
        check_vma=False,
    )
```

```python
import jax
import jax.numpy as jnp
from jax import lax
from jax.experimental import pallas as pl
from jax.experimental.pallas import tpu as pltpu
from jax.sharding import Mesh, PartitionSpec as P

NET = ("y", "z", "core")
EDGE = 1.5
PENALTY = 4.0
F32 = jnp.float32
BF16 = jnp.bfloat16


def iota(shape, dim):
    return lax.broadcasted_iota(jnp.int32, shape, dim)


def thirds(v):
    a = v.astype(BF16)
    rest = v - a.astype(F32)
    b = rest.astype(BF16)
    c = (rest - b.astype(F32)).astype(BF16)
    return a, b, c


def halves(v):
    a = v.astype(BF16)
    return a, (v - a.astype(F32)).astype(BF16)


def mm(a, b):
    return jnp.dot(a, b, preferred_element_type=F32)


def pick(exact, v):
    a, b, c = thirds(v)
    return (mm(exact, c) + mm(exact, b)) + mm(exact, a)


def product(x, t_hi, t_lo):
    hi, lo = halves(x)
    return (mm(lo, t_hi) + mm(hi, t_lo)) + mm(hi, t_hi)


def forward(v, taps):
    t0h, t0l, t1h, t1l = taps
    rows = v.shape[0]
    half = v.shape[1] // 2
    both = jnp.concatenate([v[:, :half], v[:, half:]], axis=0)
    near = product(both, t0h[...], t0l[...])
    far = product(v[:, :half], t1h[...], t1l[...])
    return jnp.concatenate([near[:rows], near[rows:] + far], axis=1)


def backward(v, taps):
    t0h, t0l, t1h, t1l = taps
    rows = v.shape[0]
    half = v.shape[1] // 2
    both = jnp.concatenate([v[:, :half], v[:, half:]], axis=0)
    near = product(both, t0h[...], t0l[...])
    far = product(v[:, half:], t1h[...], t1l[...])
    return jnp.concatenate([near[:rows] + far, near[rows:]], axis=1)


def lanes_sum(v):
    rows, cols = v.shape
    total = None
    for i in range(0, rows, 8):
        for j in range(0, cols, 128):
            part = v[i : i + 8, j : j + 128]
            total = part if total is None else total + part
    return total


def column(row, n):
    return jnp.sum(jnp.where(iota((n, n), 0) == iota((n, n), 1), row, 0.0), axis=1, keepdims=True)


def stack3(v):
    a = v.astype(BF16).astype(F32)
    rest = v - a
    b = rest.astype(BF16).astype(F32)
    return jnp.concatenate([rest - b, b, a], axis=0).astype(BF16)


def thrice(m):
    return jnp.concatenate([m, m, m], axis=1).astype(BF16)


def fold(tile):
    hi, lo = tile, jnp.zeros_like(tile)
    for axis, shifts in ((0, (4, 2, 1)), (1, (64, 32, 16, 8, 4, 2, 1))):
        for s in shifts:
            hi, e = two_sum(hi, pltpu.roll(hi, s, axis))
            lo = (lo + pltpu.roll(lo, s, axis)) + e
    return hi[0:1, :], lo[0:1, :]


def chosen(odd, ref, flip):
    lower, upper = ref[0, 0:1, :].astype(F32), ref[0, 1:2, :].astype(F32)
    return jnp.where(odd != flip, lower, upper)


def selectors(odd, bp, bc, pipes):
    cap = bp.shape[2]
    counts = bc[0:1, :].astype(F32)
    count_a = jnp.where(odd, counts[:, 0:1], counts[:, 1:2])
    count_b = jnp.where(odd, counts[:, 1:2], counts[:, 0:1])
    slot = iota((cap, 1), 0).astype(F32)
    live_a = jnp.where(slot < count_a, 1.0, 0.0)
    live_b = jnp.where(slot < count_b, 1.0, 0.0)
    pipe = iota((cap, pipes), 1).astype(F32)
    sel_a = jnp.where(column(chosen(odd, bp, False), cap) == pipe, live_a, 0.0)
    sel_b = jnp.where(column(chosen(odd, bp, True), cap) == pipe, live_b, 0.0)
    return sel_a, sel_b


def is_odd():
    return lax.axis_index("core") == 1


def open_kernel(prior_in, *refs):
    count = 8
    ins, prior, copies = (prior_in, *refs[: count - 1]), refs[count - 1], refs[count - 1 : 2 * count - 1]
    msg, sems, pipe_of, count_of = refs[2 * count - 1 :]
    moves = [pltpu.make_async_copy(ins[1], pipe_of, sems.at[count]), pltpu.make_async_copy(ins[2], count_of, sems.at[count + 1])]
    piece = prior.shape[0] // 4
    for k in range(4):
        rows = pl.ds(k * piece, piece)
        moves.append(pltpu.make_async_copy(prior_in.at[rows, :], prior.at[rows, :], sems.at[count + 2 + k]))
    moves += [pltpu.make_async_copy(i, o, sems.at[k]) for k, (i, o) in enumerate(zip(ins, copies)) if k]
    for m in moves:
        m.start()
    for m in moves[:6]:
        m.wait()
    cap = pipe_of.shape[2]
    side = jnp.where(is_odd(), 0, 1)
    live = count_of[0, side]
    for k in range(cap):
        row = prior[pl.ds(pipe_of[0, side, k], 1), :]
        msg[k : k + 1, :] = jnp.where(k < live, -row, 0.0)
    msg[cap:, :] = jnp.where(iota((cap, prior.shape[1]), 0) < live, 1.0, 0.0)
    for m in moves[6:]:
        m.wait()


def lists_kernel(sent, prior, bp, bc, aj, head, tail, demand, s_a, s_at, inc, l_a, l_b, it_sb, out_b, out_a, mid_b, mid_a, own, gain, part, base):
    cap = bp.shape[2]
    pipes = prior.shape[0]
    juncs = inc.shape[0]
    odd = is_odd()
    sel_a, sel_b = selectors(odd, bp, bc, pipes)
    inner = 1.0 - jnp.sum(sel_a + sel_b, axis=0, keepdims=True)
    junction = iota((juncs, pipes), 0)
    heads = jnp.where(junction == head[...], inner, 0.0)
    tails = jnp.where(junction == tail[...], 1.0, 0.0)
    both = heads - tails
    land = iota((juncs, cap), 0).astype(F32)
    to_a, to_b = chosen(odd, aj, False), chosen(odd, aj, True)
    land_a = jnp.where(land == to_a, 1.0, 0.0)
    land_b = jnp.where(land == to_b, 1.0, 0.0)
    row = iota((cap, juncs), 1).astype(F32)
    land_at = jnp.where(row == column(to_a, cap), 1.0, 0.0)
    land_bt = jnp.where(row == column(to_b, cap), 1.0, 0.0)
    square = jnp.transpose(jnp.concatenate([both, jnp.zeros((pipes - juncs, pipes), F32)], axis=0))
    both_t = square[:, :juncs]
    pad = jnp.zeros((128 - 2 * cap, 128), F32)
    turned = jnp.transpose(jnp.concatenate([sel_a, sel_b, pad], axis=0))
    sel_at, sel_bt = turned[:, :cap], turned[:, cap : 2 * cap]
    both16, a16, b16 = both.astype(BF16), land_a.astype(BF16), land_b.astype(BF16)
    bt16 = land_bt.astype(BF16)
    s_a[...] = sel_a.astype(BF16)
    s_at[...] = sel_at.astype(BF16)
    inc[...] = both16
    l_a[...] = a16
    l_b[...] = b16
    it_sb[...] = jnp.concatenate([both_t, sel_bt], axis=1).astype(BF16)
    b_inc = mm(bt16, both16)
    a_inc = mm(sel_a.astype(BF16), both_t.astype(BF16))
    out_b[...] = jnp.concatenate([sel_b, b_inc], axis=0).astype(BF16)
    out_a[...] = jnp.concatenate([land_at, a_inc], axis=0).astype(BF16)
    mid_b[...] = thrice(jnp.concatenate([mm(b_inc.astype(BF16), sel_at.astype(BF16)), mm(bt16, a16)], axis=1))
    mid_a[...] = thrice(jnp.concatenate([mm(land_at.astype(BF16), b16), mm(a_inc.astype(BF16), b16)], axis=0))
    own[...] = mm(bt16, b16)
    gain[...] = jnp.full(gain.shape, PENALTY, F32)
    x = prior[...]
    p = demand[...] - pick(both16, x)
    part[...] = p
    base[0:cap, :] = -pick(sel_b.astype(BF16), x)
    base[cap:, :] = pick(bt16, p)


def across_first(got, base, mid_b, own, msg, arrived, live):
    cap = own.shape[0]
    hours = base.shape[1]
    arr = got[0:cap, :]
    arrived[...] = arr
    live[...] = got[cap:, 0:128]
    msg[0:cap, 0:hours] = base[0:cap, :]
    both = jnp.concatenate([jnp.zeros_like(arr), arr], axis=0)
    msg[cap:, 0:hours] = base[cap:, :] + mm(mid_b[...], stack3(both))
    msg[:, hours:] = jnp.zeros((2 * cap, msg.shape[1] - hours), F32)
    msg[0:cap, hours : hours + cap] = own[...]


def wide(tile, v):
    return jnp.concatenate([tile] * (v.shape[1] // 128), axis=1)


def across_next(gain, sent, got, live, base, mid_b, msg, arrived):
    cap = live.shape[0]
    g = gain[...]
    added = wide(g, sent) * got[0:cap, :]
    arr = got[cap:, :] + wide(g * live[...], sent) * sent[0:cap, :]
    arrived[...] = arr
    msg[0:cap, :] = base[0:cap, :]
    msg[cap:, :] = base[cap:, :] + mm(mid_b[...], stack3(jnp.concatenate([added, arr], axis=0)))


def whole_kernel(gain, w, got, s_at, r_out):
    cap = s_at.shape[1]
    r_out[...] = w[...] + gain[0:1, 0:1] * pick(s_at[...], got[0:cap, :])


def back_kernel(gain, got, base, mid_a, msg):
    cap, hours = msg.shape[0] // 2, msg.shape[1]
    x = mm(mid_a[...], stack3(got[0:cap, 0:hours]))
    msg[0:cap, :] = base[0:cap, :] + x[0:cap]
    msg[cap:, :] = base[cap:, :] + wide(gain[...], msg) * x[cap:]


def outward(gain, part, near, s_a, out_a, base):
    cap = s_a.shape[0]
    x = pick(out_a[...], part)
    base[0:cap, :] = x[0:cap]
    base[cap:, :] = gain * x[cap:] + pick(s_a[...], near)


def inside_first(
    sent, coef, sigma, measured, prior, part_in, arrived, l_a, s_a, out_a,
    t0h, t0l, t1h, t1l, u0h, u0l, u1h, u1l, weight, near, rvar, gain, part, base,
):
    length = coef.shape[1]
    half = length // 2
    c = coef[...]
    shifted = pltpu.roll(jnp.broadcast_to(c, (half, length)), 0, 1, stride=1, stride_axis=0)
    upper = iota((half, half), 1) >= iota((half, half), 0)
    t0 = jnp.where(upper, shifted[:, :half], 0.0)
    t1 = shifted[:, half:]
    for hi, lo, x in ((t0h, t0l, t0), (t1h, t1l, t1), (u0h, u0l, t0.T), (u1h, u1l, t1.T)):
        a, b = halves(x)
        hi[...] = a
        lo[...] = b
    size = jnp.sum(jnp.abs(c), axis=1, keepdims=True)
    scale = 1.0 / (4.0 * size * size + 64.0)
    gain[...] = jnp.broadcast_to(PENALTY * scale, gain.shape)
    sig = jnp.transpose(jnp.broadcast_to(sigma[...], (128, 128)))[:, 0:1]
    rsig = 1.0 / sig
    whitened = forward((measured[...] - prior[...]) * rsig, (t0h, t0l, t1h, t1l))
    h = EDGE / jnp.maximum(jnp.abs(whitened), EDGE)
    weight[...] = h
    n = backward(h * whitened, (u0h, u0l, u1h, u1l)) * rsig
    near[...] = n
    rvar[...] = jnp.broadcast_to(rsig * rsig * scale, rvar.shape)
    p = part_in[...] + pick(l_a[...], arrived[...])
    part[...] = p
    outward(PENALTY, p, n, s_a, out_a, base)


def inside(gain0, gain, sent, w, got, arrived, weight, rvar, s_a, s_at, inc, l_a, out_a, taps, r_out, part, near, base):
    cap = s_a.shape[0]
    r = w[...] + gain0[0:1, 0:1] * pick(s_at[...], got[0:cap, :])
    r_out[...] = r
    p = pick(inc[...], r) + pick(l_a[...], arrived[...])
    part[...] = p
    n = backward(weight[...] * forward(r, taps[:4]), taps[4:]) * rvar[:, 0:1]
    near[...] = n
    outward(gain[0:1, 0:1], p, n, s_a, out_a, base)
    return r, p, n


def inside_one(*refs):
    *refs, sums = refs
    r, _, _ = inside(*refs[:13], refs[13:21], *refs[21:])
    sums[...] = lanes_sum(r * r)


def inside_two(before, *refs):
    *refs, sums = refs
    r, _, _ = inside(*refs[:13], refs[13:21], *refs[21:])
    sums[0:8, :] = lanes_sum(before[...] * r)
    sums[8:16, :] = lanes_sum(r * r)


def inside_three(before, sum0, sum1, *refs):
    *refs, row = refs
    gain = refs[1]
    r, p, n = inside(*refs[:13], refs[13:21], *refs[21:])
    tiles = (
        sum0[0:8, :], sum1[0:8, :], sum1[8:16, :], lanes_sum(before[...] * r), lanes_sum(r * r),
        lanes_sum(r * n) + gain[0:1, 0:1] * lanes_sum(p * p),
    )
    lane = iota((1, 128), 1)
    out = jnp.zeros((1, 128), F32)
    for k, tile in enumerate(tiles):
        hi, lo = fold(tile)
        out = jnp.where(lane == 2 * k, hi, jnp.where(lane == 2 * k + 1, lo, out))
    row[...] = jnp.broadcast_to(out, row.shape)


def close_kernel(gain, sent, got, own, row, rows):
    cap = own.shape[0]
    f = got[0:cap, :]
    extra = f * (2.0 * sent[cap : 2 * cap, :] + pick(own[...].astype(BF16), f))
    x = gain[0:1, 0:1] * jnp.sum(lanes_sum(extra), axis=0, keepdims=True)
    x = x + pltpu.roll(x, 64, 1)
    out = jnp.where(iota((1, 128), 1) < 64, row[0:1, :], x)
    rows[...] = jnp.broadcast_to(out, rows.shape)


def join(gain, sent_back, got, sent, far, part, near, l_b, it_sb, w_out):
    cap, hours = far.shape[0], part.shape[1]
    y = part[...] + pick(l_b[...], got[0:cap, 0:hours])
    y_far = got[cap:, 0:hours] + pick(far[...].astype(BF16), sent[0:cap, 0:hours])
    w = near[...] + gain[0:1, 0:1] * pick(it_sb[...], jnp.concatenate([y, y_far], axis=0))
    w_out[...] = w
    return w


def join_first(gain, sent_back, got, sent, part, near, l_b, it_sb, out_b, w_out, base, far):
    cap = far.shape[0]
    hours = part.shape[1]
    far[...] = got[0:cap, hours : hours + cap]
    w = join(gain, sent_back, got, sent, far, part, near, l_b, it_sb, w_out)
    base[...] = pick(out_b[...], w)


def join_next(gain, sent_back, got, sent, far, part, near, l_b, it_sb, out_b, w_out, base):
    w = join(gain, sent_back, got, sent, far, part, near, l_b, it_sb, w_out)
    base[...] = pick(out_b[...], w)


def two_sum(a, b):
    s = a + b
    t = s - a
    return s, (a - (s - t)) + (b - t)


def finish_kernel(rows, gain, prior, r0, r1, r2, r3, flows, residual, x_s, e_s, sems):
    n = rows.shape[0]
    tots = [(rows[i : i + 8, :], None) for i in range(0, n, 8)]
    while len(tots) > 1:
        pairs = []
        for (a, ae), (b, be) in zip(tots[::2], tots[1::2]):
            t, e = two_sum(a, b)
            pairs.append((t, e if ae is None else (ae + be) + e))
        tots = pairs
    hi, lo = tots[0]
    for sh in (4, 2, 1):
        hi, e = two_sum(hi, pltpu.roll(hi, sh, 0))
        lo = (lo + pltpu.roll(lo, sh, 0)) + e
    at = iota((8, 128), 1)
    cut = jnp.sum(jnp.where(at >= 64, hi + lo, 0.0), axis=1, keepdims=True)
    low = lo + (pltpu.roll(hi, 127, 1) + pltpu.roll(lo, 127, 1))
    hi, e = two_sum(hi, jnp.where(at == 10, cut, 0.0))
    hi, lo = two_sum(hi, low + e)

    def lane(v, k):
        return jnp.broadcast_to(v[:, k : k + 1], (8, 128))

    m = [(lane(hi, 2 * k), lane(lo, 2 * k)) for k in range(6)]
    s = (m[1][0] / m[0][0]).astype(BF16).astype(F32)
    mu = [m[0][0]]
    for _ in range(5):
        level = []
        for (h0, l0), (h1, l1) in zip(m[:-1], m[1:]):
            top = h0.astype(BF16).astype(F32)
            a, e = two_sum(h1, -(s * top))
            b, e2 = two_sum(a, -(s * (h0 - top)))
            level.append((b, (e + e2) + (l1 - s * l0)))
        m = level
        mu.append(m[0][0] + m[0][1])
    nu = [mu[k + 1] + s * mu[k] for k in range(5)]

    def form(u, v, m):
        total = None
        for i, a in enumerate(u):
            for j, b in enumerate(v):
                term = a * b * m[i + j]
                total = term if total is None else total + term
        return total

    def image(d):
        out = [s * x for x in d] + [jnp.zeros_like(s)]
        return [out[k] + (d[k - 1] if k else 0.0) for k in range(len(out))]

    a0 = mu[0] / nu[0]
    res1 = [mu[1] / nu[0], -a0]
    rr1 = form(res1, res1, mu)
    b0 = rr1 / mu[0]
    d1 = [res1[0] + b0, res1[1]]
    a1 = rr1 / form(d1, d1, nu)
    im1 = image(d1)
    res2 = [res1[0] - a1 * im1[0], res1[1] - a1 * im1[1], -a1 * im1[2]]
    rr2 = form(res2, res2, mu)
    b1 = rr2 / rr1
    d2 = [res2[0] + b1 * d1[0], res2[1] + b1 * d1[1], res2[2]]
    a2 = rr2 / form(d2, d2, nu)
    im2 = image(d2)
    f = [a0 + a1 * d1[0] + a2 * d2[0], a1 * d1[1] + a2 * d2[1], a2 * d2[2]]
    e = [res2[0] - a2 * im2[0], res2[1] - a2 * im2[1], res2[2] - a2 * im2[2], -a2 * im2[3]]
    ss = s * s
    f = [f[0] - s * f[1] + ss * f[2], f[1] - 2.0 * s * f[2], f[2]]
    e = [
        ((e[0] - s * e[1]) + ss * e[2]) - ss * s * e[3],
        (e[1] - 2.0 * s * e[2]) + 3.0 * ss * e[3],
        e[2] - 3.0 * s * e[3],
        e[3],
    ]
    g = jnp.broadcast_to(gain[0:1, 0:1], (8, 128)) * (1.0 / PENALTY)
    f = [x[0:1, 0:1] * g[0:1, 0:1] for x in f]
    e = [x[0:1, 0:1] for x in e]
    moves = []
    step = prior.shape[0] // 4
    for i in range(4):
        at = slice(i * step, (i + 1) * step)
        x0, x1, x2 = r0[at, :], r1[at, :], r2[at, :]
        x_s[at, :] = prior[at, :] + ((f[0] * x0 + f[1] * x1) + f[2] * x2)
        e_s[at, :] = ((e[0] * x0 + e[1] * x1) + e[2] * x2) + e[3] * r3[at, :]
        for k, (src, dst) in enumerate(((x_s, flows), (e_s, residual))):
            moves.append(pltpu.make_async_copy(src.at[pl.ds(i * step, step), :], dst.at[pl.ds(i * step, step), :], sems.at[2 * i + k]))
            moves[-1].start()
    for m in moves:
        m.wait()


def call(kernel, outs, *args):
    return pl.pallas_call(
        kernel,
        out_shape=tuple(pltpu.VMEM(s, d) for s, d in outs),
        in_specs=[pl.BlockSpec(memory_space=pltpu.VMEM)] * len(args),
        out_specs=tuple(pl.BlockSpec(memory_space=pltpu.VMEM) for _ in outs),
        compiler_params=pltpu.CompilerParams(vmem_limit_bytes=16 * 2**20),
    )(*(pltpu.with_memory_space_constraint(x, pltpu.VMEM) for x in args))


def bring(args, msg):
    lists = (args[1], args[2])
    return pl.pallas_call(
        open_kernel,
        out_shape=tuple(pltpu.VMEM(x.shape, x.dtype) for x in args) + (pltpu.VMEM(*msg),),
        in_specs=[pl.BlockSpec(memory_space=pltpu.HBM)] * len(args),
        out_specs=tuple(pl.BlockSpec(memory_space=pltpu.VMEM) for _ in range(len(args) + 1)),
        scratch_shapes=[pltpu.SemaphoreType.DMA((len(args) + 6,))] + [pltpu.SMEM(x.shape, x.dtype) for x in lists],
        compiler_params=pltpu.CompilerParams(vmem_limit_bytes=16 * 2**20),
    )(*(pltpu.with_memory_space_constraint(x, pltpu.HBM) for x in args))


def finish(rows, *args):
    field = args[1]
    args = (rows, *args)
    return pl.pallas_call(
        finish_kernel,
        out_shape=(jax.ShapeDtypeStruct(field.shape, F32),) * 2,
        in_specs=[pl.BlockSpec(memory_space=pltpu.VMEM)] * len(args),
        out_specs=(pl.BlockSpec(memory_space=pltpu.HBM),) * 2,
        scratch_shapes=[pltpu.VMEM(field.shape, F32)] * 2 + [pltpu.SemaphoreType.DMA((8,))],
        compiler_params=pltpu.CompilerParams(vmem_limit_bytes=16 * 2**20),
    )(*(pltpu.with_memory_space_constraint(x, pltpu.VMEM) for x in args))


def shards(
    measured,
    prior_flow,
    demand,
    pipe_sigma,
    whiten_coef,
    pipe_tail,
    pipe_head,
    boundary_pipe,
    boundary_count,
    arrival_junction,
):
    pipes, hours = prior_flow.shape
    juncs = demand.shape[0]
    cap = boundary_pipe.shape[2]
    nets = lax.axis_size(NET)
    hour_blocks = lax.axis_size("hour")
    devices = nets * hour_blocks
    field = ((pipes, hours), F32)
    heads = ((juncs, hours), F32)
    slots = ((cap, hours), F32)
    msg2 = ((2 * cap, hours), F32)
    wide = ((2 * cap, hours + 128), F32)
    tile = ((8, 128), F32)
    half = ((hours // 2, hours // 2), BF16)
    on_chip = [(i, i ^ 1) for i in range(nets)]
    across = []
    for h in range(hour_blocks):
        for i in range(1, nets - 1, 2):
            a, b = i * hour_blocks + h, (i + 1) * hour_blocks + h
            across += [(a, b), (b, a)]
        for i in (0, nets - 1):
            across.append((i * hour_blocks + h, i * hour_blocks + (h ^ 1)))

    def swap(x):
        return lax.ppermute(x, NET, on_chip)

    def cross(x):
        return lax.ppermute(x, (*NET, "hour"), across)

    args = (
        prior_flow, boundary_pipe, boundary_count, arrival_junction,
        pipe_head.reshape(1, pipes), pipe_tail.reshape(1, pipes), whiten_coef.reshape(1, hours), pipe_sigma.reshape(1, pipes),
    )
    prior, bp, bc, aj, head, tail, coef, sigma, back = bring(args, msg2)
    got = swap(back)
    s_a, s_at, inc, l_a, l_b, it_sb, out_b, out_a, mid_b, mid_a, own, gain0, part, base = call(
        lists_kernel,
        [
            ((cap, pipes), BF16), ((pipes, cap), BF16), ((juncs, pipes), BF16), ((juncs, cap), BF16),
            ((juncs, cap), BF16), ((pipes, juncs + cap), BF16), ((2 * cap, pipes), BF16), ((2 * cap, juncs), BF16),
            ((cap, 6 * cap), BF16), ((2 * cap, 3 * cap), BF16), ((cap, cap), F32), tile, heads, msg2,
        ],
        back, prior, bp, bc, aj, head, tail, demand,
    )
    sent, arrived, live = call(across_first, [wide, slots, tile], got, base, mid_b, own)
    got = cross(sent)
    out = call(
        inside_first,
        [half] * 8 + [field, field, ((pipes, 128), F32), tile, heads, msg2],
        sent, coef, sigma, measured, prior, part, arrived, l_a, s_a, out_a,
    )
    taps, (weight, near, rvar, gain, part, base) = out[:8], out[8:]
    (back,) = call(back_kernel, [msg2], gain0, got, base, mid_a)
    back_got = swap(back)
    w, base, far = call(
        join_first, [field, msg2, ((cap, cap), F32)], gain0, back, got, sent, part, near, l_b, it_sb, out_b
    )
    fields, sums = [], []
    for step in range(3):
        g = gain if step else gain0
        sent, arrived = call(across_next, [msg2, slots], g, back, back_got, live, base, mid_b)
        got = cross(sent)
        given = (g, gain, sent, w, back_got, arrived, weight, rvar, s_a, s_at, inc, l_a, out_a, *taps)
        gives = [field, heads, field, msg2]
        if step == 0:
            r, part, near, base, acc = call(inside_one, gives + [tile], *given)
        elif step == 1:
            r, part, near, base, acc = call(inside_two, gives + [((16, 128), F32)], fields[-1], *given)
        else:
            r, part, near, base, acc = call(inside_three, gives + [tile], fields[-1], *sums, *given)
        fields.append(r)
        sums.append(acc)
        if step == 2:
            (rows,) = call(close_kernel, [((devices, 128), F32)], gain, sent, got, own, acc)
            rows = lax.all_to_all(
                rows.reshape(devices, 1, 128), ("core", "z", "y", "hour"), 0, 0, tiled=True
            ).reshape(devices, 128)
        (back,) = call(back_kernel, [msg2], gain, got, base, mid_a)
        back_got = swap(back)
        w, base = call(join_next, [field, msg2], gain, back, got, sent, far, part, near, l_b, it_sb, out_b)
    (last,) = call(whole_kernel, [field], gain, w, back_got, s_at)
    return finish(rows, gain, prior, *fields, last)


def solution(mesh):
    nets, hours = mesh.devices.shape
    fine = Mesh(mesh.devices.reshape(nets // 8, 4, 2, hours), (*NET, "hour"))
    placed = (
        P(NET, "hour"),
        P(NET, "hour"),
        P(NET, "hour"),
        P(NET),
        P(),
        P(NET),
        P(NET),
        P(NET, None, None),
        P(NET, None),
        P(NET, None, None),
    )
    return jax.shard_map(
        shards,
        mesh=fine,
        in_specs=placed,
        out_specs=(P(NET, "hour"), P(NET, "hour")),
        check_vma=False,
    )
```

```python
import jax
import jax.numpy as jnp
from jax import lax
from jax.experimental import pallas as pl
from jax.experimental.pallas import tpu as pltpu
from jax.sharding import Mesh, PartitionSpec as P

NET = ("y", "z", "core")
EDGE = 1.5
PENALTY = 4.0
F32 = jnp.float32
BF16 = jnp.bfloat16


def iota(shape, dim):
    return lax.broadcasted_iota(jnp.int32, shape, dim)


def thirds(v):
    a = v.astype(BF16)
    rest = v - a.astype(F32)
    b = rest.astype(BF16)
    c = (rest - b.astype(F32)).astype(BF16)
    return a, b, c


def mm(a, b):
    return jnp.dot(a, b, preferred_element_type=F32)


def pick(exact, v):
    a, b, c = thirds(v)
    return (mm(exact, c) + mm(exact, b)) + mm(exact, a)


def product(x, taps):
    a, b, c = thirds(x)
    h, m, l = (t[...] for t in taps)
    return ((mm(c, h) + mm(a, l)) + mm(b, m)) + (mm(b, h) + mm(a, m)) + mm(a, h)


def forward(v, taps):
    rows = v.shape[0]
    half = v.shape[1] // 2
    near = product(jnp.concatenate([v[:, :half], v[:, half:]], axis=0), taps[:3])
    far = product(v[:, :half], taps[3:])
    return jnp.concatenate([near[:rows], near[rows:] + far], axis=1)


def backward(v, taps):
    rows = v.shape[0]
    half = v.shape[1] // 2
    near = product(jnp.concatenate([v[:, :half], v[:, half:]], axis=0), taps[:3])
    far = product(v[:, half:], taps[3:])
    return jnp.concatenate([near[:rows] + far, near[rows:]], axis=1)


def lanes_sum(v):
    rows, cols = v.shape
    total = None
    for i in range(0, rows, 8):
        for j in range(0, cols, 128):
            part = v[i : i + 8, j : j + 128]
            total = part if total is None else total + part
    return total


def column(row, n):
    return jnp.sum(jnp.where(iota((n, n), 0) == iota((n, n), 1), row, 0.0), axis=1, keepdims=True)


def stack3(v):
    a = v.astype(BF16).astype(F32)
    rest = v - a
    b = rest.astype(BF16).astype(F32)
    return jnp.concatenate([rest - b, b, a], axis=0).astype(BF16)


def thrice(m):
    return jnp.concatenate([m, m, m], axis=1).astype(BF16)


def fold(tile):
    hi, lo = tile, jnp.zeros_like(tile)
    for axis, shifts in ((0, (4, 2, 1)), (1, (64, 32, 16, 8, 4, 2, 1))):
        for s in shifts:
            hi, e = two_sum(hi, pltpu.roll(hi, s, axis))
            lo = (lo + pltpu.roll(lo, s, axis)) + e
    return hi[0:1, :], lo[0:1, :]


def chosen(odd, ref, flip):
    lower, upper = ref[0, 0:1, :].astype(F32), ref[0, 1:2, :].astype(F32)
    return jnp.where(odd != flip, lower, upper)


def selectors(odd, bp, bc, pipes):
    cap = bp.shape[2]
    counts = bc[0:1, :].astype(F32)
    count_a = jnp.where(odd, counts[:, 0:1], counts[:, 1:2])
    count_b = jnp.where(odd, counts[:, 1:2], counts[:, 0:1])
    slot = iota((cap, 1), 0).astype(F32)
    live_a = jnp.where(slot < count_a, 1.0, 0.0)
    live_b = jnp.where(slot < count_b, 1.0, 0.0)
    pipe = iota((cap, pipes), 1).astype(F32)
    sel_a = jnp.where(column(chosen(odd, bp, False), cap) == pipe, live_a, 0.0)
    sel_b = jnp.where(column(chosen(odd, bp, True), cap) == pipe, live_b, 0.0)
    return sel_a, sel_b


def is_odd():
    return lax.axis_index("core") == 1


def open_kernel(prior_in, *refs):
    count = 8
    ins, prior, copies = (prior_in, *refs[: count - 1]), refs[count - 1], refs[count - 1 : 2 * count - 1]
    msg, sems, pipe_of, count_of = refs[2 * count - 1 :]
    moves = [pltpu.make_async_copy(ins[1], pipe_of, sems.at[count]), pltpu.make_async_copy(ins[2], count_of, sems.at[count + 1])]
    piece = prior.shape[0] // 4
    for k in range(4):
        rows = pl.ds(k * piece, piece)
        moves.append(pltpu.make_async_copy(prior_in.at[rows, :], prior.at[rows, :], sems.at[count + 2 + k]))
    moves += [pltpu.make_async_copy(i, o, sems.at[k]) for k, (i, o) in enumerate(zip(ins, copies)) if k]
    for m in moves:
        m.start()
    for m in moves[:6]:
        m.wait()
    cap = pipe_of.shape[2]
    side = jnp.where(is_odd(), 0, 1)
    live = count_of[0, side]
    for k in range(cap):
        row = prior[pl.ds(pipe_of[0, side, k], 1), :]
        msg[k : k + 1, :] = jnp.where(k < live, -row, 0.0)
    msg[cap:, :] = jnp.where(iota((cap, prior.shape[1]), 0) < live, 1.0, 0.0)
    for m in moves[6:]:
        m.wait()


def lists_kernel(sent, prior, bp, bc, aj, head, tail, demand, s_a, s_at, inc, l_a, l_b, it_sb, out_b, out_a, mid_b, mid_a, own, gain, part, base):
    cap = bp.shape[2]
    pipes = prior.shape[0]
    juncs = inc.shape[0]
    odd = is_odd()
    sel_a, sel_b = selectors(odd, bp, bc, pipes)
    inner = 1.0 - jnp.sum(sel_a + sel_b, axis=0, keepdims=True)
    junction = iota((juncs, pipes), 0)
    heads = jnp.where(junction == head[...], inner, 0.0)
    tails = jnp.where(junction == tail[...], 1.0, 0.0)
    both = heads - tails
    land = iota((juncs, cap), 0).astype(F32)
    to_a, to_b = chosen(odd, aj, False), chosen(odd, aj, True)
    land_a = jnp.where(land == to_a, 1.0, 0.0)
    land_b = jnp.where(land == to_b, 1.0, 0.0)
    row = iota((cap, juncs), 1).astype(F32)
    land_at = jnp.where(row == column(to_a, cap), 1.0, 0.0)
    land_bt = jnp.where(row == column(to_b, cap), 1.0, 0.0)
    square = jnp.transpose(jnp.concatenate([both, jnp.zeros((pipes - juncs, pipes), F32)], axis=0))
    both_t = square[:, :juncs]
    pad = jnp.zeros((128 - 2 * cap, 128), F32)
    turned = jnp.transpose(jnp.concatenate([sel_a, sel_b, pad], axis=0))
    sel_at, sel_bt = turned[:, :cap], turned[:, cap : 2 * cap]
    both16, a16, b16 = both.astype(BF16), land_a.astype(BF16), land_b.astype(BF16)
    bt16 = land_bt.astype(BF16)
    s_a[...] = sel_a.astype(BF16)
    s_at[...] = sel_at.astype(BF16)
    inc[...] = both16
    l_a[...] = a16
    l_b[...] = b16
    it_sb[...] = jnp.concatenate([both_t, sel_bt], axis=1).astype(BF16)
    b_inc = mm(bt16, both16)
    a_inc = mm(sel_a.astype(BF16), both_t.astype(BF16))
    out_b[...] = jnp.concatenate([sel_b, b_inc], axis=0).astype(BF16)
    out_a[...] = jnp.concatenate([land_at, a_inc], axis=0).astype(BF16)
    mid_b[...] = thrice(jnp.concatenate([mm(b_inc.astype(BF16), sel_at.astype(BF16)), mm(bt16, a16)], axis=1))
    mid_a[...] = thrice(jnp.concatenate([mm(land_at.astype(BF16), b16), mm(a_inc.astype(BF16), b16)], axis=0))
    own[...] = mm(bt16, b16)
    gain[...] = jnp.full(gain.shape, PENALTY, F32)
    x = prior[...]
    p = demand[...] - pick(both16, x)
    part[...] = p
    base[0:cap, :] = -pick(sel_b.astype(BF16), x)
    base[cap:, :] = pick(bt16, p)


def across_first(got, base, mid_b, own, msg, arrived, live):
    cap = own.shape[0]
    hours = base.shape[1]
    arr = got[0:cap, :]
    arrived[...] = arr
    live[...] = got[cap:, 0:128]
    msg[0:cap, 0:hours] = base[0:cap, :]
    both = jnp.concatenate([jnp.zeros_like(arr), arr], axis=0)
    msg[cap:, 0:hours] = base[cap:, :] + mm(mid_b[...], stack3(both))
    msg[:, hours:] = jnp.zeros((2 * cap, msg.shape[1] - hours), F32)
    msg[0:cap, hours : hours + cap] = own[...]


def wide(tile, v):
    return jnp.concatenate([tile] * (v.shape[1] // 128), axis=1)


def across_next(gain, sent, got, live, base, mid_b, msg, arrived):
    cap = live.shape[0]
    g = gain[...]
    added = wide(g, sent) * got[0:cap, :]
    arr = got[cap:, :] + wide(g * live[...], sent) * sent[0:cap, :]
    arrived[...] = arr
    msg[0:cap, :] = base[0:cap, :]
    msg[cap:, :] = base[cap:, :] + mm(mid_b[...], stack3(jnp.concatenate([added, arr], axis=0)))


def whole_kernel(gain, w, got, s_at, r_out):
    cap = s_at.shape[1]
    r_out[...] = w[...] + gain[0:1, 0:1] * pick(s_at[...], got[0:cap, :])


def back_kernel(gain, got, base, mid_a, msg):
    cap, hours = msg.shape[0] // 2, msg.shape[1]
    x = mm(mid_a[...], stack3(got[0:cap, 0:hours]))
    msg[0:cap, :] = base[0:cap, :] + x[0:cap]
    msg[cap:, :] = base[cap:, :] + wide(gain[...], msg) * x[cap:]


def outward(gain, part, near, s_a, out_a, base):
    cap = s_a.shape[0]
    x = pick(out_a[...], part)
    base[0:cap, :] = x[0:cap]
    base[cap:, :] = gain * x[cap:] + pick(s_a[...], near)


def inside_first(
    sent, coef, sigma, measured, prior, part_in, arrived, l_a, s_a, out_a, *outs,
):
    taps, (weight, near, rvar, gain, part, base) = outs[:12], outs[12:]
    length = coef.shape[1]
    half = length // 2
    c = coef[...]
    shifted = pltpu.roll(jnp.broadcast_to(c, (half, length)), 0, 1, stride=1, stride_axis=0)
    upper = iota((half, half), 1) >= iota((half, half), 0)
    t0 = jnp.where(upper, shifted[:, :half], 0.0)
    t1 = shifted[:, half:]
    for k, x in enumerate((t0, t1, t0.T, t1.T)):
        for ref, term in zip(taps[3 * k : 3 * k + 3], thirds(x)):
            ref[...] = term
    size = jnp.sum(jnp.abs(c), axis=1, keepdims=True)
    scale = 1.0 / (4.0 * size * size + 64.0)
    gain[...] = jnp.broadcast_to(PENALTY * scale, gain.shape)
    sig = jnp.transpose(jnp.broadcast_to(sigma[...], (128, 128)))[:, 0:1]
    rsig = 1.0 / sig
    whitened = forward((measured[...] - prior[...]) * rsig, taps[:6])
    h = EDGE / jnp.maximum(jnp.abs(whitened), EDGE)
    weight[...] = h
    n = backward(h * whitened, taps[6:]) * rsig
    near[...] = n
    rvar[...] = jnp.broadcast_to(rsig * rsig * scale, rvar.shape)
    p = part_in[...] + pick(l_a[...], arrived[...])
    part[...] = p
    outward(PENALTY, p, n, s_a, out_a, base)


def inside(gain0, gain, sent, w, got, arrived, weight, rvar, s_a, s_at, inc, l_a, out_a, taps, r_out, part, near, base):
    cap = s_a.shape[0]
    r = w[...] + gain0[0:1, 0:1] * pick(s_at[...], got[0:cap, :])
    r_out[...] = r
    p = pick(inc[...], r) + pick(l_a[...], arrived[...])
    part[...] = p
    n = backward(weight[...] * forward(r, taps[:6]), taps[6:]) * rvar[:, 0:1]
    near[...] = n
    outward(gain[0:1, 0:1], p, n, s_a, out_a, base)
    return r, p, n


def inside_one(*refs):
    *refs, sums = refs
    r, _, _ = inside(*refs[:13], refs[13:25], *refs[25:])
    sums[...] = lanes_sum(r * r)


def inside_two(before, *refs):
    *refs, sums = refs
    r, _, _ = inside(*refs[:13], refs[13:25], *refs[25:])
    sums[0:8, :] = lanes_sum(before[...] * r)
    sums[8:16, :] = lanes_sum(r * r)


def inside_three(before, sum0, sum1, *refs):
    *refs, row = refs
    gain = refs[1]
    r, p, n = inside(*refs[:13], refs[13:25], *refs[25:])
    tiles = (
        sum0[0:8, :], sum1[0:8, :], sum1[8:16, :], lanes_sum(before[...] * r), lanes_sum(r * r),
        lanes_sum(r * n) + gain[0:1, 0:1] * lanes_sum(p * p),
    )
    lane = iota((1, 128), 1)
    out = jnp.zeros((1, 128), F32)
    for k, tile in enumerate(tiles):
        hi, lo = fold(tile)
        out = jnp.where(lane == 2 * k, hi, jnp.where(lane == 2 * k + 1, lo, out))
    row[...] = jnp.broadcast_to(out, row.shape)


def close_kernel(gain, sent, got, own, row, rows):
    cap = own.shape[0]
    f = got[0:cap, :]
    extra = f * (2.0 * sent[cap : 2 * cap, :] + pick(own[...].astype(BF16), f))
    x = gain[0:1, 0:1] * jnp.sum(lanes_sum(extra), axis=0, keepdims=True)
    x = x + pltpu.roll(x, 64, 1)
    out = jnp.where(iota((1, 128), 1) < 64, row[0:1, :], x)
    rows[...] = jnp.broadcast_to(out, rows.shape)


def join(gain, sent_back, got, sent, far, part, near, l_b, it_sb, w_out):
    cap, hours = far.shape[0], part.shape[1]
    y = part[...] + pick(l_b[...], got[0:cap, 0:hours])
    y_far = got[cap:, 0:hours] + pick(far[...].astype(BF16), sent[0:cap, 0:hours])
    w = near[...] + gain[0:1, 0:1] * pick(it_sb[...], jnp.concatenate([y, y_far], axis=0))
    w_out[...] = w
    return w


def join_first(gain, sent_back, got, sent, part, near, l_b, it_sb, out_b, w_out, base, far):
    cap = far.shape[0]
    hours = part.shape[1]
    far[...] = got[0:cap, hours : hours + cap]
    w = join(gain, sent_back, got, sent, far, part, near, l_b, it_sb, w_out)
    base[...] = pick(out_b[...], w)


def join_next(gain, sent_back, got, sent, far, part, near, l_b, it_sb, out_b, w_out, base):
    w = join(gain, sent_back, got, sent, far, part, near, l_b, it_sb, w_out)
    base[...] = pick(out_b[...], w)


def two_sum(a, b):
    s = a + b
    t = s - a
    return s, (a - (s - t)) + (b - t)


def finish_kernel(rows, gain, prior, r0, r1, r2, r3, flows, residual, x_s, e_s, sems):
    n = rows.shape[0]
    tots = [(rows[i : i + 8, :], None) for i in range(0, n, 8)]
    while len(tots) > 1:
        pairs = []
        for (a, ae), (b, be) in zip(tots[::2], tots[1::2]):
            t, e = two_sum(a, b)
            pairs.append((t, e if ae is None else (ae + be) + e))
        tots = pairs
    hi, lo = tots[0]
    for sh in (4, 2, 1):
        hi, e = two_sum(hi, pltpu.roll(hi, sh, 0))
        lo = (lo + pltpu.roll(lo, sh, 0)) + e
    at = iota((8, 128), 1)
    cut = jnp.sum(jnp.where(at >= 64, hi + lo, 0.0), axis=1, keepdims=True)
    low = lo + (pltpu.roll(hi, 127, 1) + pltpu.roll(lo, 127, 1))
    hi, e = two_sum(hi, jnp.where(at == 10, cut, 0.0))
    hi, lo = two_sum(hi, low + e)

    def lane(v, k):
        return jnp.broadcast_to(v[:, k : k + 1], (8, 128))

    m = [(lane(hi, 2 * k), lane(lo, 2 * k)) for k in range(6)]
    s = (m[1][0] / m[0][0]).astype(BF16).astype(F32)
    mu = [m[0][0]]
    for _ in range(5):
        level = []
        for (h0, l0), (h1, l1) in zip(m[:-1], m[1:]):
            top = h0.astype(BF16).astype(F32)
            a, e = two_sum(h1, -(s * top))
            b, e2 = two_sum(a, -(s * (h0 - top)))
            level.append((b, (e + e2) + (l1 - s * l0)))
        m = level
        mu.append(m[0][0] + m[0][1])
    nu = [mu[k + 1] + s * mu[k] for k in range(5)]

    def form(u, v, m):
        total = None
        for i, a in enumerate(u):
            for j, b in enumerate(v):
                term = a * b * m[i + j]
                total = term if total is None else total + term
        return total

    def image(d):
        out = [s * x for x in d] + [jnp.zeros_like(s)]
        return [out[k] + (d[k - 1] if k else 0.0) for k in range(len(out))]

    a0 = mu[0] / nu[0]
    res1 = [mu[1] / nu[0], -a0]
    rr1 = form(res1, res1, mu)
    b0 = rr1 / mu[0]
    d1 = [res1[0] + b0, res1[1]]
    a1 = rr1 / form(d1, d1, nu)
    im1 = image(d1)
    res2 = [res1[0] - a1 * im1[0], res1[1] - a1 * im1[1], -a1 * im1[2]]
    rr2 = form(res2, res2, mu)
    b1 = rr2 / rr1
    d2 = [res2[0] + b1 * d1[0], res2[1] + b1 * d1[1], res2[2]]
    a2 = rr2 / form(d2, d2, nu)
    im2 = image(d2)
    f = [a0 + a1 * d1[0] + a2 * d2[0], a1 * d1[1] + a2 * d2[1], a2 * d2[2]]
    e = [res2[0] - a2 * im2[0], res2[1] - a2 * im2[1], res2[2] - a2 * im2[2], -a2 * im2[3]]
    ss = s * s
    f = [f[0] - s * f[1] + ss * f[2], f[1] - 2.0 * s * f[2], f[2]]
    e = [
        ((e[0] - s * e[1]) + ss * e[2]) - ss * s * e[3],
        (e[1] - 2.0 * s * e[2]) + 3.0 * ss * e[3],
        e[2] - 3.0 * s * e[3],
        e[3],
    ]
    g = jnp.broadcast_to(gain[0:1, 0:1], (8, 128)) * (1.0 / PENALTY)
    f = [x[0:1, 0:1] * g[0:1, 0:1] for x in f]
    e = [x[0:1, 0:1] for x in e]
    moves = []
    step = prior.shape[0] // 4
    for i in range(4):
        at = slice(i * step, (i + 1) * step)
        x0, x1, x2 = r0[at, :], r1[at, :], r2[at, :]
        x_s[at, :] = prior[at, :] + ((f[0] * x0 + f[1] * x1) + f[2] * x2)
        e_s[at, :] = ((e[0] * x0 + e[1] * x1) + e[2] * x2) + e[3] * r3[at, :]
        for k, (src, dst) in enumerate(((x_s, flows), (e_s, residual))):
            moves.append(pltpu.make_async_copy(src.at[pl.ds(i * step, step), :], dst.at[pl.ds(i * step, step), :], sems.at[2 * i + k]))
            moves[-1].start()
    for m in moves:
        m.wait()


def call(kernel, outs, *args):
    return pl.pallas_call(
        kernel,
        out_shape=tuple(pltpu.VMEM(s, d) for s, d in outs),
        in_specs=[pl.BlockSpec(memory_space=pltpu.VMEM)] * len(args),
        out_specs=tuple(pl.BlockSpec(memory_space=pltpu.VMEM) for _ in outs),
        compiler_params=pltpu.CompilerParams(vmem_limit_bytes=16 * 2**20),
    )(*(pltpu.with_memory_space_constraint(x, pltpu.VMEM) for x in args))


def bring(args, msg):
    lists = (args[1], args[2])
    return pl.pallas_call(
        open_kernel,
        out_shape=tuple(pltpu.VMEM(x.shape, x.dtype) for x in args) + (pltpu.VMEM(*msg),),
        in_specs=[pl.BlockSpec(memory_space=pltpu.HBM)] * len(args),
        out_specs=tuple(pl.BlockSpec(memory_space=pltpu.VMEM) for _ in range(len(args) + 1)),
        scratch_shapes=[pltpu.SemaphoreType.DMA((len(args) + 6,))] + [pltpu.SMEM(x.shape, x.dtype) for x in lists],
        compiler_params=pltpu.CompilerParams(vmem_limit_bytes=16 * 2**20),
    )(*(pltpu.with_memory_space_constraint(x, pltpu.HBM) for x in args))


def finish(rows, *args):
    field = args[1]
    args = (rows, *args)
    return pl.pallas_call(
        finish_kernel,
        out_shape=(jax.ShapeDtypeStruct(field.shape, F32),) * 2,
        in_specs=[pl.BlockSpec(memory_space=pltpu.VMEM)] * len(args),
        out_specs=(pl.BlockSpec(memory_space=pltpu.HBM),) * 2,
        scratch_shapes=[pltpu.VMEM(field.shape, F32)] * 2 + [pltpu.SemaphoreType.DMA((8,))],
        compiler_params=pltpu.CompilerParams(vmem_limit_bytes=16 * 2**20),
    )(*(pltpu.with_memory_space_constraint(x, pltpu.VMEM) for x in args))


def shards(
    measured,
    prior_flow,
    demand,
    pipe_sigma,
    whiten_coef,
    pipe_tail,
    pipe_head,
    boundary_pipe,
    boundary_count,
    arrival_junction,
):
    pipes, hours = prior_flow.shape
    juncs = demand.shape[0]
    cap = boundary_pipe.shape[2]
    nets = lax.axis_size(NET)
    hour_blocks = lax.axis_size("hour")
    devices = nets * hour_blocks
    field = ((pipes, hours), F32)
    heads = ((juncs, hours), F32)
    slots = ((cap, hours), F32)
    msg2 = ((2 * cap, hours), F32)
    wide = ((2 * cap, hours + 128), F32)
    tile = ((8, 128), F32)
    half = ((hours // 2, hours // 2), BF16)
    on_chip = [(i, i ^ 1) for i in range(nets)]
    across = []
    for h in range(hour_blocks):
        for i in range(1, nets - 1, 2):
            a, b = i * hour_blocks + h, (i + 1) * hour_blocks + h
            across += [(a, b), (b, a)]
        for i in (0, nets - 1):
            across.append((i * hour_blocks + h, i * hour_blocks + (h ^ 1)))

    def swap(x):
        return lax.ppermute(x, NET, on_chip)

    def cross(x):
        return lax.ppermute(x, (*NET, "hour"), across)

    args = (
        prior_flow, boundary_pipe, boundary_count, arrival_junction,
        pipe_head.reshape(1, pipes), pipe_tail.reshape(1, pipes), whiten_coef.reshape(1, hours), pipe_sigma.reshape(1, pipes),
    )
    prior, bp, bc, aj, head, tail, coef, sigma, back = bring(args, msg2)
    got = swap(back)
    s_a, s_at, inc, l_a, l_b, it_sb, out_b, out_a, mid_b, mid_a, own, gain0, part, base = call(
        lists_kernel,
        [
            ((cap, pipes), BF16), ((pipes, cap), BF16), ((juncs, pipes), BF16), ((juncs, cap), BF16),
            ((juncs, cap), BF16), ((pipes, juncs + cap), BF16), ((2 * cap, pipes), BF16), ((2 * cap, juncs), BF16),
            ((cap, 6 * cap), BF16), ((2 * cap, 3 * cap), BF16), ((cap, cap), F32), tile, heads, msg2,
        ],
        back, prior, bp, bc, aj, head, tail, demand,
    )
    sent, arrived, live = call(across_first, [wide, slots, tile], got, base, mid_b, own)
    got = cross(sent)
    out = call(
        inside_first,
        [half] * 12 + [field, field, ((pipes, 128), F32), tile, heads, msg2],
        sent, coef, sigma, measured, prior, part, arrived, l_a, s_a, out_a,
    )
    taps, (weight, near, rvar, gain, part, base) = out[:12], out[12:]
    (back,) = call(back_kernel, [msg2], gain0, got, base, mid_a)
    back_got = swap(back)
    w, base, far = call(
        join_first, [field, msg2, ((cap, cap), F32)], gain0, back, got, sent, part, near, l_b, it_sb, out_b
    )
    fields, sums = [], []
    for step in range(3):
        g = gain if step else gain0
        sent, arrived = call(across_next, [msg2, slots], g, back, back_got, live, base, mid_b)
        got = cross(sent)
        given = (g, gain, sent, w, back_got, arrived, weight, rvar, s_a, s_at, inc, l_a, out_a, *taps)
        gives = [field, heads, field, msg2]
        if step == 0:
            r, part, near, base, acc = call(inside_one, gives + [tile], *given)
        elif step == 1:
            r, part, near, base, acc = call(inside_two, gives + [((16, 128), F32)], fields[-1], *given)
        else:
            r, part, near, base, acc = call(inside_three, gives + [tile], fields[-1], *sums, *given)
        fields.append(r)
        sums.append(acc)
        if step == 2:
            (rows,) = call(close_kernel, [((devices, 128), F32)], gain, sent, got, own, acc)
            rows = lax.all_to_all(
                rows.reshape(devices, 1, 128), ("core", "z", "y", "hour"), 0, 0, tiled=True
            ).reshape(devices, 128)
        (back,) = call(back_kernel, [msg2], gain, got, base, mid_a)
        back_got = swap(back)
        w, base = call(join_next, [field, msg2], gain, back, got, sent, far, part, near, l_b, it_sb, out_b)
    (last,) = call(whole_kernel, [field], gain, w, back_got, s_at)
    return finish(rows, gain, prior, *fields, last)


def solution(mesh):
    nets, hours = mesh.devices.shape
    fine = Mesh(mesh.devices.reshape(nets // 8, 4, 2, hours), (*NET, "hour"))
    placed = (
        P(NET, "hour"),
        P(NET, "hour"),
        P(NET, "hour"),
        P(NET),
        P(),
        P(NET),
        P(NET),
        P(NET, None, None),
        P(NET, None),
        P(NET, None, None),
    )
    return jax.shard_map(
        shards,
        mesh=fine,
        in_specs=placed,
        out_specs=(P(NET, "hour"), P(NET, "hour")),
        check_vma=False,
    )
```

```python
import jax
import jax.numpy as jnp
from jax import lax
from jax.experimental import pallas as pl
from jax.experimental.pallas import tpu as pltpu
from jax.sharding import Mesh, PartitionSpec as P

NET = ("y", "z", "core")
EDGE = 1.5
PENALTY = 4.0
F32 = jnp.float32
BF16 = jnp.bfloat16


def iota(shape, dim):
    return lax.broadcasted_iota(jnp.int32, shape, dim)


def thirds(v):
    a = v.astype(BF16)
    rest = v - a.astype(F32)
    b = rest.astype(BF16)
    c = (rest - b.astype(F32)).astype(BF16)
    return a, b, c


def mm(a, b):
    return jnp.dot(a, b, preferred_element_type=F32)


def pick(exact, v):
    a, b, c = thirds(v)
    return (mm(exact, c) + mm(exact, b)) + mm(exact, a)


def product(x, taps):
    a, b, c = thirds(x)
    h, m, l = (t[...] for t in taps)
    return ((mm(c, h) + mm(a, l)) + mm(b, m)) + (mm(b, h) + mm(a, m)) + mm(a, h)


def forward(v, taps):
    rows = v.shape[0]
    half = v.shape[1] // 2
    near = product(jnp.concatenate([v[:, :half], v[:, half:]], axis=0), taps[:3])
    far = product(v[:, :half], taps[3:])
    return jnp.concatenate([near[:rows], near[rows:] + far], axis=1)


def backward(v, taps):
    rows = v.shape[0]
    half = v.shape[1] // 2
    near = product(jnp.concatenate([v[:, :half], v[:, half:]], axis=0), taps[:3])
    far = product(v[:, half:], taps[3:])
    return jnp.concatenate([near[:rows] + far, near[rows:]], axis=1)


def lanes_sum(v):
    rows, cols = v.shape
    total = None
    for i in range(0, rows, 8):
        for j in range(0, cols, 128):
            part = v[i : i + 8, j : j + 128]
            total = part if total is None else total + part
    return total


def column(row, n):
    return jnp.sum(jnp.where(iota((n, n), 0) == iota((n, n), 1), row, 0.0), axis=1, keepdims=True)


def stack3(v):
    a = v.astype(BF16).astype(F32)
    rest = v - a
    b = rest.astype(BF16).astype(F32)
    return jnp.concatenate([rest - b, b, a], axis=0).astype(BF16)


def thrice(m):
    return jnp.concatenate([m, m, m], axis=1).astype(BF16)


def fold(tile):
    hi, lo = tile, jnp.zeros_like(tile)
    for axis, shifts in ((0, (4, 2, 1)), (1, (64, 32, 16, 8, 4, 2, 1))):
        for s in shifts:
            hi, e = two_sum(hi, pltpu.roll(hi, s, axis))
            lo = (lo + pltpu.roll(lo, s, axis)) + e
    return hi[0:1, :], lo[0:1, :]


def chosen(odd, ref, flip):
    lower, upper = ref[0, 0:1, :].astype(F32), ref[0, 1:2, :].astype(F32)
    return jnp.where(odd != flip, lower, upper)


def selectors(odd, bp, bc, pipes):
    cap = bp.shape[2]
    counts = bc[0:1, :].astype(F32)
    count_a = jnp.where(odd, counts[:, 0:1], counts[:, 1:2])
    count_b = jnp.where(odd, counts[:, 1:2], counts[:, 0:1])
    slot = iota((cap, 1), 0).astype(F32)
    live_a = jnp.where(slot < count_a, 1.0, 0.0)
    live_b = jnp.where(slot < count_b, 1.0, 0.0)
    pipe = iota((cap, pipes), 1).astype(F32)
    sel_a = jnp.where(column(chosen(odd, bp, False), cap) == pipe, live_a, 0.0)
    sel_b = jnp.where(column(chosen(odd, bp, True), cap) == pipe, live_b, 0.0)
    return sel_a, sel_b


def is_odd():
    return lax.axis_index("core") == 1


def open_kernel(prior_in, *refs):
    count = 8
    ins, prior, copies = (prior_in, *refs[: count - 1]), refs[count - 1], refs[count - 1 : 2 * count - 1]
    msg, flow, sems, pipe_of, count_of = refs[2 * count - 1 :]
    moves = [pltpu.make_async_copy(ins[1], pipe_of, sems.at[count]), pltpu.make_async_copy(ins[2], count_of, sems.at[count + 1])]
    piece = prior.shape[0] // 4
    for k in range(4):
        rows = pl.ds(k * piece, piece)
        moves.append(pltpu.make_async_copy(prior_in.at[rows, :], prior.at[rows, :], sems.at[count + 2 + k]))
    moves += [pltpu.make_async_copy(i, o, sems.at[k]) for k, (i, o) in enumerate(zip(ins, copies)) if k]
    for m in moves:
        m.start()
    for m in moves[:6]:
        m.wait()
    cap = pipe_of.shape[2]
    side = jnp.where(is_odd(), 0, 1)
    live = count_of[0, side]
    live_b = count_of[0, 1 - side]
    for k in range(cap):
        row = prior[pl.ds(pipe_of[0, side, k], 1), :]
        msg[k : k + 1, :] = jnp.where(k < live, -row, 0.0)
        row = prior[pl.ds(pipe_of[0, 1 - side, k], 1), :]
        flow[k : k + 1, :] = jnp.where(k < live_b, -row, 0.0)
    msg[cap:, :] = jnp.where(iota((cap, prior.shape[1]), 0) < live, 1.0, 0.0)
    for m in moves[6:]:
        m.wait()


def lists_kernel(sent, prior, bp, bc, aj, head, tail, demand, s_ab, s_abt, inc, inc_t, l_a, l_b, out_b, out_a, mid_b, mid_a, own, gain, live_b, part, base):
    cap = bp.shape[2]
    pipes = prior.shape[0]
    juncs = inc.shape[0]
    odd = is_odd()
    sel_a, sel_b = selectors(odd, bp, bc, pipes)
    inner = 1.0 - jnp.sum(sel_a + sel_b, axis=0, keepdims=True)
    junction = iota((juncs, pipes), 0)
    heads = jnp.where(junction == head[...], inner, 0.0)
    tails = jnp.where(junction == tail[...], 1.0, 0.0)
    both = heads - tails
    land = iota((juncs, cap), 0).astype(F32)
    to_a, to_b = chosen(odd, aj, False), chosen(odd, aj, True)
    land_a = jnp.where(land == to_a, 1.0, 0.0)
    land_b = jnp.where(land == to_b, 1.0, 0.0)
    row = iota((cap, juncs), 1).astype(F32)
    land_at = jnp.where(row == column(to_a, cap), 1.0, 0.0)
    land_bt = jnp.where(row == column(to_b, cap), 1.0, 0.0)
    square = jnp.transpose(jnp.concatenate([both, jnp.zeros((pipes - juncs, pipes), F32)], axis=0))
    both_t = square[:, :juncs]
    pad = jnp.zeros((128 - 2 * cap, 128), F32)
    turned = jnp.transpose(jnp.concatenate([sel_a, sel_b, pad], axis=0))
    both16, a16, b16 = both.astype(BF16), land_a.astype(BF16), land_b.astype(BF16)
    at16, bt16, inc_t16 = land_at.astype(BF16), land_bt.astype(BF16), both_t.astype(BF16)
    sel16, selt16 = jnp.concatenate([sel_a, sel_b], axis=0).astype(BF16), turned[:, : 2 * cap].astype(BF16)
    s_ab[...] = sel16
    s_abt[...] = selt16
    inc[...] = both16
    inc_t[...] = inc_t16
    l_a[...] = a16
    l_b[...] = b16
    b_inc = mm(bt16, both16)
    b_inc16 = b_inc.astype(BF16)
    out_b[...] = b_inc16
    ends = jnp.concatenate([land_at, mm(sel16, inc_t16)], axis=0)
    out_a[...] = ends.astype(BF16)
    to_sel = mm(b_inc16, selt16)
    mid_b[...] = thrice(jnp.concatenate([to_sel, mm(bt16, a16)], axis=1))
    mid_a[...] = thrice(mm(ends.astype(BF16), b16))
    own[...] = mm(bt16, b16)
    gain[...] = jnp.full(gain.shape, PENALTY, F32)
    live_b[...] = jnp.broadcast_to(jnp.sum(sel_b, axis=1, keepdims=True), live_b.shape)
    p = demand[...] - pick(both16, prior[...])
    part[...] = p
    base[...] = pick(bt16, p)


def across_first(got, base, mid_b, own, msg, arrived, live):
    cap, hours = base.shape
    arr = got[0:cap, :]
    arrived[...] = arr
    live[...] = got[cap:, 0:128]
    none = jnp.zeros_like(arr)
    msg[:, 0:hours] = base[...] + mm(mid_b[...], stack3(jnp.concatenate([none, none, arr], axis=0)))
    msg[:, hours:] = jnp.zeros((cap, msg.shape[1] - hours), F32)
    msg[:, hours : hours + cap] = own[...]


def wide(tile, v):
    return jnp.concatenate([tile] * (v.shape[1] // 128), axis=1)


def across(gain, sent, got, live, base, mid_b, cut_b, adds, arrived):
    cap = live.shape[0]
    g = gain[...]
    added = wide(g, sent) * got[0:cap, :]
    arr = got[cap:, :] + wide(g * live[...], sent) * sent[0:cap, :]
    arrived[...] = arr
    adds[0:cap, :] = added
    adds[cap:, :] = cut_b
    return base[...] + mm(mid_b[...], stack3(jnp.concatenate([added, cut_b, arr], axis=0)))


def across_zero(gain, sent, got, live, base, mid_b, flow, heads, sent_flow, live_b, msg, adds, arrived, far):
    cap, hours = base.shape
    match = heads[:, hours : hours + cap]
    far[...] = match
    y_far = heads[:, 0:hours] + mm(thrice(match), stack3(sent_flow[...]))
    cut_b = wide(gain[...] * live_b[...], y_far) * y_far
    msg[0:cap, :] = flow[...] + cut_b
    msg[cap:, :] = across(gain, sent, got, live, base, mid_b, cut_b, adds, arrived)


def across_both(gain, sent, got, live, base, mid_b, flow, cut_b, msg, adds, arrived):
    cap = base.shape[0]
    msg[0:cap, :] = flow[...]
    msg[cap:, :] = across(gain, sent, got, live, base, mid_b, cut_b[...], adds, arrived)


def whole_kernel(gain, w, got, cut_b, s_abt, r_out):
    cap = cut_b.shape[0]
    added = jnp.concatenate([gain[0:1, 0:1] * got[0:cap, :], cut_b[...]], axis=0)
    r_out[...] = w[...] + pick(s_abt[...], added)


def back(gain, flows, base, mid_a, msg):
    cap = flows.shape[0]
    x = mm(mid_a[...], stack3(flows))
    g = wide(gain[...], x)
    msg[0:cap, :] = base[0:cap, :] + x[0:cap]
    msg[cap:, :] = base[cap : 2 * cap, :] + g * x[cap : 2 * cap]
    return base[2 * cap :, :] + g * x[2 * cap :]


def back_flows(gain, got, base, mid_a, msg, flow):
    flow[...] = back(gain, got[...], base, mid_a, msg)


def back_both(gain, got, base, mid_a, own_heads, live_b, msg, flow, cut_b):
    cap = own_heads.shape[0]
    y_far = got[cap:, :] + own_heads[...]
    c = wide(gain[...] * live_b[...], y_far) * y_far
    cut_b[...] = c
    flow[...] = back(gain, got[0:cap, :], base, mid_a, msg) + c


def outward(gain, part, near, s_ab, out_a, base):
    cap = s_ab.shape[0] // 2
    x = pick(out_a[...], part)
    base[0:cap, :] = x[0:cap]
    base[cap:, :] = gain * x[cap:] + pick(s_ab[...], near)


def inside_first(
    sent, coef, sigma, measured, prior, part_in, arrived, l_a, s_ab, out_a, *outs,
):
    taps, (weight, near, rvar, gain, part, base) = outs[:12], outs[12:]
    length = coef.shape[1]
    half = length // 2
    c = coef[...]
    shifted = pltpu.roll(jnp.broadcast_to(c, (half, length)), 0, 1, stride=1, stride_axis=0)
    upper = iota((half, half), 1) >= iota((half, half), 0)
    t0 = jnp.where(upper, shifted[:, :half], 0.0)
    t1 = shifted[:, half:]
    for k, x in enumerate((t0, t1, t0.T, t1.T)):
        for ref, term in zip(taps[3 * k : 3 * k + 3], thirds(x)):
            ref[...] = term
    size = jnp.sum(jnp.abs(c), axis=1, keepdims=True)
    scale = 1.0 / (4.0 * size * size + 64.0)
    gain[...] = jnp.broadcast_to(PENALTY * scale, gain.shape)
    sig = jnp.transpose(jnp.broadcast_to(sigma[...], (128, 128)))[:, 0:1]
    rsig = 1.0 / sig
    whitened = forward((measured[...] - prior[...]) * rsig, taps[:6])
    h = EDGE / jnp.maximum(jnp.abs(whitened), EDGE)
    weight[...] = h
    n = backward(h * whitened, taps[6:]) * rsig
    near[...] = n
    rvar[...] = jnp.broadcast_to(rsig * rsig * scale, rvar.shape)
    p = part_in[...] + pick(l_a[...], arrived[...])
    part[...] = p
    outward(PENALTY, p, n, s_ab, out_a, base)


def inside(refs):
    gain, sent, w, adds, arrived, far, weight, rvar, s_ab, s_abt, inc, l_a, out_a = refs[:13]
    taps, (r_out, part, near, base, heads) = refs[13:25], refs[25:]
    r = w[...] + pick(s_abt[...], adds[...])
    r_out[...] = r
    p = pick(inc[...], r) + pick(l_a[...], arrived[...])
    part[...] = p
    n = backward(weight[...] * forward(r, taps[:6]), taps[6:]) * rvar[:, 0:1]
    near[...] = n
    outward(gain[0:1, 0:1], p, n, s_ab, out_a, base)
    heads[...] = pick(far[...].astype(BF16), sent[0 : heads.shape[0], :])
    return r, p, n


def inside_one(*refs):
    *refs, sums = refs
    r, _, _ = inside(refs)
    sums[...] = lanes_sum(r * r)


def inside_two(before, *refs):
    *refs, sums = refs
    r, _, _ = inside(refs)
    sums[0:8, :] = lanes_sum(before[...] * r)
    sums[8:16, :] = lanes_sum(r * r)


def inside_three(before, sum0, sum1, *refs):
    *refs, row = refs
    gain = refs[0]
    r, p, n = inside(refs)
    tiles = (
        sum0[0:8, :], sum1[0:8, :], sum1[8:16, :], lanes_sum(before[...] * r), lanes_sum(r * r),
        lanes_sum(r * n) + gain[0:1, 0:1] * lanes_sum(p * p),
    )
    lane = iota((1, 128), 1)
    out = jnp.zeros((1, 128), F32)
    for k, tile in enumerate(tiles):
        hi, lo = fold(tile)
        out = jnp.where(lane == 2 * k, hi, jnp.where(lane == 2 * k + 1, lo, out))
    row[...] = jnp.broadcast_to(out, row.shape)


def close_kernel(gain, sent, got, own, row, rows):
    cap = own.shape[0]
    f = got[0:cap, :]
    extra = f * (2.0 * sent[cap : 2 * cap, :] + pick(own[...].astype(BF16), f))
    x = gain[0:1, 0:1] * jnp.sum(lanes_sum(extra), axis=0, keepdims=True)
    x = x + pltpu.roll(x, 64, 1)
    out = jnp.where(iota((1, 128), 1) < 64, row[0:1, :], x)
    rows[...] = jnp.broadcast_to(out, rows.shape)


def join(gain, sent_back, got, part, near, l_b, inc_t, out_b, w_out, base):
    cap = l_b.shape[1]
    y = part[...] + pick(l_b[...], got[0:cap, :])
    w = near[...] + gain[0:1, 0:1] * pick(inc_t[...], y)
    w_out[...] = w
    base[...] = pick(out_b[...], w)


def two_sum(a, b):
    s = a + b
    t = s - a
    return s, (a - (s - t)) + (b - t)


def finish_kernel(rows, gain, prior, r0, r1, r2, r3, flows, residual, x_s, e_s, sems):
    n = rows.shape[0]
    tots = [(rows[i : i + 8, :], None) for i in range(0, n, 8)]
    while len(tots) > 1:
        pairs = []
        for (a, ae), (b, be) in zip(tots[::2], tots[1::2]):
            t, e = two_sum(a, b)
            pairs.append((t, e if ae is None else (ae + be) + e))
        tots = pairs
    hi, lo = tots[0]
    for sh in (4, 2, 1):
        hi, e = two_sum(hi, pltpu.roll(hi, sh, 0))
        lo = (lo + pltpu.roll(lo, sh, 0)) + e
    at = iota((8, 128), 1)
    cut = jnp.sum(jnp.where(at >= 64, hi + lo, 0.0), axis=1, keepdims=True)
    low = lo + (pltpu.roll(hi, 127, 1) + pltpu.roll(lo, 127, 1))
    hi, e = two_sum(hi, jnp.where(at == 10, cut, 0.0))
    hi, lo = two_sum(hi, low + e)

    def lane(v, k):
        return jnp.broadcast_to(v[:, k : k + 1], (8, 128))

    m = [(lane(hi, 2 * k), lane(lo, 2 * k)) for k in range(6)]
    s = (m[1][0] / m[0][0]).astype(BF16).astype(F32)
    mu = [m[0][0]]
    for _ in range(5):
        level = []
        for (h0, l0), (h1, l1) in zip(m[:-1], m[1:]):
            top = h0.astype(BF16).astype(F32)
            a, e = two_sum(h1, -(s * top))
            b, e2 = two_sum(a, -(s * (h0 - top)))
            level.append((b, (e + e2) + (l1 - s * l0)))
        m = level
        mu.append(m[0][0] + m[0][1])
    nu = [mu[k + 1] + s * mu[k] for k in range(5)]

    def form(u, v, m):
        total = None
        for i, a in enumerate(u):
            for j, b in enumerate(v):
                term = a * b * m[i + j]
                total = term if total is None else total + term
        return total

    def image(d):
        out = [s * x for x in d] + [jnp.zeros_like(s)]
        return [out[k] + (d[k - 1] if k else 0.0) for k in range(len(out))]

    a0 = mu[0] / nu[0]
    res1 = [mu[1] / nu[0], -a0]
    rr1 = form(res1, res1, mu)
    b0 = rr1 / mu[0]
    d1 = [res1[0] + b0, res1[1]]
    a1 = rr1 / form(d1, d1, nu)
    im1 = image(d1)
    res2 = [res1[0] - a1 * im1[0], res1[1] - a1 * im1[1], -a1 * im1[2]]
    rr2 = form(res2, res2, mu)
    b1 = rr2 / rr1
    d2 = [res2[0] + b1 * d1[0], res2[1] + b1 * d1[1], res2[2]]
    a2 = rr2 / form(d2, d2, nu)
    im2 = image(d2)
    f = [a0 + a1 * d1[0] + a2 * d2[0], a1 * d1[1] + a2 * d2[1], a2 * d2[2]]
    e = [res2[0] - a2 * im2[0], res2[1] - a2 * im2[1], res2[2] - a2 * im2[2], -a2 * im2[3]]
    ss = s * s
    f = [f[0] - s * f[1] + ss * f[2], f[1] - 2.0 * s * f[2], f[2]]
    e = [
        ((e[0] - s * e[1]) + ss * e[2]) - ss * s * e[3],
        (e[1] - 2.0 * s * e[2]) + 3.0 * ss * e[3],
        e[2] - 3.0 * s * e[3],
        e[3],
    ]
    g = jnp.broadcast_to(gain[0:1, 0:1], (8, 128)) * (1.0 / PENALTY)
    f = [x[0:1, 0:1] * g[0:1, 0:1] for x in f]
    e = [x[0:1, 0:1] for x in e]
    moves = []
    step = prior.shape[0] // 4
    for i in range(4):
        at = slice(i * step, (i + 1) * step)
        x0, x1, x2 = r0[at, :], r1[at, :], r2[at, :]
        x_s[at, :] = prior[at, :] + ((f[0] * x0 + f[1] * x1) + f[2] * x2)
        e_s[at, :] = ((e[0] * x0 + e[1] * x1) + e[2] * x2) + e[3] * r3[at, :]
        for k, (src, dst) in enumerate(((x_s, flows), (e_s, residual))):
            moves.append(pltpu.make_async_copy(src.at[pl.ds(i * step, step), :], dst.at[pl.ds(i * step, step), :], sems.at[2 * i + k]))
            moves[-1].start()
    for m in moves:
        m.wait()


def call(kernel, outs, *args):
    return pl.pallas_call(
        kernel,
        out_shape=tuple(pltpu.VMEM(s, d) for s, d in outs),
        in_specs=[pl.BlockSpec(memory_space=pltpu.VMEM)] * len(args),
        out_specs=tuple(pl.BlockSpec(memory_space=pltpu.VMEM) for _ in outs),
        compiler_params=pltpu.CompilerParams(vmem_limit_bytes=16 * 2**20),
    )(*(pltpu.with_memory_space_constraint(x, pltpu.VMEM) for x in args))


def bring(args, *msgs):
    lists = (args[1], args[2])
    return pl.pallas_call(
        open_kernel,
        out_shape=tuple(pltpu.VMEM(x.shape, x.dtype) for x in args) + tuple(pltpu.VMEM(*m) for m in msgs),
        in_specs=[pl.BlockSpec(memory_space=pltpu.HBM)] * len(args),
        out_specs=tuple(pl.BlockSpec(memory_space=pltpu.VMEM) for _ in range(len(args) + len(msgs))),
        scratch_shapes=[pltpu.SemaphoreType.DMA((len(args) + 6,))] + [pltpu.SMEM(x.shape, x.dtype) for x in lists],
        compiler_params=pltpu.CompilerParams(vmem_limit_bytes=16 * 2**20),
    )(*(pltpu.with_memory_space_constraint(x, pltpu.HBM) for x in args))


def finish(rows, *args):
    field = args[1]
    args = (rows, *args)
    return pl.pallas_call(
        finish_kernel,
        out_shape=(jax.ShapeDtypeStruct(field.shape, F32),) * 2,
        in_specs=[pl.BlockSpec(memory_space=pltpu.VMEM)] * len(args),
        out_specs=(pl.BlockSpec(memory_space=pltpu.HBM),) * 2,
        scratch_shapes=[pltpu.VMEM(field.shape, F32)] * 2 + [pltpu.SemaphoreType.DMA((8,))],
        compiler_params=pltpu.CompilerParams(vmem_limit_bytes=16 * 2**20),
    )(*(pltpu.with_memory_space_constraint(x, pltpu.VMEM) for x in args))


def shards(
    measured,
    prior_flow,
    demand,
    pipe_sigma,
    whiten_coef,
    pipe_tail,
    pipe_head,
    boundary_pipe,
    boundary_count,
    arrival_junction,
):
    pipes, hours = prior_flow.shape
    juncs = demand.shape[0]
    cap = boundary_pipe.shape[2]
    nets = lax.axis_size(NET)
    hour_blocks = lax.axis_size("hour")
    devices = nets * hour_blocks
    field = ((pipes, hours), F32)
    heads = ((juncs, hours), F32)
    slots = ((cap, hours), F32)
    msg2 = ((2 * cap, hours), F32)
    msg3 = ((3 * cap, hours), F32)
    tile = ((8, 128), F32)
    half = ((hours // 2, hours // 2), BF16)
    on_chip = [(i, i ^ 1) for i in range(nets)]
    across_pairs = []
    for h in range(hour_blocks):
        for i in range(1, nets - 1, 2):
            a, b = i * hour_blocks + h, (i + 1) * hour_blocks + h
            across_pairs += [(a, b), (b, a)]
        for i in (0, nets - 1):
            across_pairs.append((i * hour_blocks + h, i * hour_blocks + (h ^ 1)))

    def swap(x):
        return lax.ppermute(x, NET, on_chip)

    def cross(x):
        return lax.ppermute(x, (*NET, "hour"), across_pairs)

    args = (
        prior_flow, boundary_pipe, boundary_count, arrival_junction,
        pipe_head.reshape(1, pipes), pipe_tail.reshape(1, pipes), whiten_coef.reshape(1, hours), pipe_sigma.reshape(1, pipes),
    )
    prior, bp, bc, aj, head, tail, coef, sigma, msg, flow = bring(args, msg2, slots)
    got = swap(msg)
    flow_got = cross(flow)
    s_ab, s_abt, inc, inc_t, l_a, l_b, out_b, out_a, mid_b, mid_a, own, gain0, live_b, part, base = call(
        lists_kernel,
        [
            ((2 * cap, pipes), BF16), ((pipes, 2 * cap), BF16), ((juncs, pipes), BF16), ((pipes, juncs), BF16),
            ((juncs, cap), BF16), ((juncs, cap), BF16), ((cap, pipes), BF16), ((3 * cap, juncs), BF16),
            ((cap, 9 * cap), BF16), ((3 * cap, 3 * cap), BF16), ((cap, cap), F32), tile, tile, heads, slots,
        ],
        msg, prior, bp, bc, aj, head, tail, demand,
    )
    sent, arrived, live = call(across_first, [((cap, hours + 128), F32), slots, tile], got, base, mid_b, own)
    heads_got = cross(sent)
    out = call(
        inside_first,
        [half] * 12 + [field, field, ((pipes, 128), F32), tile, heads, msg3],
        sent, coef, sigma, measured, prior, part, arrived, l_a, s_ab, out_a,
    )
    taps, (weight, near, rvar, gain, part, base) = out[:12], out[12:]

    def joined(g, msg, flows):
        return call(join, [field, slots], g, msg, flows, part, near, l_b, inc_t, out_b)

    def filtered(kernel, acc, first, sent, w, adds, arrived):
        return call(
            kernel, [field, heads, field, msg3, slots, acc],
            *first, gain, sent, w, adds, arrived, far, weight, rvar, s_ab, s_abt, inc, l_a, out_a, *taps,
        )

    msg, fore = call(back_flows, [msg2, slots], gain0, flow_got, base, mid_a)
    got = swap(msg)
    w, base = joined(gain0, msg, flow_got)
    both, adds, arrived, far = call(
        across_zero, [msg2, msg2, slots, ((cap, cap), F32)],
        gain0, msg, got, live, base, mid_b, fore, heads_got, flow, live_b,
    )
    both_got = cross(both)
    r0, part, near, base, own_heads, sum0 = filtered(inside_one, tile, (), both, w, adds, arrived)
    fields, sums = [r0], [sum0]
    for k in (1, 2):
        msg, flow, cut_b = call(back_both, [msg2, slots, slots], gain, both_got, base, mid_a, own_heads, live_b)
        got = swap(msg)
        w, base = joined(gain, msg, both_got)
        both, adds, arrived = call(
            across_both, [msg2, msg2, slots], gain, msg, got, live, base, mid_b, flow, cut_b
        )
        both_got = cross(both)
        if k == 1:
            r, part, near, base, own_heads, acc = filtered(
                inside_two, ((16, 128), F32), (fields[0],), both, w, adds, arrived
            )
        else:
            r, part, near, base, own_heads, acc = filtered(
                inside_three, tile, (fields[1], *sums), both, w, adds, arrived
            )
        fields.append(r)
        sums.append(acc)
    (rows,) = call(close_kernel, [((devices, 128), F32)], gain, both, both_got, own, acc)
    rows = lax.all_to_all(
        rows.reshape(devices, 1, 128), ("core", "z", "y", "hour"), 0, 0, tiled=True
    ).reshape(devices, 128)
    msg, _, cut_b = call(back_both, [msg2, slots, slots], gain, both_got, base, mid_a, own_heads, live_b)
    got = swap(msg)
    w, _ = joined(gain, msg, both_got)
    (r3,) = call(whole_kernel, [field], gain, w, got, cut_b, s_abt)
    return finish(rows, gain, prior, *fields, r3)


def solution(mesh):
    nets, hours = mesh.devices.shape
    fine = Mesh(mesh.devices.reshape(nets // 8, 4, 2, hours), (*NET, "hour"))
    placed = (
        P(NET, "hour"),
        P(NET, "hour"),
        P(NET, "hour"),
        P(NET),
        P(),
        P(NET),
        P(NET),
        P(NET, None, None),
        P(NET, None),
        P(NET, None, None),
    )

    return jax.shard_map(
        shards,
        mesh=fine,
        in_specs=placed,
        out_specs=(P(NET, "hour"), P(NET, "hour")),
        check_vma=False,
    )
```
